256 devices in a mesh: row: 32 (over z_lo, x, core), col: 8 (over z_hi, y).
Axes of the slice: x: 4, y: 4, z: 8 (z_hi: 2, z_lo: 4; z = z_hi * 4 + z_lo), core: 2. Of those that a mesh axis runs over, the one named last changes fastest.
Arguments:
- positions: float32 [3, 1048576], P(None, ('row', 'col')), may hold values from 0 to 385, as said below
- atom_type: int32 [1048576], P(('row', 'col')), may hold values from 0 to 5
- krylov: float32 [16, 1048576], P(None, ('row', 'col')), may hold values from -6 to 6
- block_order: int32 [1048576], P(('row', 'col')), may hold values from 0 to 4095, as said below
- type_width: float32 [6], replicated, may hold values from 0.5 to 2.5
- type_hard: float32 [6], replicated, may hold values from 1 to 4
- pair_rows: int32 [32, 8, 512], P('row', 'col'), may hold values from 0 to 255, as said below
- pair_cols: int32 [32, 8, 512], P('row', 'col'), may hold values from 0 to 1023, as said below
- pair_count: int32 [32, 8], P('row', 'col'), may hold values from 1 to 512, as said below
Outputs:
- coulomb_response: float32 [16, 1048576], P(None, ('row', 'col'))
The draws below stay inside these ranges and needn't reach their ends.
Inputs may be any that keep to these rules, and one draw needn't show every extreme that they name: `positions`: global block g is a cell of a grid with coordinates (g // 256, (g // 32) % 8, g % 32); each atom of block g lies in the box of sides 44, 30 and 44 whose lowest corner is the cell's coordinates times 11, 5 and 11. `block_order`: within each device's shard of 4096 atoms, the entries are a permutation of 0 to 4095. `pair_rows`: in slots below pair_count the pairs (i, j) are distinct, have i <= j, and their grid cells differ by at most 2 along the first and third dimensions and at most 4 along the second; for device (r, c), pair_cols // 32 is r, r + 1 or r + 2 there. Other slots hold indices in range that are not used. `pair_cols`: see pair_rows. `pair_count`: some device's list is full.
All inputs are finite; a program needn't handle non-finite values.
Results may differ from the reference program's by a relative error of at most 0.00665.
Values may be sent and summed in bfloat16 or wider, within the bound.
No kernel may reach another device: no remote copies, remote signals or barrier semaphores. Data moves between devices by JAX's collectives and lax.ppermute only.
A program may use at most 128 MiB of HBM per device.

```python
import math
import jax
import jax.numpy as jnp
from jax import lax

VECS = 16
BLK = 128
NTYPES = 6
BLOCKS_DEV = 32
PAIRS_DEV = 512
ATOMS = 1048576
N_ROW = 32
N_COL = 8


def block_orders(key):
    shard_keys = jax.random.split(jax.random.fold_in(key, 29), N_ROW * N_COL)

    def one_shard(shard_key):
        return jax.random.permutation(shard_key, BLOCKS_DEV * BLK).astype(jnp.int32)
    return jax.vmap(one_shard)(shard_keys)


def draw_block_order(key, part):
    return block_orders(key).reshape(-1)


def draw_positions(key, part):
    orders = block_orders(key)
    shard_atoms = BLOCKS_DEV * BLK
    atom_total = N_ROW * N_COL * shard_atoms
    blocked = jnp.arange(atom_total, dtype=jnp.int32)
    global_block = blocked // BLK
    cell_z = global_block % BLOCKS_DEV
    cell_y = global_block // BLOCKS_DEV % N_COL
    cell_x = global_block // (BLOCKS_DEV * N_COL)
    cells = jnp.stack([cell_x, cell_y, cell_z]).astype(jnp.float32)
    jitter = jax.random.uniform(jax.random.fold_in(key, 41), (3, atom_total), jnp.float32, 0.0, 0.999)
    spacing = jnp.array([11.0, 5.0, 11.0], jnp.float32)[:, None]
    extent = jnp.array([44.0, 30.0, 44.0], jnp.float32)[:, None]
    values = spacing * cells + extent * jitter
    atom_index = (blocked // shard_atoms * shard_atoms + orders.reshape(-1)).astype(jnp.int32)
    return jnp.zeros((3, atom_total), jnp.float32).at[:, atom_index].set(values)


def pair_lists(key):
    device_total = N_ROW * N_COL
    device_keys = jax.random.split(jax.random.fold_in(key, 11), device_total)
    row_blocks = N_COL * BLOCKS_DEV
    candidates = 3 * row_blocks * BLOCKS_DEV
    full_device = min(2, N_COL - 1)

    def one_device(device_key, device):
        row_index = device // N_COL
        col_index = device % N_COL
        shuffled = jax.random.permutation(device_key, candidates).astype(jnp.int32)
        local_row = shuffled % row_blocks
        rest = shuffled // row_blocks
        col_z = rest % BLOCKS_DEV
        step_x = rest // BLOCKS_DEV
        col_slab = row_index + step_x
        row_y = local_row // BLOCKS_DEV
        row_z = local_row % BLOCKS_DEV
        near = (jnp.abs(row_y - col_index) <= 4) & (jnp.abs(row_z - col_z) <= 2) & (col_slab < N_ROW)
        upper = (step_x > 0) | (col_index * BLOCKS_DEV + col_z >= local_row)
        valid = (near & upper).astype(jnp.int32)
        local_col = jnp.minimum(col_slab * BLOCKS_DEV + col_z, N_ROW * BLOCKS_DEV - 1).astype(jnp.int32)
        scores = (1 - valid) * candidates + jnp.arange(candidates, dtype=jnp.int32)
        picked = jnp.argsort(scores)[:PAIRS_DEV]
        wanted = jax.random.randint(jax.random.fold_in(device_key, 3), (), PAIRS_DEV // 4, PAIRS_DEV + 1)
        wanted = jnp.where(device == full_device, PAIRS_DEV, wanted)
        live_count = jnp.minimum(wanted, jnp.sum(valid)).astype(jnp.int32)
        return (local_row[picked], local_col[picked], live_count)
    rows_all, cols_all, counts_all = jax.vmap(one_device)(device_keys, jnp.arange(device_total, dtype=jnp.int32))
    return (rows_all.reshape(N_ROW, N_COL, PAIRS_DEV), cols_all.reshape(N_ROW, N_COL, PAIRS_DEV), counts_all.reshape(N_ROW, N_COL))


def draw_pair_rows(key, part):
    return pair_lists(key)[0]


def draw_pair_cols(key, part):
    return pair_lists(key)[1]


def draw_pair_count(key, part):
    return pair_lists(key)[2]


def touch_ends(values, own_key, low, high):
    place = [jax.random.randint(jax.random.fold_in(own_key, axis), (), 0, length) for axis, length in enumerate(values.shape)]
    widest = values.shape.index(max(values.shape))
    neighbour = place[:widest] + [(place[widest] + 1) % values.shape[widest]] + place[widest + 1:]
    return values.at[tuple(place)].set(low).at[tuple(neighbour)].set(high)


def levels(stream_key, dims, cuts, low, high):
    gain = 1.0
    for position, blocks in cuts:
        heights = jax.random.uniform(jax.random.fold_in(jax.random.fold_in(stream_key, 6), position), (blocks,), jnp.float32, low / len(cuts), high / len(cuts))
        gain = gain * jnp.repeat(jnp.exp(heights), dims[position] // blocks).reshape((-1,) + (1,) * (len(dims) - 1 - position))
    return gain


def normal_values(rng, shape, scale, reach, shards=(), kind=jnp.bfloat16):
    gain = levels(rng, shape, shards, -0.22, 0.18) if shards else 1.0
    values = jax.random.normal(rng, shape, jnp.float32) * scale * gain
    return jnp.minimum(jnp.maximum(values, -reach), reach).astype(kind)


def setup_inputs(seed: int = 0) -> dict:
    keys = jax.random.split(jax.random.key(seed), 10)
    positions = draw_positions(jax.random.fold_in(keys[9], 71), 0)
    atom_type = touch_ends(jax.random.randint(keys[1], (ATOMS,), 0, NTYPES), jax.random.fold_in(keys[1], 1), 0, NTYPES - 1).astype(jnp.int32)
    krylov = normal_values(keys[2], (VECS, ATOMS), 1.0, 6.0, ((1, 256),), jnp.float32)
    block_order = draw_block_order(jax.random.fold_in(keys[9], 71), 0)
    type_width = jnp.clip(jnp.exp(jax.random.uniform(keys[4], (NTYPES,), jnp.float32, math.log(0.5), math.log(2.5))), 0.5, 2.5)
    type_hard = jnp.clip(jax.random.uniform(keys[5], (NTYPES,), jnp.float32, 1.0, 4.0), 1.0, 4.0)
    pair_rows = draw_pair_rows(jax.random.fold_in(keys[9], 71), 0)
    pair_cols = draw_pair_cols(jax.random.fold_in(keys[9], 71), 0)
    pair_count = draw_pair_count(jax.random.fold_in(keys[9], 71), 0)
    return dict(positions=positions, atom_type=atom_type, krylov=krylov, block_order=block_order, type_width=type_width, type_hard=type_hard, pair_rows=pair_rows, pair_cols=pair_cols, pair_count=pair_count)


SOFTENING = 0.5

def kernel_tiles(left_geometry, right_geometry):
    offsets = left_geometry[:, 0:3, :, None] - right_geometry[:, 0:3, None, :]
    distance = jnp.sqrt(lax.optimization_barrier(jnp.sum(offsets * offsets, axis=1)) + SOFTENING * SOFTENING)
    spread = left_geometry[:, 3, :, None] ** 2 + right_geometry[:, 3, None, :] ** 2
    return (lax.erf(distance * lax.rsqrt(spread)) / distance).astype(jnp.bfloat16)

def reference(positions, atom_type, krylov, block_order, type_width, type_hard, pair_rows, pair_cols, pair_count):
    atom_total = positions.shape[1]
    shard_atoms = BLOCKS_DEV * BLK
    blocks_all = atom_total // BLK
    offsets = jnp.arange(atom_total, dtype=jnp.int32) // shard_atoms * shard_atoms
    ordering = (offsets + block_order).astype(jnp.int32)
    widths = type_width[atom_type]
    hardness = type_hard[atom_type]
    geometry = jnp.concatenate([positions, widths[None, :]], axis=0)[:, ordering]
    vectors = krylov.astype(jnp.bfloat16)[:, ordering]
    geometry_blocks = geometry.reshape(4, blocks_all, BLK).transpose(1, 0, 2)
    vector_blocks = vectors.reshape(VECS, blocks_all, BLK).transpose(1, 0, 2)
    row_ids = jnp.arange(N_ROW, dtype=jnp.int32)[:, None, None]
    col_ids = jnp.arange(N_COL, dtype=jnp.int32)[None, :, None]
    row_global = (row_ids * (N_COL * BLOCKS_DEV) + pair_rows).astype(jnp.int32)
    col_global = ((pair_cols // BLOCKS_DEV * N_COL + col_ids) * BLOCKS_DEV + pair_cols % BLOCKS_DEV).astype(jnp.int32)
    slot_index = jnp.arange(PAIRS_DEV, dtype=jnp.int32)[None, None, :]
    live_flags = (slot_index < pair_count[:, :, None]).astype(jnp.float32)
    pair_total = N_ROW * N_COL * PAIRS_DEV
    batch_rows = math.gcd(pair_total, 256)
    row_global = row_global.reshape(-1, batch_rows)
    col_global = col_global.reshape(-1, batch_rows)
    live_flags = live_flags.reshape(-1, batch_rows)

    def pair_step(accumulated, pair_items):
        left_block, right_block, alive_now = pair_items
        tiles_now = kernel_tiles(geometry_blocks[left_block], geometry_blocks[right_block]).astype(jnp.float32)
        left_vectors = vector_blocks[left_block].astype(jnp.float32)
        right_vectors = vector_blocks[right_block].astype(jnp.float32)
        forward = jnp.einsum('pab,pvb->pva', tiles_now, right_vectors) * alive_now[:, None, None]
        mirror = alive_now * (left_block != right_block).astype(jnp.float32)
        backward = jnp.einsum('pab,pva->pvb', tiles_now, left_vectors) * mirror[:, None, None]
        accumulated = accumulated.at[left_block].add(forward).at[right_block].add(backward)
        return (accumulated, None)
    initial = jnp.zeros((blocks_all, VECS, BLK), jnp.float32)
    summed, _ = lax.scan(pair_step, initial, (row_global, col_global, live_flags))
    blocked = summed.transpose(1, 0, 2).reshape(VECS, atom_total)
    result = jnp.zeros((VECS, atom_total), jnp.float32).at[:, ordering].set(blocked)
    return result + hardness[None, :] * krylov
```

```python
import functools

import jax
import jax.numpy as jnp
from jax import lax
from jax.experimental import pallas as pl
from jax.experimental.pallas import tpu as pltpu
from jax.sharding import PartitionSpec as P

BLK = 128
VECS = 16
NTYPES = 6
BLOCKS = 32
HALF = 4 * BLOCKS
COLS = 3 * BLOCKS
ROWS = VECS + 8
DEPTH = 80
UNROLL = 4
CELL = (11.0, 5.0, 11.0)
BOX = (44.0, 30.0, 44.0)
SOFTENING = 0.5

ERF_COEFFS = (
    1.1283815681128107,
    -7.621837438329706e-05,
    0.10341113638200404,
    -0.002217632183960096,
    0.003526363187890101,
    -0.0031284691084128495,
    0.0005233424709803657,
)

VMEM = pl.BlockSpec(memory_space=pltpu.VMEM)
SMEM = pl.BlockSpec(memory_space=pltpu.SMEM)
Y_GROUPS = [[0, 1, 2, 3], [4, 5, 6, 7]]
F32 = jnp.float32
BF16 = jnp.bfloat16


def sublane():
    return lax.broadcasted_iota(jnp.int32, (8, BLK), 0)


def split3(value):
    high = value.astype(BF16).astype(F32)
    rest = value - high
    middle = rest.astype(BF16).astype(F32)
    return high, middle, rest - middle


def lane_gather(source, index):
    return jnp.take_along_axis(source, index, axis=1, mode="promise_in_bounds")


def prep_kernel(place, positions, atom_type, krylov, order, packed, geometry):
    geometry[...] = jnp.zeros_like(geometry)
    geometry[0:3, :] = positions[...]
    geometry[3:4, :] = atom_type[...].astype(F32)
    level = sublane()
    corner_x = CELL[0] * place[0].astype(F32) + BOX[0] / 2
    corner_y = CELL[1] * place[1].astype(F32) + BOX[1] / 2

    def one_block(block, carry):
        wanted = jnp.broadcast_to(order[pl.ds(block, 1), :], (8, BLK))
        chunk = wanted >> 7
        lane = wanted & 127
        top = jnp.zeros((8, BLK), F32)
        low = jnp.zeros((8, BLK), F32)
        geo = jnp.zeros((8, BLK), F32)
        for s in range(BLOCKS):
            here = chunk == s
            span = slice(s * BLK, (s + 1) * BLK)
            top = jnp.where(here, lane_gather(krylov[0:8, span], lane), top)
            low = jnp.where(here, lane_gather(krylov[8:16, span], lane), low)
            geo = jnp.where(here, lane_gather(geometry[:, span], lane), geo)
        corner_z = CELL[2] * block.astype(F32) + BOX[2] / 2
        corner = jnp.where(
            level == 0, corner_x, jnp.where(level == 1, corner_y, jnp.where(level == 2, corner_z, 0.0))
        )
        local = geo - corner
        coarse = jnp.floor(local * 4.0 + 0.5) * 0.25
        fine = jnp.where(level < 3, local - coarse, local)
        coded = jnp.where(level < 3, coarse, pltpu.roll(fine, 3, 0))
        packed[block, 0:VECS, :] = jnp.concatenate([top, low], axis=0).astype(BF16)
        packed[block, VECS:ROWS, :] = coded.astype(BF16)
        return carry

    lax.fori_loop(0, BLOCKS, one_block, 0)


def side_kernel(place, rows, cols, count, order, inverse, codes, counts):
    row_index = place[0]
    col_index = place[1]
    own_half = col_index >> 2

    def one_slot(slot, seen):
        first, second = seen
        row = rows[slot]
        col = cols[slot] - row_index * BLOCKS
        half = row >> 7
        same = half == own_half
        diagonal = jnp.logical_and(col < BLOCKS, row == col_index * BLOCKS + col)
        step_y = col_index - (row >> 5) + 4
        step_z = (col & 31) - (row & 31) + 2
        code = (
            (row & 127)
            | (col << 7)
            | (step_y << 14)
            | (step_z << 18)
            | (diagonal.astype(jnp.int32) << 21)
        )
        codes[jnp.where(same, first, codes.shape[0] // 2 + second)] = code
        one = same.astype(jnp.int32)
        return first + one, second + 1 - one

    first, second = lax.fori_loop(0, count[0], one_slot, (jnp.int32(0), jnp.int32(0)))
    spare = (4 << 14) | (2 << 18) | (1 << 21) | (1 << 22)
    for extra in range(UNROLL):
        codes[first + extra] = spare
        codes[codes.shape[0] // 2 + second + extra] = spare
    counts[0] = first
    counts[1] = second

    level_h = lax.broadcasted_iota(jnp.int32, (BLOCKS, BLK), 0)
    level_l = lax.broadcasted_iota(jnp.int32, (BLK, BLK), 0)
    lanes = lax.broadcasted_iota(jnp.int32, (BLOCKS, BLK), 1).astype(F32)
    total = jnp.zeros((2 * BLOCKS, BLK), F32)
    for block in range(BLOCKS):
        wanted = order[block : block + 1, :]
        in_high = (level_h == jnp.broadcast_to(wanted >> 7, (BLOCKS, BLK))).astype(F32)
        in_low = (level_l == jnp.broadcast_to(wanted & 127, (BLK, BLK))).astype(F32).astype(BF16)
        left = jnp.concatenate([in_high * float(block), in_high * lanes], axis=0).astype(BF16)
        total = total + lax.dot_general(
            left, in_low, (((1,), (1,)), ((), ())), preferred_element_type=F32
        )
    inverse[...] = (total[0:BLOCKS] * float(BLK) + total[BLOCKS:]).astype(jnp.int32)


def feature_kernel(type_width, own, after, second, features, vectors):
    level = sublane()
    squares = jnp.zeros((8, BLK), F32)
    for t in range(NTYPES):
        squares = jnp.where(level == t, type_width[t] * type_width[t], squares)
    low3 = level < 3
    low6 = level < 6
    last = level == 7
    zero = jnp.zeros((8, BLK), F32)
    ones = jnp.where(low6, 1.0, 0.0)
    twos = jnp.where(jnp.logical_and(low6, level >= 3), 2.0, 0.0)

    for part, source in enumerate((own, after, second)):

        def one_block(block, carry, part=part, source=source):
            vectors[part * BLOCKS + block] = source[block, 0:VECS, :]
            coded = source[block, VECS:ROWS, :].astype(F32)
            near = coded + pltpu.roll(coded, 5, 0)
            square = near * near
            weight = square[0:1] + square[1:2] + square[2:3] + SOFTENING * SOFTENING
            weight_h, weight_m, weight_l = split3(weight)
            coarse = jnp.where(low3, coded, pltpu.roll(coded, 3, 0)) * -2.0
            fine = jnp.where(low3, pltpu.roll(coded, 5, 0), coded) * -2.0
            own_type = jnp.broadcast_to(coded[6:7], (8, BLK))
            own_square = jnp.zeros((8, BLK), F32)
            for t in range(NTYPES):
                own_square = jnp.where(own_type == float(t), type_width[t] * type_width[t], own_square)
            scale = lax.rsqrt(own_square + squares)
            scale_h, scale_m, scale_l = split3(jnp.where(low6, scale, 0.0))
            wide = lambda v: jnp.broadcast_to(v, (8, BLK))
            stacked = jnp.concatenate(
                [
                    jnp.where(low6, coarse, jnp.where(last, wide(weight_h), 0.0)),
                    jnp.where(low6, fine, jnp.where(last, wide(weight_m), 0.0)),
                    jnp.where(last, wide(weight_l), ones),
                    ones,
                    twos,
                    twos,
                    scale_h,
                    scale_m,
                    scale_l,
                ]
                + [zero] * 7,
                axis=0,
            )
            features[part * BLOCKS + block] = stacked.T.astype(BF16)
            return carry

        lax.fori_loop(0, BLOCKS, one_block, 0)


def pair_tiles(code, row_ref, features, steps):
    row = code & 127
    col = (code >> 7) & 127
    step_x = col >> 5
    step_y = (code >> 14) & 15
    step_z = (code >> 18) & 7
    coded = row_ref[row, VECS:ROWS, :].astype(F32)
    shift = steps[step_x] + steps[3 + step_y] + steps[12 + step_z]
    near = coded - shift
    square = near * near
    cross = near * pltpu.roll(near, 3, 0)
    square_h = square.astype(BF16).astype(F32)
    cross_h = cross.astype(BF16).astype(F32)
    hot = (sublane().astype(F32) == jnp.broadcast_to(coded[6:7], (8, BLK))).astype(F32)
    zero = jnp.zeros((8, BLK), F32)
    left = jnp.concatenate(
        [near, near, square_h, square - square_h, cross_h, cross - cross_h, zero, zero, zero, zero],
        axis=0,
    ).astype(BF16)
    right = jnp.concatenate([zero] * 6 + [hot, hot, hot, zero], axis=0).astype(BF16)
    both = jnp.dot(
        features[col][:, 0:DEPTH],
        jnp.concatenate([left, right], axis=1),
        preferred_element_type=F32,
    )
    distance2 = both[:, 0:BLK]
    scale = both[:, BLK:]
    inverse = lax.rsqrt(distance2)
    z = distance2 * inverse * scale
    poly = ERF_COEFFS[-1]
    for coefficient in ERF_COEFFS[-2::-1]:
        poly = poly * z + coefficient
    return (jnp.tanh(poly * z) * inverse).astype(BF16)


def pair_loop(phase, counts, codes, row_ref, vectors, features, steps, row_acc, col_acc):
    base = phase * (codes.shape[0] // 2)

    def some_pairs(turn, carry):
        sums = []
        for u in range(UNROLL):
            code = codes[base + turn * UNROLL + u]
            row = code & 127
            col = (code >> 7) & 127
            tile = pair_tiles(code, row_ref, features, steps)
            forward = jnp.dot(vectors[col], tile, preferred_element_type=F32)
            backward = lax.dot_general(
                row_ref[row, 0:VECS, :],
                tile,
                (((1,), (1,)), ((), ())),
                preferred_element_type=F32,
            )
            to_row = jnp.where((code >> 22) & 1 == 1, HALF, row)
            to_col = jnp.where((code >> 21) & 1 == 1, COLS, col)
            sums.append((to_row, forward, to_col, backward))
        for to_row, forward, to_col, backward in sums:
            row_acc[to_row] += forward
            col_acc[to_col] += backward
        return carry

    lax.fori_loop(0, (counts[phase] + UNROLL - 1) // UNROLL, some_pairs, 0)


def first_kernel(counts, codes, row_ref, vectors, features, steps, row_out, col_out, row_acc, col_acc):
    row_acc[...] = jnp.zeros_like(row_acc)
    col_acc[...] = jnp.zeros_like(col_acc)
    pair_loop(0, counts, codes, row_ref, vectors, features, steps, row_acc, col_acc)
    row_out[...] = row_acc[0:HALF].astype(BF16)
    col_out[...] = col_acc[0:COLS]


def second_kernel(
    counts, codes, row_ref, vectors, features, steps, col_in, row_out, own_out, after_out, last_out, row_acc, col_acc
):
    row_acc[...] = jnp.zeros_like(row_acc)
    col_acc[0:COLS] = col_in[...]
    pair_loop(1, counts, codes, row_ref, vectors, features, steps, row_acc, col_acc)
    row_out[...] = row_acc[0:HALF].astype(BF16)
    own_out[...] = col_acc[0:BLOCKS]
    after_out[...] = col_acc[BLOCKS : 2 * BLOCKS].astype(BF16)
    last_out[...] = col_acc[2 * BLOCKS : COLS].astype(BF16)


def sum_kernel(*refs):
    total = refs[0][...].astype(F32)
    for ref in refs[1:-1]:
        total = total + ref[...].astype(F32)
    refs[-1][...] = total.astype(refs[-1].dtype)


def final_kernel(type_hard, *refs):
    atom_type, krylov, inverse, out, blocked = refs[-5:]
    parts = refs[:-5]

    def add_up(block, carry):
        total = parts[0][block]
        for part in parts[1:]:
            total = total + part[block].astype(F32)
        blocked[block] = total
        return carry

    lax.fori_loop(0, BLOCKS, add_up, 0)
    for chunk in range(BLOCKS):
        wanted = jnp.broadcast_to(inverse[chunk : chunk + 1, :], (8, BLK))
        source = wanted >> 7
        lane = wanted & 127
        span = slice(chunk * BLK, (chunk + 1) * BLK)
        kind = jnp.broadcast_to(atom_type[:, span], (8, BLK))
        hard = jnp.zeros((8, BLK), F32)
        for t in range(NTYPES):
            hard = jnp.where(kind == t, type_hard[t], hard)

        def pick(block, carry, source=source, lane=lane):
            top, low = carry
            here = source == block
            top = jnp.where(here, lane_gather(blocked[block, 0:8, :], lane), top)
            low = jnp.where(here, lane_gather(blocked[block, 8:16, :], lane), low)
            return top, low

        start = (hard * 0.0, hard * 0.0)
        top, low = lax.fori_loop(0, BLOCKS, pick, start, unroll=True)
        out[0:8, span] = top + hard * krylov[0:8, span]
        out[8:16, span] = low + hard * krylov[8:16, span]


def shape(dims, dtype):
    return jax.ShapeDtypeStruct(dims, dtype)


def call(kernel, out_shape, in_specs, out_specs, name, scratch=(), vmem=48, cost=None):
    return pl.pallas_call(
        kernel,
        out_shape=out_shape,
        in_specs=in_specs,
        out_specs=out_specs,
        scratch_shapes=list(scratch),
        compiler_params=pltpu.CompilerParams(vmem_limit_bytes=vmem << 20),
        cost_estimate=cost,
        name=name,
    )


def step_tables():
    level = lax.broadcasted_iota(jnp.int32, (17, 8, BLK), 1)
    which = lax.broadcasted_iota(jnp.int32, (17, 8, BLK), 0)
    along_x = jnp.where(level == 0, CELL[0] * which.astype(F32), jnp.where(level == 7, -1.0, 0.0))
    along_y = jnp.where(level == 1, CELL[1] * (which - 7).astype(F32), 0.0)
    along_z = jnp.where(level == 2, CELL[2] * (which - 14).astype(F32), 0.0)
    return jnp.where(which < 3, along_x, jnp.where(which < 12, along_y, along_z))


def passed_down(value, steps):
    count = lax.axis_size("row")
    return lax.ppermute(value, "row", [(s, s - steps) for s in range(steps, count)])


def passed_up(value, steps):
    count = lax.axis_size("row")
    return lax.ppermute(value, "row", [(s, s + steps) for s in range(count - steps)])


def across(value):
    return lax.ppermute(value, "col", [(c, c ^ 4) for c in range(8)])


def around(value, steps):
    return lax.ppermute(value, "col", [(c, (c & 4) + (c + steps) % 4) for c in range(8)])


def gathered(value):
    return lax.all_gather(value, "col", axis=0, axis_index_groups=Y_GROUPS, tiled=True)


def home_parts(sums):
    position = lax.axis_index("col") % 4
    pieces = [lax.dynamic_slice_in_dim(sums, position * BLOCKS, BLOCKS, 0)]
    for steps in (1, 2, 3):
        target = (position + steps) % 4
        piece = lax.dynamic_slice_in_dim(sums, target * BLOCKS, BLOCKS, 0)
        pieces.append(around(piece, steps))
    return pieces


def on_device(
    positions, atom_type, krylov, block_order, type_width, type_hard, pair_rows, pair_cols, pair_count
):
    place = jnp.stack([lax.axis_index("row"), lax.axis_index("col")]).astype(jnp.int32)
    order = block_order.reshape(BLOCKS, BLK)
    kinds = atom_type.reshape(1, -1)
    slots = pair_rows.size

    packed = call(
        prep_kernel,
        shape((BLOCKS, ROWS, BLK), BF16),
        [SMEM, VMEM, VMEM, VMEM, VMEM],
        VMEM,
        "prep",
        scratch=[pltpu.VMEM((8, BLOCKS * BLK), F32)],
    )(place, positions, kinds, krylov, order)

    other = across(packed)
    after = passed_down(packed, 1)
    second = passed_down(packed, 2)
    half_rows = gathered(packed)

    inverse, codes, counts = call(
        side_kernel,
        (
            shape((BLOCKS, BLK), jnp.int32),
            shape((2 * (slots + 8),), jnp.int32),
            shape((2,), jnp.int32),
        ),
        [SMEM, SMEM, SMEM, SMEM, VMEM],
        (VMEM, SMEM, SMEM),
        "side",
    )(place, pair_rows.reshape(-1), pair_cols.reshape(-1), pair_count.reshape(-1), order)

    features, vectors = call(
        feature_kernel,
        (shape((COLS, BLK, BLK), BF16), shape((COLS, VECS, BLK), BF16)),
        [SMEM, VMEM, VMEM, VMEM],
        (VMEM, VMEM),
        "features",
    )(type_width, packed, after, second)

    cross_rows = gathered(other)
    steps = step_tables()
    accumulators = [
        pltpu.VMEM((HALF + 1, VECS, BLK), F32),
        pltpu.VMEM((COLS + 1, VECS, BLK), F32),
    ]
    half_sums, col_sums = call(
        first_kernel,
        (shape((HALF, VECS, BLK), BF16), shape((COLS, VECS, BLK), F32)),
        [SMEM, SMEM, VMEM, VMEM, VMEM, VMEM],
        (VMEM, VMEM),
        "pairs_near",
        scratch=accumulators,
    )(counts, codes, half_rows, vectors, features, steps)
    near_parts = home_parts(half_sums)

    cross_sums, own_sum, after_sum, last_sum = call(
        second_kernel,
        (
            shape((HALF, VECS, BLK), BF16),
            shape((BLOCKS, VECS, BLK), F32),
            shape((BLOCKS, VECS, BLK), BF16),
            shape((BLOCKS, VECS, BLK), BF16),
        ),
        [SMEM, SMEM, VMEM, VMEM, VMEM, VMEM, VMEM],
        (VMEM, VMEM, VMEM, VMEM),
        "pairs_far",
        scratch=accumulators,
    )(counts, codes, cross_rows, vectors, features, steps, col_sums)

    far_parts = home_parts(cross_sums)
    from_prior = passed_up(after_sum, 1)
    from_second = passed_up(last_sum, 2)
    far_sum = call(
        sum_kernel, shape((BLOCKS, VECS, BLK), BF16), [VMEM] * 4, VMEM, "far_sum"
    )(*far_parts)
    from_far = across(far_sum)

    parts = [own_sum, from_prior, from_second, *near_parts, from_far]
    return call(
        final_kernel,
        shape(krylov.shape, F32),
        [SMEM] + [VMEM] * (len(parts) + 3),
        VMEM,
        "final",
        scratch=[pltpu.VMEM((BLOCKS, VECS, BLK), F32)],
    )(type_hard, *parts, kinds, krylov, inverse)


def solution(mesh):
    placed = (
        P(None, ("row", "col")),
        P(("row", "col")),
        P(None, ("row", "col")),
        P(("row", "col")),
        P(),
        P(),
        P("row", "col", None),
        P("row", "col", None),
        P("row", "col"),
    )
    return jax.shard_map(
        on_device, mesh=mesh, in_specs=placed, out_specs=P(None, ("row", "col")), check_vma=False
    )
```

```python
import functools

import jax
import jax.numpy as jnp
from jax import lax
from jax.experimental import pallas as pl
from jax.experimental.pallas import tpu as pltpu
from jax.sharding import PartitionSpec as P

BLK = 128
VECS = 16
NTYPES = 6
BLOCKS = 32
HALF = 4 * BLOCKS
COLS = 3 * BLOCKS
ROWS = VECS + 8
DEPTH = 80
UNROLL = 8
SLOTS = 512
SLOT_SPAN = SLOTS + UNROLL
CELL = (11.0, 5.0, 11.0)
BOX = (44.0, 30.0, 44.0)
SOFTENING = 0.5

ERF_COEFFS = (
    1.1283815681128107,
    -7.621837438329706e-05,
    0.10341113638200404,
    -0.002217632183960096,
    0.003526363187890101,
    -0.0031284691084128495,
    0.0005233424709803657,
)

PAIR_COST = pl.CostEstimate(flops=16_000_000_000, transcendentals=0, bytes_accessed=8_000_000)

VMEM = pl.BlockSpec(memory_space=pltpu.VMEM)
SMEM = pl.BlockSpec(memory_space=pltpu.SMEM)
Y_GROUPS = [[0, 1, 2, 3], [4, 5, 6, 7]]
F32 = jnp.float32
BF16 = jnp.bfloat16


def sublane():
    return lax.broadcasted_iota(jnp.int32, (8, BLK), 0)


def split3(value):
    high = value.astype(BF16).astype(F32)
    rest = value - high
    middle = rest.astype(BF16).astype(F32)
    return high, middle, rest - middle


def lane_gather(source, index):
    return jnp.take_along_axis(source, index, axis=1, mode="promise_in_bounds")


def prep_kernel(place, positions, atom_type, krylov, order, packed, geometry):
    geometry[...] = jnp.zeros_like(geometry)
    geometry[0:3, :] = positions[...]
    geometry[3:4, :] = atom_type[...].astype(F32)
    level = sublane()
    corner_x = CELL[0] * place[0].astype(F32) + BOX[0] / 2
    corner_y = CELL[1] * place[1].astype(F32) + BOX[1] / 2

    def one_block(block, carry):
        wanted = jnp.broadcast_to(order[pl.ds(block, 1), :], (8, BLK))
        chunk = wanted >> 7
        lane = wanted & 127
        top = jnp.zeros((8, BLK), F32)
        low = jnp.zeros((8, BLK), F32)
        geo = jnp.zeros((8, BLK), F32)
        for s in range(BLOCKS):
            here = chunk == s
            span = slice(s * BLK, (s + 1) * BLK)
            top = jnp.where(here, lane_gather(krylov[0:8, span], lane), top)
            low = jnp.where(here, lane_gather(krylov[8:16, span], lane), low)
            geo = jnp.where(here, lane_gather(geometry[:, span], lane), geo)
        corner_z = CELL[2] * block.astype(F32) + BOX[2] / 2
        corner = jnp.where(
            level == 0, corner_x, jnp.where(level == 1, corner_y, jnp.where(level == 2, corner_z, 0.0))
        )
        local = geo - corner
        coarse = jnp.floor(local * 4.0 + 0.5) * 0.25
        fine = jnp.where(level < 3, local - coarse, local)
        coded = jnp.where(level < 3, coarse, pltpu.roll(fine, 3, 0))
        packed[block, 0:VECS, :] = jnp.concatenate([top, low], axis=0).astype(BF16)
        packed[block, VECS:ROWS, :] = coded.astype(BF16)
        return carry

    lax.fori_loop(0, BLOCKS, one_block, 0)


def side_kernel(place, rows, cols, count, order, inverse, codes, counts):
    row_index = place[0]
    col_index = place[1]
    own_half = col_index >> 2

    live = count[0]

    def some_slots(turn, seen):
        first, second = seen
        for extra in range(4):
            slot = turn * 4 + extra
            row = rows[slot]
            col = cols[slot] - row_index * BLOCKS
            same = (row >> 7) == own_half
            diagonal = jnp.logical_and(col < BLOCKS, row == col_index * BLOCKS + col)
            code = (
                (row & 127)
                | (col << 7)
                | ((col_index - (row >> 5) + 4) << 14)
                | (((col & 31) - (row & 31) + 2) << 18)
                | (diagonal.astype(jnp.int32) << 21)
            )
            used = slot < live
            target = jnp.where(same, first, SLOT_SPAN + second)
            codes[jnp.where(used, target, 2 * SLOT_SPAN)] = code
            one = jnp.logical_and(used, same).astype(jnp.int32)
            second = second + used.astype(jnp.int32) - one
            first = first + one
        return first, second

    first, second = lax.fori_loop(0, (live + 3) // 4, some_slots, (jnp.int32(0), jnp.int32(0)))
    spare = (4 << 14) | (2 << 18) | (1 << 21) | (1 << 22)
    for extra in range(UNROLL):
        codes[first + extra] = spare
        codes[SLOT_SPAN + second + extra] = spare
    counts[0] = first
    counts[1] = second

    level_h = lax.broadcasted_iota(jnp.int32, (BLOCKS, BLK), 0)
    level_l = lax.broadcasted_iota(jnp.int32, (BLK, BLK), 0)
    lanes = lax.broadcasted_iota(jnp.int32, (BLOCKS, BLK), 1).astype(F32)
    total = jnp.zeros((2 * BLOCKS, BLK), F32)
    for block in range(BLOCKS):
        wanted = order[block : block + 1, :]
        in_high = (level_h == jnp.broadcast_to(wanted >> 7, (BLOCKS, BLK))).astype(F32)
        in_low = (level_l == jnp.broadcast_to(wanted & 127, (BLK, BLK))).astype(F32).astype(BF16)
        left = jnp.concatenate([in_high * float(block), in_high * lanes], axis=0).astype(BF16)
        total = total + lax.dot_general(
            left, in_low, (((1,), (1,)), ((), ())), preferred_element_type=F32
        )
    inverse[...] = (total[0:BLOCKS] * float(BLK) + total[BLOCKS:]).astype(jnp.int32)


def feature_kernel(type_width, own, after, second, features, vectors):
    level = sublane()
    squares = jnp.zeros((8, BLK), F32)
    for t in range(NTYPES):
        squares = jnp.where(level == t, type_width[t] * type_width[t], squares)
    low3 = level < 3
    low6 = level < 6
    last = level == 7
    zero = jnp.zeros((8, BLK), F32)
    ones = jnp.where(low6, 1.0, 0.0)
    twos = jnp.where(jnp.logical_and(low6, level >= 3), 2.0, 0.0)

    for part, source in enumerate((own, after, second)):

        def one_block(block, part=part, source=source):
            vectors[part * BLOCKS + block] = source[block, 0:VECS, :]
            coded = source[block, VECS:ROWS, :].astype(F32)
            near = coded + pltpu.roll(coded, 5, 0)
            square = near * near
            weight = square[0:1] + square[1:2] + square[2:3] + SOFTENING * SOFTENING
            weight_h, weight_m, weight_l = split3(weight)
            coarse = jnp.where(low3, coded, pltpu.roll(coded, 3, 0)) * -2.0
            fine = jnp.where(low3, pltpu.roll(coded, 5, 0), coded) * -2.0
            own_type = jnp.broadcast_to(coded[6:7], (8, BLK))
            own_square = jnp.zeros((8, BLK), F32)
            for t in range(NTYPES):
                own_square = jnp.where(own_type == float(t), type_width[t] * type_width[t], own_square)
            scale = lax.rsqrt(own_square + squares)
            scale_h, scale_m, scale_l = split3(jnp.where(low6, scale, 0.0))
            wide = lambda v: jnp.broadcast_to(v, (8, BLK))
            stacked = jnp.concatenate(
                [
                    jnp.where(low6, coarse, jnp.where(last, wide(weight_h), 0.0)),
                    jnp.where(low6, fine, jnp.where(last, wide(weight_m), 0.0)),
                    jnp.where(last, wide(weight_l), ones),
                    ones,
                    twos,
                    twos,
                    scale_h,
                    scale_m,
                    scale_l,
                ]
                + [zero] * 7,
                axis=0,
            )
            features[part * BLOCKS + block] = stacked.T.astype(BF16)

        def some_blocks(turn, carry, one_block=one_block):
            for extra in range(4):
                one_block(turn * 4 + extra)
            return carry

        lax.fori_loop(0, BLOCKS // 4, some_blocks, 0)


def pair_operand(code, row_data, steps):
    coded = row_data[code & 127, VECS:ROWS, :].astype(F32)
    col = (code >> 7) & 127
    shift = steps[col >> 5] + steps[3 + ((code >> 14) & 15)] + steps[12 + ((code >> 18) & 7)]
    near = coded - shift
    square = near * near
    cross = near * pltpu.roll(near, 3, 0)
    square_h = square.astype(BF16).astype(F32)
    cross_h = cross.astype(BF16).astype(F32)
    hot = (sublane().astype(F32) == jnp.broadcast_to(coded[6:7], (8, BLK))).astype(F32)
    zero = jnp.zeros((8, BLK), F32)
    left = jnp.concatenate(
        [near, near, square_h, square - square_h, cross_h, cross - cross_h, zero, zero, zero, zero],
        axis=0,
    ).astype(BF16)
    right = jnp.concatenate([zero] * 6 + [hot, hot, hot, zero], axis=0).astype(BF16)
    return jnp.concatenate([left, right], axis=1)


def tile_values(distance2, scale):
    inverse = lax.rsqrt(distance2)
    z = distance2 * inverse * scale
    poly = ERF_COEFFS[-1]
    for coefficient in ERF_COEFFS[-2::-1]:
        poly = poly * z + coefficient
    return (jnp.tanh(poly * z) * inverse).astype(BF16)


def pair_loop(phase, counts, codes, row_data, vectors, features, steps, row_acc, col_acc, waiting, tiles):
    base = phase * SLOT_SPAN
    batches = (counts[phase] + UNROLL - 1) // UNROLL

    def one_turn(turn, carry):
        adding = base + jnp.maximum(turn - 2, 0) * UNROLL
        opening = base + jnp.maximum(jnp.minimum(turn, batches - 1), 0) * UNROLL
        sums = []
        for first in range(0, UNROLL, 2):
            done = [codes[adding + first + k] for k in range(2)]
            both = [tiles[first + k] for k in range(2)]
            forward = jnp.dot(
                jnp.concatenate([vectors[(code >> 7) & 127] for code in done], axis=0),
                jnp.concatenate(both, axis=1),
                preferred_element_type=F32,
            )
            backward = lax.dot_general(
                jnp.concatenate([row_data[code & 127, 0:VECS, :] for code in done], axis=0),
                jnp.concatenate(both, axis=0),
                (((1,), (1,)), ((), ())),
                preferred_element_type=F32,
            )
            for k, code in enumerate(done):
                to_row = jnp.where(jnp.logical_or(turn < 2, ((code >> 22) & 1) == 1), HALF, code & 127)
                to_col = jnp.where(
                    jnp.logical_or(turn < 2, ((code >> 21) & 1) == 1), COLS, (code >> 7) & 127
                )
                own = (slice(k * VECS, (k + 1) * VECS), slice(k * BLK, (k + 1) * BLK))
                sums.append((to_row, forward[own], to_col, backward[own]))
            for k in range(2):
                slot = first + k
                tiles[slot] = tile_values(waiting[slot, :, 0:BLK], waiting[slot, :, BLK:])
                code = codes[opening + slot]
                waiting[slot] = jnp.dot(
                    features[(code >> 7) & 127][:, 0:DEPTH],
                    pair_operand(code, row_data, steps),
                    preferred_element_type=F32,
                )
        for to_row, forward, to_col, backward in sums:
            row_acc[to_row] += forward
            col_acc[to_col] += backward
        return carry

    lax.fori_loop(0, batches + 2, one_turn, 0)


def near_far_kernel(phase, *refs):
    place, counts, codes = refs[0:3]
    pieces = refs[3:7]
    vectors, features, steps = refs[7:10]
    col_in = refs[10:11] if phase == 1 else ()
    outs = refs[10 + len(col_in) : -5]
    row_data, row_acc, col_acc, waiting, tiles = refs[-5:]
    position = place[1] & 3
    for k, piece in enumerate(pieces):
        start = pl.multiple_of(((position - k) & 3) * BLOCKS, BLOCKS)
        row_data[pl.ds(start, BLOCKS)] = piece[...]
    row_acc[...] = jnp.zeros_like(row_acc)
    if phase == 0:
        col_acc[...] = jnp.zeros_like(col_acc)
    else:
        col_acc[0:COLS] = col_in[0][...]
    pair_loop(phase, counts, codes, row_data, vectors, features, steps, row_acc, col_acc, waiting, tiles)
    for k in range(4):
        start = pl.multiple_of(((position + k) & 3) * BLOCKS, BLOCKS)
        outs[k][...] = row_acc[pl.ds(start, BLOCKS)].astype(outs[k].dtype)
    if phase == 0:
        outs[4][...] = col_acc[0:COLS]
    else:
        for step in range(3):
            outs[4 + step][...] = col_acc[step * BLOCKS : (step + 1) * BLOCKS].astype(outs[4 + step].dtype)


def sum_kernel(*refs):
    total = refs[0][...].astype(F32)
    for ref in refs[1:-1]:
        total = total + ref[...].astype(F32)
    refs[-1][...] = total.astype(refs[-1].dtype)


def final_kernel(type_hard, *refs):
    atom_type, krylov, inverse, out, blocked = refs[-5:]
    parts = refs[:-5]

    def add_up(block, carry):
        total = parts[0][block]
        for part in parts[1:]:
            total = total + part[block].astype(F32)
        blocked[block] = total
        return carry

    lax.fori_loop(0, BLOCKS, add_up, 0)
    for chunk in range(BLOCKS):
        wanted = jnp.broadcast_to(inverse[chunk : chunk + 1, :], (8, BLK))
        source = wanted >> 7
        lane = wanted & 127
        span = slice(chunk * BLK, (chunk + 1) * BLK)
        kind = jnp.broadcast_to(atom_type[:, span], (8, BLK))
        hard = jnp.zeros((8, BLK), F32)
        for t in range(NTYPES):
            hard = jnp.where(kind == t, type_hard[t], hard)

        def pick(block, carry, source=source, lane=lane):
            top, low = carry
            here = source == block
            top = jnp.where(here, lane_gather(blocked[block, 0:8, :], lane), top)
            low = jnp.where(here, lane_gather(blocked[block, 8:16, :], lane), low)
            return top, low

        start = (hard * 0.0, hard * 0.0)
        top, low = lax.fori_loop(0, BLOCKS, pick, start, unroll=True)
        out[0:8, span] = top + hard * krylov[0:8, span]
        out[8:16, span] = low + hard * krylov[8:16, span]


def shape(dims, dtype):
    return jax.ShapeDtypeStruct(dims, dtype)


def call(kernel, out_shape, in_specs, out_specs, name, scratch=(), vmem=48, cost=None):
    return pl.pallas_call(
        kernel,
        out_shape=out_shape,
        in_specs=in_specs,
        out_specs=out_specs,
        scratch_shapes=list(scratch),
        compiler_params=pltpu.CompilerParams(vmem_limit_bytes=vmem << 20),
        cost_estimate=cost,
        name=name,
    )


def step_tables():
    level = lax.broadcasted_iota(jnp.int32, (17, 8, BLK), 1)
    which = lax.broadcasted_iota(jnp.int32, (17, 8, BLK), 0)
    along_x = jnp.where(level == 0, CELL[0] * which.astype(F32), jnp.where(level == 7, -1.0, 0.0))
    along_y = jnp.where(level == 1, CELL[1] * (which - 7).astype(F32), 0.0)
    along_z = jnp.where(level == 2, CELL[2] * (which - 14).astype(F32), 0.0)
    return jnp.where(which < 3, along_x, jnp.where(which < 12, along_y, along_z))


def passed_down(value, steps):
    count = lax.axis_size("row")
    return lax.ppermute(value, "row", [(s, s - steps) for s in range(steps, count)])


def passed_up(value, steps):
    count = lax.axis_size("row")
    return lax.ppermute(value, "row", [(s, s + steps) for s in range(count - steps)])


def across(value):
    return lax.ppermute(value, "col", [(c, c ^ 4) for c in range(8)])


def around(value, steps):
    return lax.ppermute(value, "col", [(c, (c & 4) + (c + steps) % 4) for c in range(8)])


def on_device(
    positions, atom_type, krylov, block_order, type_width, type_hard, pair_rows, pair_cols, pair_count
):
    place = jnp.stack([lax.axis_index("row"), lax.axis_index("col")]).astype(jnp.int32)
    order = block_order.reshape(BLOCKS, BLK)
    kinds = atom_type.reshape(1, -1)

    packed = call(
        prep_kernel,
        shape((BLOCKS, ROWS, BLK), BF16),
        [SMEM, VMEM, VMEM, VMEM, VMEM],
        VMEM,
        "prep",
        scratch=[pltpu.VMEM((8, BLOCKS * BLK), F32)],
    )(place, positions, kinds, krylov, order)

    other = across(packed)
    near_rows = [packed] + [around(packed, k) for k in (1, 2, 3)]
    after = passed_down(packed, 1)
    second = passed_down(packed, 2)
    far_rows = [other] + [around(other, k) for k in (1, 2, 3)]

    inverse, codes, counts = call(
        side_kernel,
        (
            shape((BLOCKS, BLK), jnp.int32),
            shape((2 * SLOT_SPAN + 1,), jnp.int32),
            shape((2,), jnp.int32),
        ),
        [SMEM, SMEM, SMEM, SMEM, VMEM],
        (VMEM, SMEM, SMEM),
        "side",
    )(place, pair_rows.reshape(-1), pair_cols.reshape(-1), pair_count.reshape(-1), order)

    features, vectors = call(
        feature_kernel,
        (shape((COLS, BLK, BLK), BF16), shape((COLS, VECS, BLK), BF16)),
        [SMEM, VMEM, VMEM, VMEM],
        (VMEM, VMEM),
        "features",
    )(type_width, packed, after, second)

    steps = step_tables()
    scratch = [
        pltpu.VMEM((HALF, ROWS, BLK), BF16),
        pltpu.VMEM((HALF + 1, VECS, BLK), F32),
        pltpu.VMEM((COLS + 1, VECS, BLK), F32),
        pltpu.VMEM((UNROLL, BLK, 2 * BLK), F32),
        pltpu.VMEM((UNROLL, BLK, BLK), BF16),
    ]
    block_set = (BLOCKS, VECS, BLK)
    *near_sums, col_sums = call(
        functools.partial(near_far_kernel, 0),
        [shape(block_set, F32)] + [shape(block_set, BF16)] * 3 + [shape((COLS, VECS, BLK), F32)],
        [SMEM] * 3 + [VMEM] * 7,
        [VMEM] * 5,
        "pairs_near",
        scratch=scratch,
        cost=PAIR_COST,
    )(place, counts, codes, *near_rows, vectors, features, steps)
    near_parts = [near_sums[0]] + [around(near_sums[k], k) for k in (1, 2, 3)]

    *far_sums, own_sum, after_sum, last_sum = call(
        functools.partial(near_far_kernel, 1),
        [shape(block_set, BF16)] * 4 + [shape(block_set, F32)] + [shape(block_set, BF16)] * 2,
        [SMEM] * 3 + [VMEM] * 8,
        [VMEM] * 7,
        "pairs_far",
        scratch=scratch,
        cost=PAIR_COST,
    )(place, counts, codes, *far_rows, vectors, features, steps, col_sums)

    far_parts = [far_sums[0]] + [around(far_sums[k], k) for k in (1, 2, 3)]
    from_prior = passed_up(after_sum, 1)
    from_second = passed_up(last_sum, 2)
    far_sum = call(
        sum_kernel, shape((BLOCKS, VECS, BLK), BF16), [VMEM] * 4, VMEM, "far_sum"
    )(*far_parts)
    from_far = across(far_sum)

    parts = [own_sum, from_prior, from_second, *near_parts, from_far]
    return call(
        final_kernel,
        shape(krylov.shape, F32),
        [SMEM] + [VMEM] * (len(parts) + 3),
        VMEM,
        "final",
        scratch=[pltpu.VMEM((BLOCKS, VECS, BLK), F32)],
    )(type_hard, *parts, kinds, krylov, inverse)


def solution(mesh):
    placed = (
        P(None, ("row", "col")),
        P(("row", "col")),
        P(None, ("row", "col")),
        P(("row", "col")),
        P(),
        P(),
        P("row", "col", None),
        P("row", "col", None),
        P("row", "col"),
    )
    return jax.shard_map(
        on_device, mesh=mesh, in_specs=placed, out_specs=P(None, ("row", "col")), check_vma=False
    )
```

```python
import functools

import jax
import jax.numpy as jnp
from jax import lax
from jax.experimental import pallas as pl
from jax.experimental.pallas import tpu as pltpu
from jax.sharding import PartitionSpec as P

BLK = 128
VECS = 16
NTYPES = 6
BLOCKS = 32
HALF = 4 * BLOCKS
COLS = 3 * BLOCKS
ROWS = VECS + 8
DEPTH = 80
UNROLL = 8
SLOTS = 512
SLOT_SPAN = SLOTS + UNROLL
CELL = (11.0, 5.0, 11.0)
BOX = (44.0, 30.0, 44.0)
SOFTENING = 0.5

ERF_COEFFS = (
    1.1283815681128107,
    -7.621837438329706e-05,
    0.10341113638200404,
    -0.002217632183960096,
    0.003526363187890101,
    -0.0031284691084128495,
    0.0005233424709803657,
)


def time_cost(microseconds):
    return pl.CostEstimate(
        flops=int(microseconds * 1_000_000_000), transcendentals=0, bytes_accessed=1_000_000
    )


PAIR_COST = time_cost(16)

VMEM = pl.BlockSpec(memory_space=pltpu.VMEM)
SMEM = pl.BlockSpec(memory_space=pltpu.SMEM)
Y_GROUPS = [[0, 1, 2, 3], [4, 5, 6, 7]]
F32 = jnp.float32
BF16 = jnp.bfloat16


def sublane():
    return lax.broadcasted_iota(jnp.int32, (8, BLK), 0)


def split3(value):
    high = value.astype(BF16).astype(F32)
    rest = value - high
    middle = rest.astype(BF16).astype(F32)
    return high, middle, rest - middle


def lane_gather(source, index):
    return jnp.take_along_axis(source, index, axis=1, mode="promise_in_bounds")


def prep_kernel(place, positions, atom_type, krylov, order, packed, geometry):
    geometry[...] = jnp.zeros_like(geometry)
    geometry[0:3, :] = positions[...]
    geometry[3:4, :] = atom_type[...].astype(F32)
    level = sublane()
    corner_x = CELL[0] * place[0].astype(F32) + BOX[0] / 2
    corner_y = CELL[1] * place[1].astype(F32) + BOX[1] / 2

    def one_block(block, carry):
        wanted = jnp.broadcast_to(order[pl.ds(block, 1), :], (8, BLK))
        chunk = wanted >> 7
        lane = wanted & 127
        top = jnp.zeros((8, BLK), F32)
        low = jnp.zeros((8, BLK), F32)
        geo = jnp.zeros((8, BLK), F32)
        for s in range(BLOCKS):
            here = chunk == s
            span = slice(s * BLK, (s + 1) * BLK)
            top = jnp.where(here, lane_gather(krylov[0:8, span], lane), top)
            low = jnp.where(here, lane_gather(krylov[8:16, span], lane), low)
            geo = jnp.where(here, lane_gather(geometry[:, span], lane), geo)
        corner_z = CELL[2] * block.astype(F32) + BOX[2] / 2
        corner = jnp.where(
            level == 0, corner_x, jnp.where(level == 1, corner_y, jnp.where(level == 2, corner_z, 0.0))
        )
        local = geo - corner
        coarse = jnp.floor(local * 4.0 + 0.5) * 0.25
        fine = jnp.where(level < 3, local - coarse, local)
        coded = jnp.where(level < 3, coarse, pltpu.roll(fine, 3, 0))
        packed[block, 0:VECS, :] = jnp.concatenate([top, low], axis=0).astype(BF16)
        packed[block, VECS:ROWS, :] = coded.astype(BF16)
        return carry

    lax.fori_loop(0, BLOCKS, one_block, 0)


def side_kernel(place, rows, cols, count, order, inverse, codes, counts):
    row_index = place[0]
    col_index = place[1]
    own_half = col_index >> 2

    live = count[0]

    def some_slots(turn, seen):
        first, second = seen
        for extra in range(4):
            slot = turn * 4 + extra
            row = rows[slot]
            col = cols[slot] - row_index * BLOCKS
            same = (row >> 7) == own_half
            diagonal = jnp.logical_and(col < BLOCKS, row == col_index * BLOCKS + col)
            code = (
                (row & 127)
                | (col << 7)
                | ((col_index - (row >> 5) + 4) << 14)
                | (((col & 31) - (row & 31) + 2) << 18)
                | (diagonal.astype(jnp.int32) << 21)
            )
            used = slot < live
            target = jnp.where(same, first, SLOT_SPAN + second)
            codes[jnp.where(used, target, 2 * SLOT_SPAN)] = code
            one = jnp.logical_and(used, same).astype(jnp.int32)
            second = second + used.astype(jnp.int32) - one
            first = first + one
        return first, second

    first, second = lax.fori_loop(0, (live + 3) // 4, some_slots, (jnp.int32(0), jnp.int32(0)))
    spare = (4 << 14) | (2 << 18) | (1 << 21) | (1 << 22)
    for extra in range(UNROLL):
        codes[first + extra] = spare
        codes[SLOT_SPAN + second + extra] = spare
    counts[0] = first
    counts[1] = second

    level_h = lax.broadcasted_iota(jnp.int32, (BLOCKS, BLK), 0)
    level_l = lax.broadcasted_iota(jnp.int32, (BLK, BLK), 0)
    lanes = lax.broadcasted_iota(jnp.int32, (BLOCKS, BLK), 1).astype(F32)
    total = jnp.zeros((2 * BLOCKS, BLK), F32)
    for block in range(BLOCKS):
        wanted = order[block : block + 1, :]
        in_high = (level_h == jnp.broadcast_to(wanted >> 7, (BLOCKS, BLK))).astype(F32)
        in_low = (level_l == jnp.broadcast_to(wanted & 127, (BLK, BLK))).astype(F32).astype(BF16)
        left = jnp.concatenate([in_high * float(block), in_high * lanes], axis=0).astype(BF16)
        total = total + lax.dot_general(
            left, in_low, (((1,), (1,)), ((), ())), preferred_element_type=F32
        )
    inverse[...] = (total[0:BLOCKS] * float(BLK) + total[BLOCKS:]).astype(jnp.int32)


def feature_kernel(type_width, own, after, second, features, vectors):
    level = sublane()
    squares = jnp.zeros((8, BLK), F32)
    for t in range(NTYPES):
        squares = jnp.where(level == t, type_width[t] * type_width[t], squares)
    low3 = level < 3
    low6 = level < 6
    last = level == 7
    zero = jnp.zeros((8, BLK), F32)
    ones = jnp.where(low6, 1.0, 0.0)
    twos = jnp.where(jnp.logical_and(low6, level >= 3), 2.0, 0.0)

    for part, source in enumerate((own, after, second)):

        def one_block(block, part=part, source=source):
            vectors[part * BLOCKS + block] = source[block, 0:VECS, :]
            coded = source[block, VECS:ROWS, :].astype(F32)
            near = coded + pltpu.roll(coded, 5, 0)
            square = near * near
            weight = square[0:1] + square[1:2] + square[2:3] + SOFTENING * SOFTENING
            weight_h, weight_m, weight_l = split3(weight)
            coarse = jnp.where(low3, coded, pltpu.roll(coded, 3, 0)) * -2.0
            fine = jnp.where(low3, pltpu.roll(coded, 5, 0), coded) * -2.0
            own_type = jnp.broadcast_to(coded[6:7], (8, BLK))
            own_square = jnp.zeros((8, BLK), F32)
            for t in range(NTYPES):
                own_square = jnp.where(own_type == float(t), type_width[t] * type_width[t], own_square)
            scale = lax.rsqrt(own_square + squares)
            scale_h, scale_m, scale_l = split3(jnp.where(low6, scale, 0.0))
            wide = lambda v: jnp.broadcast_to(v, (8, BLK))
            stacked = jnp.concatenate(
                [
                    jnp.where(low6, coarse, jnp.where(last, wide(weight_h), 0.0)),
                    jnp.where(low6, fine, jnp.where(last, wide(weight_m), 0.0)),
                    jnp.where(last, wide(weight_l), ones),
                    ones,
                    twos,
                    twos,
                    scale_h,
                    scale_m,
                    scale_l,
                ]
                + [zero] * 7,
                axis=0,
            )
            features[part * BLOCKS + block] = stacked.T.astype(BF16)

        def some_blocks(turn, carry, one_block=one_block):
            for extra in range(4):
                one_block(turn * 4 + extra)
            return carry

        lax.fori_loop(0, BLOCKS // 4, some_blocks, 0)


def pair_operand(code, row_data, steps):
    coded = row_data[code & 127, VECS:ROWS, :].astype(F32)
    col = (code >> 7) & 127
    shift = steps[col >> 5] + steps[3 + ((code >> 14) & 15)] + steps[12 + ((code >> 18) & 7)]
    near = coded - shift
    square = near * near
    cross = near * pltpu.roll(near, 3, 0)
    square_h = square.astype(BF16).astype(F32)
    cross_h = cross.astype(BF16).astype(F32)
    hot = (sublane().astype(F32) == jnp.broadcast_to(coded[6:7], (8, BLK))).astype(F32)
    zero = jnp.zeros((8, BLK), F32)
    left = jnp.concatenate(
        [near, near, square_h, square - square_h, cross_h, cross - cross_h, zero, zero, zero, zero],
        axis=0,
    ).astype(BF16)
    right = jnp.concatenate([zero] * 6 + [hot, hot, hot, zero], axis=0).astype(BF16)
    return jnp.concatenate([left, right], axis=1)


def tile_values(distance2, scale):
    inverse = lax.rsqrt(distance2)
    z = distance2 * inverse * scale
    poly = ERF_COEFFS[-1]
    for coefficient in ERF_COEFFS[-2::-1]:
        poly = poly * z + coefficient
    return (jnp.tanh(poly * z) * inverse).astype(BF16)


def pair_loop(phase, counts, codes, row_data, vectors, features, steps, row_acc, col_acc, waiting, tiles):
    base = phase * SLOT_SPAN
    batches = (counts[phase] + UNROLL - 1) // UNROLL

    def one_turn(turn, carry):
        adding = base + jnp.maximum(turn - 2, 0) * UNROLL
        opening = base + jnp.maximum(jnp.minimum(turn, batches - 1), 0) * UNROLL
        sums = []
        for first in range(0, UNROLL, 2):
            done = [codes[adding + first + k] for k in range(2)]
            both = [tiles[first + k] for k in range(2)]
            forward = jnp.dot(
                jnp.concatenate([vectors[(code >> 7) & 127] for code in done], axis=0),
                jnp.concatenate(both, axis=1),
                preferred_element_type=F32,
            )
            backward = lax.dot_general(
                jnp.concatenate([row_data[code & 127, 0:VECS, :] for code in done], axis=0),
                jnp.concatenate(both, axis=0),
                (((1,), (1,)), ((), ())),
                preferred_element_type=F32,
            )
            for k, code in enumerate(done):
                to_row = jnp.where(jnp.logical_or(turn < 2, ((code >> 22) & 1) == 1), HALF, code & 127)
                to_col = jnp.where(
                    jnp.logical_or(turn < 2, ((code >> 21) & 1) == 1), COLS, (code >> 7) & 127
                )
                own = (slice(k * VECS, (k + 1) * VECS), slice(k * BLK, (k + 1) * BLK))
                sums.append((to_row, forward[own], to_col, backward[own]))
            for k in range(2):
                slot = first + k
                tiles[slot] = tile_values(waiting[slot, :, 0:BLK], waiting[slot, :, BLK:])
                code = codes[opening + slot]
                waiting[slot] = jnp.dot(
                    features[(code >> 7) & 127][:, 0:DEPTH],
                    pair_operand(code, row_data, steps),
                    preferred_element_type=F32,
                )
        for to_row, forward, to_col, backward in sums:
            row_acc[to_row] += forward
            col_acc[to_col] += backward
        return carry

    lax.fori_loop(0, batches + 2, one_turn, 0)


def near_far_kernel(phase, *refs):
    place, counts, codes = refs[0:3]
    pieces = refs[3:7]
    vectors, features, steps = refs[7:10]
    col_in = refs[10:11] if phase == 1 else ()
    outs = refs[10 + len(col_in) : -5]
    row_data, row_acc, col_acc, waiting, tiles = refs[-5:]
    position = place[1] & 3
    for k, piece in enumerate(pieces):
        start = pl.multiple_of(((position - k) & 3) * BLOCKS, BLOCKS)
        row_data[pl.ds(start, BLOCKS)] = piece[...]
    row_acc[...] = jnp.zeros_like(row_acc)
    if phase == 0:
        col_acc[...] = jnp.zeros_like(col_acc)
    else:
        col_acc[0:COLS] = col_in[0][...]
    pair_loop(phase, counts, codes, row_data, vectors, features, steps, row_acc, col_acc, waiting, tiles)
    for k in range(4):
        start = pl.multiple_of(((position + k) & 3) * BLOCKS, BLOCKS)
        outs[k][...] = row_acc[pl.ds(start, BLOCKS)].astype(outs[k].dtype)
    if phase == 0:
        outs[4][...] = col_acc[0:COLS]
    else:
        for step in range(3):
            outs[4 + step][...] = col_acc[step * BLOCKS : (step + 1) * BLOCKS].astype(outs[4 + step].dtype)


def sum_kernel(*refs):
    total = refs[0][...].astype(F32)
    for ref in refs[1:-1]:
        total = total + ref[...].astype(F32)
    refs[-1][...] = total.astype(refs[-1].dtype)


def final_kernel(type_hard, *refs):
    atom_type, krylov, inverse, out, blocked = refs[-5:]
    parts = refs[:-5]

    def add_up(block, carry):
        total = parts[0][block]
        for part in parts[1:]:
            total = total + part[block].astype(F32)
        blocked[block] = total
        return carry

    lax.fori_loop(0, BLOCKS, add_up, 0)
    for chunk in range(BLOCKS):
        wanted = jnp.broadcast_to(inverse[chunk : chunk + 1, :], (8, BLK))
        source = wanted >> 7
        lane = wanted & 127
        span = slice(chunk * BLK, (chunk + 1) * BLK)
        kind = jnp.broadcast_to(atom_type[:, span], (8, BLK))
        hard = jnp.zeros((8, BLK), F32)
        for t in range(NTYPES):
            hard = jnp.where(kind == t, type_hard[t], hard)

        def pick(block, carry, source=source, lane=lane):
            top, low = carry
            here = source == block
            top = jnp.where(here, lane_gather(blocked[block, 0:8, :], lane), top)
            low = jnp.where(here, lane_gather(blocked[block, 8:16, :], lane), low)
            return top, low

        start = (hard * 0.0, hard * 0.0)
        top, low = lax.fori_loop(0, BLOCKS, pick, start, unroll=True)
        out[0:8, span] = top + hard * krylov[0:8, span]
        out[8:16, span] = low + hard * krylov[8:16, span]


def shape(dims, dtype):
    return jax.ShapeDtypeStruct(dims, dtype)


def call(kernel, out_shape, in_specs, out_specs, name, scratch=(), vmem=48, cost=None):
    return pl.pallas_call(
        kernel,
        out_shape=out_shape,
        in_specs=in_specs,
        out_specs=out_specs,
        scratch_shapes=list(scratch),
        compiler_params=pltpu.CompilerParams(vmem_limit_bytes=vmem << 20),
        cost_estimate=cost,
        name=name,
    )


def step_tables():
    level = lax.broadcasted_iota(jnp.int32, (17, 8, BLK), 1)
    which = lax.broadcasted_iota(jnp.int32, (17, 8, BLK), 0)
    along_x = jnp.where(level == 0, CELL[0] * which.astype(F32), jnp.where(level == 7, -1.0, 0.0))
    along_y = jnp.where(level == 1, CELL[1] * (which - 7).astype(F32), 0.0)
    along_z = jnp.where(level == 2, CELL[2] * (which - 14).astype(F32), 0.0)
    return jnp.where(which < 3, along_x, jnp.where(which < 12, along_y, along_z))


def passed_down(value, steps):
    count = lax.axis_size("row")
    return lax.ppermute(value, "row", [(s, s - steps) for s in range(steps, count)])


def passed_up(value, steps):
    count = lax.axis_size("row")
    return lax.ppermute(value, "row", [(s, s + steps) for s in range(count - steps)])


def across(value):
    return lax.ppermute(value, "col", [(c, c ^ 4) for c in range(8)])


def around(value, steps):
    return lax.ppermute(value, "col", [(c, (c & 4) + (c + steps) % 4) for c in range(8)])


def on_device(
    positions, atom_type, krylov, block_order, type_width, type_hard, pair_rows, pair_cols, pair_count
):
    place = jnp.stack([lax.axis_index("row"), lax.axis_index("col")]).astype(jnp.int32)
    order = block_order.reshape(BLOCKS, BLK)
    kinds = atom_type.reshape(1, -1)

    packed = call(
        prep_kernel,
        shape((BLOCKS, ROWS, BLK), BF16),
        [SMEM, VMEM, VMEM, VMEM, VMEM],
        VMEM,
        "prep",
        scratch=[pltpu.VMEM((8, BLOCKS * BLK), F32)],
    )(place, positions, kinds, krylov, order)

    other = across(packed)
    after = passed_down(packed, 1)
    second = passed_down(packed, 2)
    rows_list, _ = lax.optimization_barrier((pair_rows.reshape(-1), packed))

    inverse, codes, counts = call(
        side_kernel,
        (
            shape((BLOCKS, BLK), jnp.int32),
            shape((2 * SLOT_SPAN + 1,), jnp.int32),
            shape((2,), jnp.int32),
        ),
        [SMEM, SMEM, SMEM, SMEM, VMEM],
        (VMEM, SMEM, SMEM),
        "side",
        cost=time_cost(12),
    )(place, rows_list, pair_cols.reshape(-1), pair_count.reshape(-1), order)

    near_rows = [packed] + [around(packed, k) for k in (1, 2, 3)]

    features, vectors = call(
        feature_kernel,
        (shape((COLS, BLK, BLK), BF16), shape((COLS, VECS, BLK), BF16)),
        [SMEM, VMEM, VMEM, VMEM],
        (VMEM, VMEM),
        "features",
        cost=time_cost(5),
    )(type_width, packed, after, second)

    far_rows = [other] + [around(other, k) for k in (1, 2, 3)]
    steps, _ = lax.optimization_barrier((step_tables(), other))
    scratch = [
        pltpu.VMEM((HALF, ROWS, BLK), BF16),
        pltpu.VMEM((HALF + 1, VECS, BLK), F32),
        pltpu.VMEM((COLS + 1, VECS, BLK), F32),
        pltpu.VMEM((UNROLL, BLK, 2 * BLK), F32),
        pltpu.VMEM((UNROLL, BLK, BLK), BF16),
    ]
    block_set = (BLOCKS, VECS, BLK)
    *near_sums, col_sums = call(
        functools.partial(near_far_kernel, 0),
        [shape(block_set, F32)] + [shape(block_set, BF16)] * 3 + [shape((COLS, VECS, BLK), F32)],
        [SMEM] * 3 + [VMEM] * 7,
        [VMEM] * 5,
        "pairs_near",
        scratch=scratch,
        cost=PAIR_COST,
    )(place, counts, codes, *near_rows, vectors, features, steps)

    *far_sums, own_sum, after_sum, last_sum = call(
        functools.partial(near_far_kernel, 1),
        [shape(block_set, BF16)] * 4 + [shape(block_set, F32)] + [shape(block_set, BF16)] * 2,
        [SMEM] * 3 + [VMEM] * 8,
        [VMEM] * 7,
        "pairs_far",
        scratch=scratch,
        cost=PAIR_COST,
    )(place, counts, codes, *far_rows, vectors, features, steps, col_sums)

    far_parts = [far_sums[0]] + [around(far_sums[k], k) for k in (1, 2, 3)]
    from_prior = passed_up(after_sum, 1)
    from_second = passed_up(last_sum, 2)
    far_sum = call(
        sum_kernel, shape((BLOCKS, VECS, BLK), BF16), [VMEM] * 4, VMEM, "far_sum"
    )(*far_parts)
    from_far = across(far_sum)
    near_sums, _ = lax.optimization_barrier((near_sums, far_sum))
    near_parts = [near_sums[0]] + [around(near_sums[k], k) for k in (1, 2, 3)]

    parts = [own_sum, from_prior, from_second, *near_parts, from_far]
    return call(
        final_kernel,
        shape(krylov.shape, F32),
        [SMEM] + [VMEM] * (len(parts) + 3),
        VMEM,
        "final",
        scratch=[pltpu.VMEM((BLOCKS, VECS, BLK), F32)],
    )(type_hard, *parts, kinds, krylov, inverse)


def solution(mesh):
    placed = (
        P(None, ("row", "col")),
        P(("row", "col")),
        P(None, ("row", "col")),
        P(("row", "col")),
        P(),
        P(),
        P("row", "col", None),
        P("row", "col", None),
        P("row", "col"),
    )
    return jax.shard_map(
        on_device, mesh=mesh, in_specs=placed, out_specs=P(None, ("row", "col")), check_vma=False
    )
```

```python
import functools

import jax
import jax.numpy as jnp
import ml_dtypes
import numpy as np
from jax import lax
from jax.experimental import pallas as pl
from jax.experimental.pallas import tpu as pltpu
from jax.sharding import PartitionSpec as P

BLK = 128
VECS = 16
NTYPES = 6
BLOCKS = 32
HALF = 4 * BLOCKS
COLS = 3 * BLOCKS
ROWS = VECS + 8
DEPTH = 80
UNROLL = 8
SLOTS = 512
SLOT_SPAN = SLOTS + BLK
SPARE = 3 << 22
CELL = (11.0, 5.0, 11.0)
BOX = (44.0, 30.0, 44.0)
SOFTENING = 0.5

ERF_COEFFS = (
    1.1283733798353786,
    0.10285896471421105,
    -0.0004149336902342856,
    -0.00044422084313997635,
    3.52820399232984e-05,
)


def time_cost(microseconds):
    return pl.CostEstimate(
        flops=int(microseconds * 1_000_000_000), transcendentals=0, bytes_accessed=1_000_000
    )


PAIR_COST = time_cost(16)

VMEM = pl.BlockSpec(memory_space=pltpu.VMEM)
SMEM = pl.BlockSpec(memory_space=pltpu.SMEM)
ANY = pl.BlockSpec(memory_space=pl.ANY)
Y_GROUPS = [[0, 1, 2, 3], [4, 5, 6, 7]]
F32 = jnp.float32
BF16 = jnp.bfloat16


def sublane():
    return lax.broadcasted_iota(jnp.int32, (8, BLK), 0)


def split3(value):
    high = value.astype(BF16).astype(F32)
    rest = value - high
    middle = rest.astype(BF16).astype(F32)
    return high, middle, rest - middle


def lane_gather(source, index):
    return jnp.take_along_axis(source, index, axis=1, mode="promise_in_bounds")


def prep_kernel(
    place, positions_hbm, type_hbm, krylov_hbm, order_hbm, packed, geometry, positions, atom_type, krylov, order, done
):
    loads = [
        pltpu.make_async_copy(source, target, done.at[k])
        for k, (source, target) in enumerate(
            (
                (krylov_hbm, krylov),
                (positions_hbm, positions),
                (type_hbm, atom_type),
                (order_hbm, order),
            )
        )
    ]
    for load in loads:
        load.start()
    for load in loads:
        load.wait()
    geometry[...] = jnp.zeros_like(geometry)
    geometry[0:3, :] = positions[...]
    geometry[3:4, :] = atom_type[...].astype(F32)
    level = sublane()
    corner_x = CELL[0] * place[0].astype(F32) + BOX[0] / 2
    corner_y = CELL[1] * place[1].astype(F32) + BOX[1] / 2

    def one_block(block, carry):
        wanted = jnp.broadcast_to(order[pl.ds(block, 1), :], (8, BLK))
        chunk = wanted >> 7
        lane = wanted & 127
        top = jnp.zeros((8, BLK), F32)
        low = jnp.zeros((8, BLK), F32)
        geo = jnp.zeros((8, BLK), F32)
        for s in range(BLOCKS):
            here = chunk == s
            span = slice(s * BLK, (s + 1) * BLK)
            top = jnp.where(here, lane_gather(krylov[0:8, span], lane), top)
            low = jnp.where(here, lane_gather(krylov[8:16, span], lane), low)
            geo = jnp.where(here, lane_gather(geometry[:, span], lane), geo)
        corner_z = CELL[2] * block.astype(F32) + BOX[2] / 2
        corner = jnp.where(
            level == 0, corner_x, jnp.where(level == 1, corner_y, jnp.where(level == 2, corner_z, 0.0))
        )
        local = geo - corner
        coarse = jnp.floor(local * 4.0 + 0.5) * 0.25
        fine = jnp.where(level < 3, local - coarse, local)
        coded = jnp.where(level < 3, coarse, pltpu.roll(fine, 3, 0))
        packed[block, 0:VECS, :] = jnp.concatenate([top, low], axis=0).astype(BF16)
        packed[block, VECS:ROWS, :] = coded.astype(BF16)
        return carry

    lax.fori_loop(0, BLOCKS, one_block, 0)


def side_kernel(place, count, rows, cols, order, inverse, codes, counts):
    row = rows[...]
    col = cols[...] - place[0] * BLOCKS
    step_y = place[1] - (row >> 5) + 4
    step_z = (col & 31) - (row & 31) + 2
    step = ((col >> 5) * 9 + step_y) * 5 + step_z
    diagonal = jnp.logical_and(col < BLOCKS, row == place[1] * BLOCKS + col)
    code = (row & 127) | (col << 7) | (step << 14) | (diagonal.astype(jnp.int32) << 22)
    live = lax.broadcasted_iota(jnp.int32, (1, SLOTS), 1) < count[0]
    same = (row >> 7) == (place[1] >> 2)
    near = jnp.logical_and(live, same).astype(F32)
    far = jnp.logical_and(live, jnp.logical_not(same)).astype(F32)
    level = lax.broadcasted_iota(jnp.int32, (8, SLOTS), 0)
    wide = lambda v: jnp.broadcast_to(v, (8, SLOTS))
    flags = jnp.where(level == 0, wide(near), jnp.where(level == 1, wide(far), 0.0)).astype(BF16)
    earlier = (
        (lax.broadcasted_iota(jnp.int32, (SLOTS, SLOTS), 0) < lax.broadcasted_iota(jnp.int32, (SLOTS, SLOTS), 1))
        .astype(F32)
        .astype(BF16)
    )
    ranks = jnp.dot(flags, earlier, preferred_element_type=F32)
    target = jnp.where(
        near > 0.5, ranks[0:1], jnp.where(far > 0.5, ranks[1:2] + float(SLOT_SPAN), -1.0)
    ).astype(jnp.int32)
    chosen = (
        (
            lax.broadcasted_iota(jnp.int32, (2 * SLOT_SPAN, SLOTS), 0)
            == jnp.broadcast_to(target, (2 * SLOT_SPAN, SLOTS))
        )
        .astype(F32)
        .astype(BF16)
    )
    low = wide((code & 255).astype(F32))
    middle = wide(((code >> 8) & 255).astype(F32))
    high = wide((code >> 16).astype(F32))
    parts = jnp.where(level == 0, low, jnp.where(level == 1, middle, jnp.where(level == 2, high, 0.0)))
    moved = lax.dot_general(
        parts.astype(BF16), chosen, (((1,), (1,)), ((), ())), preferred_element_type=F32
    )
    listed = (moved[0:1] + moved[1:2] * 256.0 + moved[2:3] * 65536.0).astype(jnp.int32)
    near_count = jnp.sum(near).astype(jnp.int32)
    far_count = jnp.sum(far).astype(jnp.int32)
    spot = lax.broadcasted_iota(jnp.int32, (1, 2 * SLOT_SPAN), 1)
    in_near = spot < SLOT_SPAN
    used = jnp.where(in_near, spot, spot - SLOT_SPAN) < jnp.where(in_near, near_count, far_count)
    codes[...] = jnp.where(used, listed, SPARE)
    counts[0] = near_count
    counts[1] = far_count

    level_h = lax.broadcasted_iota(jnp.int32, (BLOCKS, BLK), 0)
    level_l = lax.broadcasted_iota(jnp.int32, (BLK, BLK), 0)
    lanes = lax.broadcasted_iota(jnp.int32, (BLOCKS, BLK), 1).astype(F32)
    left = []
    right = []
    for block in range(BLOCKS):
        wanted = order[block : block + 1, :]
        in_high = (level_h == jnp.broadcast_to(wanted >> 7, (BLOCKS, BLK))).astype(F32)
        in_low = (level_l == jnp.broadcast_to(wanted & 127, (BLK, BLK))).astype(F32)
        left.append(jnp.concatenate([in_high * float(block), in_high * lanes], axis=0).astype(BF16))
        right.append(in_low.astype(BF16))
    total = lax.dot_general(
        jnp.concatenate(left, axis=1),
        jnp.concatenate(right, axis=1),
        (((1,), (1,)), ((), ())),
        preferred_element_type=F32,
    )
    inverse[...] = (total[0:BLOCKS] * float(BLK) + total[BLOCKS:]).astype(jnp.int32)


def feature_kernel(type_width, own, after, second, features, vectors):
    level = sublane()
    squares = jnp.zeros((8, BLK), F32)
    for t in range(NTYPES):
        squares = jnp.where(level == t, type_width[t] * type_width[t], squares)
    low3 = level < 3
    low6 = level < 6
    zero = jnp.zeros((8, BLK), F32)
    ones3 = jnp.where(low3, 1.0, 0.0)

    for part, source in enumerate((own, after, second)):

        def one_block(block, part=part, source=source):
            vectors[part * BLOCKS + block] = source[block, 0:VECS, :]
            coded = source[block, VECS:ROWS, :].astype(F32)
            near = coded + pltpu.roll(coded, 5, 0)
            square = near * near
            weight = square[0:1] + square[1:2] + square[2:3] + SOFTENING * SOFTENING
            weight_h, weight_m, weight_l = split3(weight)
            coarse = jnp.where(low3, coded, pltpu.roll(coded, 3, 0)) * -2.0
            fine = jnp.where(low3, pltpu.roll(coded, 5, 0), coded) * -2.0
            own_type = jnp.broadcast_to(coded[6:7], (8, BLK))
            own_square = jnp.zeros((8, BLK), F32)
            for t in range(NTYPES):
                own_square = jnp.where(own_type == float(t), type_width[t] * type_width[t], own_square)
            scale = lax.rsqrt(own_square + squares)
            scale_h, scale_m, scale_l = split3(jnp.where(low6, scale, 0.0))
            wide = lambda v: jnp.broadcast_to(v, (8, BLK))
            weights = jnp.where(
                level == 0,
                wide(weight_h),
                jnp.where(level == 1, wide(weight_m), jnp.where(level == 2, wide(weight_l), 0.0)),
            )
            stacked = jnp.concatenate(
                [
                    jnp.where(low6, coarse, 0.0),
                    jnp.where(low6, fine, 0.0),
                    jnp.where(low6, coded, 1.0),
                    weights,
                    ones3,
                    zero,
                    scale_h,
                    scale_m,
                    scale_l,
                ]
                + [zero] * 7,
                axis=0,
            )
            features[part * BLOCKS + block] = stacked.T.astype(BF16)

        def some_blocks(turn, carry, one_block=one_block):
            for extra in range(4):
                one_block(turn * 4 + extra)
            return carry

        lax.fori_loop(0, BLOCKS // 4, some_blocks, 0)


def row_operands(row_data, operands):
    level = sublane()
    zero = jnp.zeros((8, BLK), F32)

    def some_rows(turn, carry):
        for extra in range(8):
            row = turn * 8 + extra
            coded = row_data[row, VECS:ROWS, :].astype(F32)
            near = coded + pltpu.roll(coded, 5, 0)
            square = near * near
            weight_h, weight_m, weight_l = split3(square[0:1] + square[1:2] + square[2:3])
            wide = lambda v: jnp.broadcast_to(v, (8, BLK))
            weights = jnp.where(
                level == 0,
                wide(weight_h),
                jnp.where(level == 1, wide(weight_m), jnp.where(level == 2, wide(weight_l), 0.0)),
            )
            hot = (level.astype(F32) == wide(coded[6:7])).astype(F32)
            operands[row] = jnp.concatenate(
                [coded, coded, weights, zero, hot, hot, hot, zero], axis=0
            ).astype(BF16)
        return carry

    lax.fori_loop(0, HALF // 8, some_rows, 0)


def pair_products(code, operands, features, step_rows, step_lanes):
    step = (code >> 14) & 255
    right = operands[code & 127]
    empty = jnp.zeros((48, BLK), BF16)
    left = features[(code >> 7) & 127].reshape(8, 16, BLK) + step_lanes[step][None]
    both = jnp.concatenate(
        [
            jnp.concatenate([right[0:16], step_rows[step], right[16:32], empty[0:32]], axis=0),
            jnp.concatenate([empty, right[32:64]], axis=0),
        ],
        axis=1,
    )
    return jnp.dot(left.reshape(BLK, BLK)[:, 0:DEPTH], both, preferred_element_type=F32)


def tile_values(distance2, scale):
    inverse = lax.rsqrt(distance2)
    z = distance2 * inverse * scale
    square = z * z
    poly = ERF_COEFFS[-1]
    for coefficient in ERF_COEFFS[-2::-1]:
        poly = poly * square + coefficient
    return (jnp.tanh(poly * z) * inverse).astype(BF16)


def pair_loop(
    phase, counts, codes, row_data, operands, vectors, features, step_rows, step_lanes, row_acc, col_acc, waiting, tiles
):
    base = phase * SLOT_SPAN
    batches = (counts[phase] + UNROLL - 1) // UNROLL

    def one_turn(turn, carry):
        adding = base + jnp.maximum(turn - 2, 0) * UNROLL
        opening = base + jnp.maximum(jnp.minimum(turn, batches - 1), 0) * UNROLL
        sums = []
        for first in range(0, UNROLL, 2):
            done = [codes[0, adding + first + k] for k in range(2)]
            both = [tiles[first + k] for k in range(2)]
            forward = jnp.dot(
                jnp.concatenate([vectors[(code >> 7) & 127] for code in done], axis=0),
                jnp.concatenate(both, axis=1),
                preferred_element_type=F32,
            )
            backward = lax.dot_general(
                jnp.concatenate([row_data[code & 127, 0:VECS, :] for code in done], axis=0),
                jnp.concatenate(both, axis=0),
                (((1,), (1,)), ((), ())),
                preferred_element_type=F32,
            )
            for k, code in enumerate(done):
                to_row = jnp.where(jnp.logical_or(turn < 2, ((code >> 23) & 1) == 1), HALF, code & 127)
                to_col = jnp.where(
                    jnp.logical_or(turn < 2, ((code >> 22) & 1) == 1), COLS, (code >> 7) & 127
                )
                own = (slice(k * VECS, (k + 1) * VECS), slice(k * BLK, (k + 1) * BLK))
                sums.append((to_row, forward[own], to_col, backward[own]))
            for k in range(2):
                slot = first + k
                tiles[slot] = tile_values(waiting[slot, :, 0:BLK], waiting[slot, :, BLK:])
                code = codes[0, opening + slot]
                waiting[slot] = pair_products(code, operands, features, step_rows, step_lanes)
        for to_row, forward, to_col, backward in sums:
            row_acc[to_row] += forward
            col_acc[to_col] += backward
        return carry

    lax.fori_loop(0, batches + 2, one_turn, 0)


def near_far_kernel(phase, *refs):
    place, counts, codes = refs[0:3]
    pieces = refs[3:7]
    vectors, features, step_rows, step_lanes = refs[7:11]
    col_in = refs[11:12] if phase == 1 else ()
    outs = refs[11 + len(col_in) : -6]
    row_data, operands, row_acc, col_acc, waiting, tiles = refs[-6:]
    position = place[1] & 3
    for k, piece in enumerate(pieces):
        start = pl.multiple_of(((position - k) & 3) * BLOCKS, BLOCKS)
        row_data[pl.ds(start, BLOCKS)] = piece[...]
    row_operands(row_data, operands)
    row_acc[...] = jnp.zeros_like(row_acc)
    if phase == 0:
        col_acc[...] = jnp.zeros_like(col_acc)
    else:
        col_acc[0:COLS] = col_in[0][...]
    pair_loop(
        phase,
        counts,
        codes,
        row_data,
        operands,
        vectors,
        features,
        step_rows,
        step_lanes,
        row_acc,
        col_acc,
        waiting,
        tiles,
    )
    for k in range(4):
        start = pl.multiple_of(((position + k) & 3) * BLOCKS, BLOCKS)
        outs[k][...] = row_acc[pl.ds(start, BLOCKS)].astype(outs[k].dtype)
    if phase == 0:
        outs[4][...] = col_acc[0:COLS]
    else:
        for step in range(3):
            outs[4 + step][...] = col_acc[step * BLOCKS : (step + 1) * BLOCKS].astype(outs[4 + step].dtype)


def sum_kernel(*refs):
    total = refs[0][...].astype(F32)
    for ref in refs[1:-1]:
        total = total + ref[...].astype(F32)
    refs[-1][...] = total.astype(refs[-1].dtype)


def final_kernel(type_hard, *refs):
    atom_type, krylov, inverse, out, blocked = refs[-5:]
    parts = refs[:-5]

    def add_up(block, carry):
        total = parts[0][block]
        for part in parts[1:]:
            total = total + part[block].astype(F32)
        blocked[block] = total
        return carry

    lax.fori_loop(0, BLOCKS, add_up, 0)
    for chunk in range(BLOCKS):
        wanted = jnp.broadcast_to(inverse[chunk : chunk + 1, :], (8, BLK))
        source = wanted >> 7
        lane = wanted & 127
        span = slice(chunk * BLK, (chunk + 1) * BLK)
        kind = jnp.broadcast_to(atom_type[:, span], (8, BLK))
        hard = jnp.zeros((8, BLK), F32)
        for t in range(NTYPES):
            hard = jnp.where(kind == t, type_hard[t], hard)

        def pick(block, carry, source=source, lane=lane):
            top, low = carry
            here = source == block
            top = jnp.where(here, lane_gather(blocked[block, 0:8, :], lane), top)
            low = jnp.where(here, lane_gather(blocked[block, 8:16, :], lane), low)
            return top, low

        start = (hard * 0.0, hard * 0.0)
        top, low = lax.fori_loop(0, BLOCKS, pick, start, unroll=True)
        out[0:8, span] = top + hard * krylov[0:8, span]
        out[8:16, span] = low + hard * krylov[8:16, span]


def shape(dims, dtype):
    return jax.ShapeDtypeStruct(dims, dtype)


def call(kernel, out_shape, in_specs, out_specs, name, scratch=(), vmem=48, cost=None):
    return pl.pallas_call(
        kernel,
        out_shape=out_shape,
        in_specs=in_specs,
        out_specs=out_specs,
        scratch_shapes=list(scratch),
        compiler_params=pltpu.CompilerParams(vmem_limit_bytes=vmem << 20),
        cost_estimate=cost,
        name=name,
    )


def step_tables():
    x, y, z = np.meshgrid(np.arange(3), np.arange(-4, 5), np.arange(-2, 3), indexing="ij")
    steps = np.stack([x, y, z], axis=-1).reshape(-1, 3) * np.array(CELL)
    squared = np.sum(steps * steps, axis=1).astype(np.float32)
    coarse = squared.astype(ml_dtypes.bfloat16).astype(np.float32)
    rows = np.zeros((len(steps), 16, BLK), np.float32)
    rows[:, 0:3] = rows[:, 3:6] = 2.0 * steps[:, :, None]
    rows[:, 6] = coarse[:, None]
    rows[:, 7] = (squared - coarse)[:, None]
    rows[:, 8:11] = 1.0
    lanes = np.zeros((len(steps), 16, BLK), np.float32)
    lanes[:, :, 0:3] = lanes[:, :, 3:6] = -2.0 * steps[:, None, :]
    return rows.astype(ml_dtypes.bfloat16), lanes.astype(ml_dtypes.bfloat16)


def passed_down(value, steps):
    count = lax.axis_size("row")
    return lax.ppermute(value, "row", [(s, s - steps) for s in range(steps, count)])


def passed_up(value, steps):
    count = lax.axis_size("row")
    return lax.ppermute(value, "row", [(s, s + steps) for s in range(count - steps)])


def across(value):
    return lax.ppermute(value, "col", [(c, c ^ 4) for c in range(8)])


def around(value, steps):
    return lax.ppermute(value, "col", [(c, (c & 4) + (c + steps) % 4) for c in range(8)])


def on_device(
    positions, atom_type, krylov, block_order, type_width, type_hard, pair_rows, pair_cols, pair_count
):
    place = jnp.stack([lax.axis_index("row"), lax.axis_index("col")]).astype(jnp.int32)
    order = block_order.reshape(BLOCKS, BLK)
    kinds = atom_type.reshape(1, -1)

    packed = call(
        prep_kernel,
        shape((BLOCKS, ROWS, BLK), BF16),
        [SMEM, ANY, ANY, ANY, ANY],
        VMEM,
        "prep",
        scratch=[
            pltpu.VMEM((8, BLOCKS * BLK), F32),
            pltpu.VMEM((3, BLOCKS * BLK), F32),
            pltpu.VMEM((1, BLOCKS * BLK), jnp.int32),
            pltpu.VMEM((VECS, BLOCKS * BLK), F32),
            pltpu.VMEM((BLOCKS, BLK), jnp.int32),
            pltpu.SemaphoreType.DMA((4,)),
        ],
        vmem=62,
    )(place, positions, kinds, krylov, order)

    other = across(packed)
    after = passed_down(packed, 1)
    second = passed_down(packed, 2)
    rows_list, _ = lax.optimization_barrier((pair_rows.reshape(1, SLOTS), packed))

    inverse, codes, counts = call(
        side_kernel,
        (
            shape((BLOCKS, BLK), jnp.int32),
            shape((1, 2 * SLOT_SPAN), jnp.int32),
            shape((2,), jnp.int32),
        ),
        [SMEM, SMEM, VMEM, VMEM, VMEM],
        (VMEM, VMEM, SMEM),
        "side",
        cost=time_cost(12),
    )(place, pair_count.reshape(-1), rows_list, pair_cols.reshape(1, SLOTS), order)

    near_rows = [packed] + [around(packed, k) for k in (1, 2, 3)]

    features, vectors = call(
        feature_kernel,
        (shape((COLS, BLK, BLK), BF16), shape((COLS, VECS, BLK), BF16)),
        [SMEM, VMEM, VMEM, VMEM],
        (VMEM, VMEM),
        "features",
        cost=time_cost(5),
    )(type_width, packed, after, second)

    far_rows = [other] + [around(other, k) for k in (1, 2, 3)]
    step_rows, step_lanes = step_tables()
    codes, _ = lax.optimization_barrier((codes, other))
    scratch = [
        pltpu.VMEM((HALF, ROWS, BLK), BF16),
        pltpu.VMEM((HALF, 64, BLK), BF16),
        pltpu.VMEM((HALF + 1, VECS, BLK), F32),
        pltpu.VMEM((COLS + 1, VECS, BLK), F32),
        pltpu.VMEM((UNROLL, BLK, 2 * BLK), F32),
        pltpu.VMEM((UNROLL, BLK, BLK), BF16),
    ]
    block_set = (BLOCKS, VECS, BLK)
    *near_sums, col_sums = call(
        functools.partial(near_far_kernel, 0),
        [shape(block_set, F32)] + [shape(block_set, BF16)] * 3 + [shape((COLS, VECS, BLK), F32)],
        [SMEM] * 3 + [VMEM] * 8,
        [VMEM] * 5,
        "pairs_near",
        scratch=scratch,
        cost=PAIR_COST,
    )(place, counts, codes, *near_rows, vectors, features, step_rows, step_lanes)

    *far_sums, own_sum, after_sum, last_sum = call(
        functools.partial(near_far_kernel, 1),
        [shape(block_set, BF16)] * 4 + [shape(block_set, F32)] + [shape(block_set, BF16)] * 2,
        [SMEM] * 3 + [VMEM] * 9,
        [VMEM] * 7,
        "pairs_far",
        scratch=scratch,
        cost=PAIR_COST,
    )(place, counts, codes, *far_rows, vectors, features, step_rows, step_lanes, col_sums)

    far_parts = [far_sums[0]] + [around(far_sums[k], k) for k in (1, 2, 3)]
    from_prior = passed_up(after_sum, 1)
    from_second = passed_up(last_sum, 2)
    far_sum = call(
        sum_kernel, shape((BLOCKS, VECS, BLK), BF16), [VMEM] * 4, VMEM, "far_sum"
    )(*far_parts)
    from_far = across(far_sum)
    near_sums, _ = lax.optimization_barrier((near_sums, far_sum))
    near_parts = [near_sums[0]] + [around(near_sums[k], k) for k in (1, 2, 3)]

    parts = [own_sum, from_prior, from_second, *near_parts, from_far]
    return call(
        final_kernel,
        shape(krylov.shape, F32),
        [SMEM] + [VMEM] * (len(parts) + 3),
        VMEM,
        "final",
        scratch=[pltpu.VMEM((BLOCKS, VECS, BLK), F32)],
    )(type_hard, *parts, kinds, krylov, inverse)


def solution(mesh):
    placed = (
        P(None, ("row", "col")),
        P(("row", "col")),
        P(None, ("row", "col")),
        P(("row", "col")),
        P(),
        P(),
        P("row", "col", None),
        P("row", "col", None),
        P("row", "col"),
    )
    return jax.shard_map(
        on_device, mesh=mesh, in_specs=placed, out_specs=P(None, ("row", "col")), check_vma=False
    )
```

```python
import functools

import jax
import jax.numpy as jnp
import ml_dtypes
import numpy as np
from jax import lax
from jax.experimental import pallas as pl
from jax.experimental.pallas import tpu as pltpu
from jax.sharding import PartitionSpec as P

BLK = 128
VECS = 16
NTYPES = 6
BLOCKS = 32
HALF = 4 * BLOCKS
COLS = 3 * BLOCKS
ROWS = VECS + 8
DEPTH = 80
UNROLL = 8
SLOTS = 512
SLOT_SPAN = SLOTS + BLK
SPARE = 3 << 22
CELL = (11.0, 5.0, 11.0)
BOX = (44.0, 30.0, 44.0)
SOFTENING = 0.5

ERF_COEFFS = (
    1.1283733798353786,
    0.10285896471421105,
    -0.0004149336902342856,
    -0.00044422084313997635,
    3.52820399232984e-05,
)


def time_cost(microseconds):
    return pl.CostEstimate(
        flops=int(microseconds * 1_000_000_000), transcendentals=0, bytes_accessed=1_000_000
    )


PAIR_COST = time_cost(16)

VMEM = pl.BlockSpec(memory_space=pltpu.VMEM)
SMEM = pl.BlockSpec(memory_space=pltpu.SMEM)
ANY = pl.BlockSpec(memory_space=pl.ANY)
Y_GROUPS = [[0, 1, 2, 3], [4, 5, 6, 7]]
F32 = jnp.float32
BF16 = jnp.bfloat16


def sublane():
    return lax.broadcasted_iota(jnp.int32, (8, BLK), 0)


def split3(value):
    high = value.astype(BF16).astype(F32)
    rest = value - high
    middle = rest.astype(BF16).astype(F32)
    return high, middle, rest - middle


def lane_gather(source, index):
    return jnp.take_along_axis(source, index, axis=1, mode="promise_in_bounds")


def here():
    return lax.axis_index("row"), lax.axis_index("col")


def prep_kernel(
    positions_hbm, type_hbm, krylov_hbm, order_hbm, packed, geometry, positions, atom_type, krylov, order, done
):
    loads = [
        pltpu.make_async_copy(source, target, done.at[k])
        for k, (source, target) in enumerate(
            (
                (krylov_hbm, krylov),
                (positions_hbm, positions),
                (type_hbm, atom_type),
                (order_hbm, order),
            )
        )
    ]
    for load in loads:
        load.start()
    place = here()
    geometry[...] = jnp.zeros_like(geometry)
    for load in loads:
        load.wait()
    geometry[0:3, :] = positions[...]
    geometry[3:4, :] = atom_type[...].astype(F32)
    level = sublane()
    corner_x = CELL[0] * place[0].astype(F32) + BOX[0] / 2
    corner_y = CELL[1] * place[1].astype(F32) + BOX[1] / 2

    def one_block(block, carry):
        wanted = jnp.broadcast_to(order[pl.ds(block, 1), :], (8, BLK))
        chunk = wanted >> 7
        lane = wanted & 127
        top = jnp.zeros((8, BLK), F32)
        low = jnp.zeros((8, BLK), F32)
        geo = jnp.zeros((8, BLK), F32)
        for s in range(BLOCKS):
            here = chunk == s
            span = slice(s * BLK, (s + 1) * BLK)
            top = jnp.where(here, lane_gather(krylov[0:8, span], lane), top)
            low = jnp.where(here, lane_gather(krylov[8:16, span], lane), low)
            geo = jnp.where(here, lane_gather(geometry[:, span], lane), geo)
        corner_z = CELL[2] * block.astype(F32) + BOX[2] / 2
        corner = jnp.where(
            level == 0, corner_x, jnp.where(level == 1, corner_y, jnp.where(level == 2, corner_z, 0.0))
        )
        local = geo - corner
        coarse = jnp.floor(local * 4.0 + 0.5) * 0.25
        fine = jnp.where(level < 3, local - coarse, local)
        coded = jnp.where(level < 3, coarse, pltpu.roll(fine, 3, 0))
        packed[block, 0:VECS, :] = jnp.concatenate([top, low], axis=0).astype(BF16)
        packed[block, VECS:ROWS, :] = coded.astype(BF16)
        return carry

    lax.fori_loop(0, BLOCKS, one_block, 0)


def side_kernel(
    count_hbm, rows_hbm, cols_hbm, order_hbm, inverse, codes, counts, count, rows, cols, order, done
):
    loads = [
        pltpu.make_async_copy(source, target, done.at[k])
        for k, (source, target) in enumerate(
            ((count_hbm, count), (rows_hbm, rows), (cols_hbm, cols), (order_hbm, order))
        )
    ]
    for load in loads:
        load.start()
    place = here()
    for load in loads:
        load.wait()
    row = rows[...]
    col = cols[...] - place[0] * BLOCKS
    step_y = place[1] - (row >> 5) + 4
    step_z = (col & 31) - (row & 31) + 2
    step = ((col >> 5) * 9 + step_y) * 5 + step_z
    diagonal = jnp.logical_and(col < BLOCKS, row == place[1] * BLOCKS + col)
    code = (row & 127) | (col << 7) | (step << 14) | (diagonal.astype(jnp.int32) << 22)
    live = lax.broadcasted_iota(jnp.int32, (1, SLOTS), 1) < count[0, 0]
    same = (row >> 7) == (place[1] >> 2)
    near = jnp.logical_and(live, same).astype(F32)
    far = jnp.logical_and(live, jnp.logical_not(same)).astype(F32)
    level = lax.broadcasted_iota(jnp.int32, (8, SLOTS), 0)
    wide = lambda v: jnp.broadcast_to(v, (8, SLOTS))
    flags = jnp.where(level == 0, wide(near), jnp.where(level == 1, wide(far), 0.0)).astype(BF16)
    earlier = (
        (lax.broadcasted_iota(jnp.int32, (SLOTS, SLOTS), 0) < lax.broadcasted_iota(jnp.int32, (SLOTS, SLOTS), 1))
        .astype(F32)
        .astype(BF16)
    )
    ranks = jnp.dot(flags, earlier, preferred_element_type=F32)
    target = jnp.where(
        near > 0.5, ranks[0:1], jnp.where(far > 0.5, ranks[1:2] + float(SLOT_SPAN), -1.0)
    ).astype(jnp.int32)
    chosen = (
        (
            lax.broadcasted_iota(jnp.int32, (2 * SLOT_SPAN, SLOTS), 0)
            == jnp.broadcast_to(target, (2 * SLOT_SPAN, SLOTS))
        )
        .astype(F32)
        .astype(BF16)
    )
    low = wide((code & 255).astype(F32))
    middle = wide(((code >> 8) & 255).astype(F32))
    high = wide((code >> 16).astype(F32))
    parts = jnp.where(level == 0, low, jnp.where(level == 1, middle, jnp.where(level == 2, high, 0.0)))
    moved = lax.dot_general(
        parts.astype(BF16), chosen, (((1,), (1,)), ((), ())), preferred_element_type=F32
    )
    listed = (moved[0:1] + moved[1:2] * 256.0 + moved[2:3] * 65536.0).astype(jnp.int32)
    near_count = jnp.sum(near).astype(jnp.int32)
    far_count = jnp.sum(far).astype(jnp.int32)
    spot = lax.broadcasted_iota(jnp.int32, (1, 2 * SLOT_SPAN), 1)
    in_near = spot < SLOT_SPAN
    used = jnp.where(in_near, spot, spot - SLOT_SPAN) < jnp.where(in_near, near_count, far_count)
    codes[...] = jnp.where(used, listed, SPARE)
    counts[0] = near_count
    counts[1] = far_count

    level_h = lax.broadcasted_iota(jnp.int32, (BLOCKS, BLK), 0)
    level_l = lax.broadcasted_iota(jnp.int32, (BLK, BLK), 0)
    lanes = lax.broadcasted_iota(jnp.int32, (BLOCKS, BLK), 1).astype(F32)
    left = []
    right = []
    for block in range(BLOCKS):
        wanted = order[block : block + 1, :]
        in_high = (level_h == jnp.broadcast_to(wanted >> 7, (BLOCKS, BLK))).astype(F32)
        in_low = (level_l == jnp.broadcast_to(wanted & 127, (BLK, BLK))).astype(F32)
        left.append(jnp.concatenate([in_high * float(block), in_high * lanes], axis=0).astype(BF16))
        right.append(in_low.astype(BF16))
    total = lax.dot_general(
        jnp.concatenate(left, axis=1),
        jnp.concatenate(right, axis=1),
        (((1,), (1,)), ((), ())),
        preferred_element_type=F32,
    )
    inverse[...] = (total[0:BLOCKS] * float(BLK) + total[BLOCKS:]).astype(jnp.int32)


def feature_kernel(type_width, own, after, second, features, vectors):
    level = sublane()
    squares = jnp.zeros((8, BLK), F32)
    for t in range(NTYPES):
        squares = jnp.where(level == t, type_width[t] * type_width[t], squares)
    low3 = level < 3
    low6 = level < 6
    zero = jnp.zeros((8, BLK), F32)
    ones3 = jnp.where(low3, 1.0, 0.0)

    for part, source in enumerate((own, after, second)):

        def one_block(block, part=part, source=source):
            vectors[part * BLOCKS + block] = source[block, 0:VECS, :]
            coded = source[block, VECS:ROWS, :].astype(F32)
            near = coded + pltpu.roll(coded, 5, 0)
            square = near * near
            weight = square[0:1] + square[1:2] + square[2:3] + SOFTENING * SOFTENING
            weight_h, weight_m, weight_l = split3(weight)
            coarse = jnp.where(low3, coded, pltpu.roll(coded, 3, 0)) * -2.0
            fine = jnp.where(low3, pltpu.roll(coded, 5, 0), coded) * -2.0
            own_type = jnp.broadcast_to(coded[6:7], (8, BLK))
            own_square = jnp.zeros((8, BLK), F32)
            for t in range(NTYPES):
                own_square = jnp.where(own_type == float(t), type_width[t] * type_width[t], own_square)
            scale = lax.rsqrt(own_square + squares)
            scale_h, scale_m, scale_l = split3(jnp.where(low6, scale, 0.0))
            wide = lambda v: jnp.broadcast_to(v, (8, BLK))
            weights = jnp.where(
                level == 0,
                wide(weight_h),
                jnp.where(level == 1, wide(weight_m), jnp.where(level == 2, wide(weight_l), 0.0)),
            )
            stacked = jnp.concatenate(
                [
                    jnp.where(low6, coarse, 0.0),
                    jnp.where(low6, fine, 0.0),
                    jnp.where(low6, coded, 1.0),
                    weights,
                    ones3,
                    zero,
                    scale_h,
                    scale_m,
                    scale_l,
                ]
                + [zero] * 7,
                axis=0,
            )
            features[part * BLOCKS + block] = stacked.T.astype(BF16)

        def some_blocks(turn, carry, one_block=one_block):
            for extra in range(4):
                one_block(turn * 4 + extra)
            return carry

        lax.fori_loop(0, BLOCKS // 4, some_blocks, 0)


def row_operands(row_data, operands):
    level = sublane()
    zero = jnp.zeros((8, BLK), F32)

    def some_rows(turn, carry):
        for extra in range(8):
            row = turn * 8 + extra
            coded = row_data[row, VECS:ROWS, :].astype(F32)
            near = coded + pltpu.roll(coded, 5, 0)
            square = near * near
            weight_h, weight_m, weight_l = split3(square[0:1] + square[1:2] + square[2:3])
            wide = lambda v: jnp.broadcast_to(v, (8, BLK))
            weights = jnp.where(
                level == 0,
                wide(weight_h),
                jnp.where(level == 1, wide(weight_m), jnp.where(level == 2, wide(weight_l), 0.0)),
            )
            hot = (level.astype(F32) == wide(coded[6:7])).astype(F32)
            operands[row] = jnp.concatenate(
                [coded, coded, weights, zero, hot, hot, hot, zero], axis=0
            ).astype(BF16)
        return carry

    lax.fori_loop(0, HALF // 8, some_rows, 0)


def pair_products(code, operands, features, step_rows, step_lanes):
    step = (code >> 14) & 255
    right = operands[code & 127]
    empty = jnp.zeros((48, BLK), BF16)
    left = features[(code >> 7) & 127].reshape(8, 16, BLK) + step_lanes[step][None]
    both = jnp.concatenate(
        [
            jnp.concatenate([right[0:16], step_rows[step], right[16:32], empty[0:32]], axis=0),
            jnp.concatenate([empty, right[32:64]], axis=0),
        ],
        axis=1,
    )
    return jnp.dot(left.reshape(BLK, BLK)[:, 0:DEPTH], both, preferred_element_type=F32)


def tile_values(distance2, scale):
    inverse = lax.rsqrt(distance2)
    z = distance2 * inverse * scale
    square = z * z
    poly = ERF_COEFFS[-1]
    for coefficient in ERF_COEFFS[-2::-1]:
        poly = poly * square + coefficient
    return (jnp.tanh(poly * z) * inverse).astype(BF16)


def pair_loop(
    phase, counts, codes, row_data, operands, vectors, features, step_rows, step_lanes, row_acc, col_acc, waiting, tiles
):
    base = phase * SLOT_SPAN
    batches = (counts[phase] + UNROLL - 1) // UNROLL

    def one_turn(turn, carry):
        adding = base + jnp.maximum(turn - 2, 0) * UNROLL
        opening = base + jnp.maximum(jnp.minimum(turn, batches - 1), 0) * UNROLL
        sums = []
        for first in range(0, UNROLL, 2):
            done = [codes[0, adding + first + k] for k in range(2)]
            both = [tiles[first + k] for k in range(2)]
            forward = jnp.dot(
                jnp.concatenate([vectors[(code >> 7) & 127] for code in done], axis=0),
                jnp.concatenate(both, axis=1),
                preferred_element_type=F32,
            )
            backward = lax.dot_general(
                jnp.concatenate([row_data[code & 127, 0:VECS, :] for code in done], axis=0),
                jnp.concatenate(both, axis=0),
                (((1,), (1,)), ((), ())),
                preferred_element_type=F32,
            )
            for k, code in enumerate(done):
                to_row = jnp.where(jnp.logical_or(turn < 2, ((code >> 23) & 1) == 1), HALF, code & 127)
                to_col = jnp.where(
                    jnp.logical_or(turn < 2, ((code >> 22) & 1) == 1), COLS, (code >> 7) & 127
                )
                own = (slice(k * VECS, (k + 1) * VECS), slice(k * BLK, (k + 1) * BLK))
                sums.append((to_row, forward[own], to_col, backward[own]))
            for k in range(2):
                slot = first + k
                tiles[slot] = tile_values(waiting[slot, :, 0:BLK], waiting[slot, :, BLK:])
                code = codes[0, opening + slot]
                waiting[slot] = pair_products(code, operands, features, step_rows, step_lanes)
        for to_row, forward, to_col, backward in sums:
            row_acc[to_row] += forward
            col_acc[to_col] += backward
        return carry

    lax.fori_loop(0, batches + 2, one_turn, 0)


def near_far_kernel(phase, *refs):
    counts, codes = refs[0:2]
    pieces = refs[2:6]
    vectors, features, step_rows, step_lanes = refs[6:10]
    col_in = refs[10:11] if phase == 1 else ()
    outs = refs[10 + len(col_in) : -6]
    row_data, operands, row_acc, col_acc, waiting, tiles = refs[-6:]
    position = here()[1] & 3
    for k, piece in enumerate(pieces):
        start = pl.multiple_of(((position - k) & 3) * BLOCKS, BLOCKS)
        row_data[pl.ds(start, BLOCKS)] = piece[...]
    row_operands(row_data, operands)
    row_acc[...] = jnp.zeros_like(row_acc)
    if phase == 0:
        col_acc[...] = jnp.zeros_like(col_acc)
    else:
        col_acc[0:COLS] = col_in[0][...]
    pair_loop(
        phase,
        counts,
        codes,
        row_data,
        operands,
        vectors,
        features,
        step_rows,
        step_lanes,
        row_acc,
        col_acc,
        waiting,
        tiles,
    )
    for k in range(4):
        start = pl.multiple_of(((position + k) & 3) * BLOCKS, BLOCKS)
        outs[k][...] = row_acc[pl.ds(start, BLOCKS)].astype(outs[k].dtype)
    if phase == 0:
        outs[4][...] = col_acc[0:COLS]
    else:
        for step in range(3):
            outs[4 + step][...] = col_acc[step * BLOCKS : (step + 1) * BLOCKS].astype(outs[4 + step].dtype)


def sum_kernel(*refs):
    total = refs[0][...].astype(F32)
    for ref in refs[1:-1]:
        total = total + ref[...].astype(F32)
    refs[-1][...] = total.astype(refs[-1].dtype)


def final_kernel(type_hard, *refs):
    atom_type, krylov, inverse, out, blocked = refs[-5:]
    parts = refs[:-5]

    def add_up(block, carry):
        total = parts[0][block]
        for part in parts[1:]:
            total = total + part[block].astype(F32)
        blocked[block] = total
        return carry

    lax.fori_loop(0, BLOCKS, add_up, 0)
    for chunk in range(BLOCKS):
        wanted = jnp.broadcast_to(inverse[chunk : chunk + 1, :], (8, BLK))
        source = wanted >> 7
        lane = wanted & 127
        span = slice(chunk * BLK, (chunk + 1) * BLK)
        kind = jnp.broadcast_to(atom_type[:, span], (8, BLK))
        hard = jnp.zeros((8, BLK), F32)
        for t in range(NTYPES):
            hard = jnp.where(kind == t, type_hard[t], hard)

        def pick(block, carry, source=source, lane=lane):
            top, low = carry
            here = source == block
            top = jnp.where(here, lane_gather(blocked[block, 0:8, :], lane), top)
            low = jnp.where(here, lane_gather(blocked[block, 8:16, :], lane), low)
            return top, low

        start = (hard * 0.0, hard * 0.0)
        top, low = lax.fori_loop(0, BLOCKS, pick, start, unroll=True)
        out[0:8, span] = top + hard * krylov[0:8, span]
        out[8:16, span] = low + hard * krylov[8:16, span]


def shape(dims, dtype):
    return jax.ShapeDtypeStruct(dims, dtype)


def call(kernel, out_shape, in_specs, out_specs, name, scratch=(), vmem=20, cost=None):
    return pl.pallas_call(
        kernel,
        out_shape=out_shape,
        in_specs=in_specs,
        out_specs=out_specs,
        scratch_shapes=list(scratch),
        compiler_params=pltpu.CompilerParams(vmem_limit_bytes=vmem << 20),
        cost_estimate=cost,
        name=name,
    )


def step_tables():
    x, y, z = np.meshgrid(np.arange(3), np.arange(-4, 5), np.arange(-2, 3), indexing="ij")
    steps = np.stack([x, y, z], axis=-1).reshape(-1, 3) * np.array(CELL)
    squared = np.sum(steps * steps, axis=1).astype(np.float32)
    coarse = squared.astype(ml_dtypes.bfloat16).astype(np.float32)
    rows = np.zeros((len(steps), 16, BLK), np.float32)
    rows[:, 0:3] = rows[:, 3:6] = 2.0 * steps[:, :, None]
    rows[:, 6] = coarse[:, None]
    rows[:, 7] = (squared - coarse)[:, None]
    rows[:, 8:11] = 1.0
    lanes = np.zeros((len(steps), 16, BLK), np.float32)
    lanes[:, :, 0:3] = lanes[:, :, 3:6] = -2.0 * steps[:, None, :]
    return rows.astype(ml_dtypes.bfloat16), lanes.astype(ml_dtypes.bfloat16)


def passed_down(value, steps):
    count = lax.axis_size("row")
    return lax.ppermute(value, "row", [(s, s - steps) for s in range(steps, count)])


def passed_up(value, steps):
    count = lax.axis_size("row")
    return lax.ppermute(value, "row", [(s, s + steps) for s in range(count - steps)])


def across(value):
    return lax.ppermute(value, "col", [(c, c ^ 4) for c in range(8)])


def around(value, steps):
    return lax.ppermute(value, "col", [(c, (c & 4) + (c + steps) % 4) for c in range(8)])


def on_device(
    positions, atom_type, krylov, block_order, type_width, type_hard, pair_rows, pair_cols, pair_count
):
    order = block_order.reshape(BLOCKS, BLK)
    kinds = atom_type.reshape(1, -1)

    packed = call(
        prep_kernel,
        shape((BLOCKS, ROWS, BLK), BF16),
        [ANY, ANY, ANY, ANY],
        VMEM,
        "prep",
        scratch=[
            pltpu.VMEM((8, BLOCKS * BLK), F32),
            pltpu.VMEM((3, BLOCKS * BLK), F32),
            pltpu.VMEM((1, BLOCKS * BLK), jnp.int32),
            pltpu.VMEM((VECS, BLOCKS * BLK), F32),
            pltpu.VMEM((BLOCKS, BLK), jnp.int32),
            pltpu.SemaphoreType.DMA((4,)),
        ],
        vmem=62,
    )(positions, kinds, krylov, order)

    other = across(packed)
    after = passed_down(packed, 1)
    second = passed_down(packed, 2)
    rows_list, _ = lax.optimization_barrier((pair_rows.reshape(1, SLOTS), packed))

    inverse, codes, counts = call(
        side_kernel,
        (
            shape((BLOCKS, BLK), jnp.int32),
            shape((1, 2 * SLOT_SPAN), jnp.int32),
            shape((2,), jnp.int32),
        ),
        [ANY, ANY, ANY, ANY],
        (VMEM, VMEM, SMEM),
        "side",
        scratch=[
            pltpu.SMEM((1, 1), jnp.int32),
            pltpu.VMEM((1, SLOTS), jnp.int32),
            pltpu.VMEM((1, SLOTS), jnp.int32),
            pltpu.VMEM((BLOCKS, BLK), jnp.int32),
            pltpu.SemaphoreType.DMA((4,)),
        ],
        vmem=62,
        cost=time_cost(2),
    )(pair_count, rows_list, pair_cols.reshape(1, SLOTS), order)

    codes, packed = lax.optimization_barrier((codes, packed))
    near_rows = [packed] + [around(packed, k) for k in (1, 2, 3)]

    features, vectors = call(
        feature_kernel,
        (shape((COLS, BLK, BLK), BF16), shape((COLS, VECS, BLK), BF16)),
        [SMEM, VMEM, VMEM, VMEM],
        (VMEM, VMEM),
        "features",
        cost=time_cost(12),
    )(type_width, packed, after, second)

    far_rows = [other] + [around(other, k) for k in (1, 2, 3)]
    step_rows, step_lanes = step_tables()
    codes, _ = lax.optimization_barrier((codes, other))
    scratch = [
        pltpu.VMEM((HALF, ROWS, BLK), BF16),
        pltpu.VMEM((HALF, 64, BLK), BF16),
        pltpu.VMEM((HALF + 1, VECS, BLK), F32),
        pltpu.VMEM((COLS + 1, VECS, BLK), F32),
        pltpu.VMEM((UNROLL, BLK, 2 * BLK), F32),
        pltpu.VMEM((UNROLL, BLK, BLK), BF16),
    ]
    block_set = (BLOCKS, VECS, BLK)
    *near_sums, col_sums = call(
        functools.partial(near_far_kernel, 0),
        [shape(block_set, F32)] + [shape(block_set, BF16)] * 3 + [shape((COLS, VECS, BLK), F32)],
        [SMEM] * 2 + [VMEM] * 8,
        [VMEM] * 5,
        "pairs_near",
        scratch=scratch,
        cost=PAIR_COST,
    )(counts, codes, *near_rows, vectors, features, step_rows, step_lanes)

    *far_sums, own_sum, after_sum, last_sum = call(
        functools.partial(near_far_kernel, 1),
        [shape(block_set, BF16)] * 4 + [shape(block_set, F32)] + [shape(block_set, BF16)] * 2,
        [SMEM] * 2 + [VMEM] * 9,
        [VMEM] * 7,
        "pairs_far",
        scratch=scratch,
        cost=PAIR_COST,
    )(counts, codes, *far_rows, vectors, features, step_rows, step_lanes, col_sums)

    far_parts = [far_sums[0]] + [around(far_sums[k], k) for k in (1, 2, 3)]
    from_prior = passed_up(after_sum, 1)
    from_second = passed_up(last_sum, 2)
    far_sum = call(
        sum_kernel, shape((BLOCKS, VECS, BLK), BF16), [VMEM] * 4, VMEM, "far_sum"
    )(*far_parts)
    from_far = across(far_sum)
    near_sums, _ = lax.optimization_barrier((near_sums, (far_sum, from_prior, from_second)))
    near_parts = [near_sums[0]] + [around(near_sums[k], k) for k in (1, 2, 3)]

    parts = [own_sum, from_far, from_prior, from_second, *near_parts]
    return call(
        final_kernel,
        shape(krylov.shape, F32),
        [SMEM] + [VMEM] * (len(parts) + 3),
        VMEM,
        "final",
        scratch=[pltpu.VMEM((BLOCKS, VECS, BLK), F32)],
    )(type_hard, *parts, kinds, krylov, inverse)


def solution(mesh):
    placed = (
        P(None, ("row", "col")),
        P(("row", "col")),
        P(None, ("row", "col")),
        P(("row", "col")),
        P(),
        P(),
        P("row", "col", None),
        P("row", "col", None),
        P("row", "col"),
    )
    return jax.shard_map(
        on_device, mesh=mesh, in_specs=placed, out_specs=P(None, ("row", "col")), check_vma=False
    )
```

```python
import functools

import jax
import jax.numpy as jnp
import ml_dtypes
import numpy as np
from jax import lax
from jax.experimental import pallas as pl
from jax.experimental.pallas import tpu as pltpu
from jax.sharding import PartitionSpec as P

BLK = 128
VECS = 16
NTYPES = 6
BLOCKS = 32
HALF = 4 * BLOCKS
COLS = 3 * BLOCKS
ROWS = VECS + 8
DEPTH = 80
UNROLL = 8
SLOTS = 512
SLOT_SPAN = SLOTS + BLK
SPARE = 3 << 22
CELL = (11.0, 5.0, 11.0)
BOX = (44.0, 30.0, 44.0)
SOFTENING = 0.5

ERF_COEFFS = (
    1.2732353673862733,
    0.23198340332298037,
    0.01001461653081914,
    -0.0013852189685132543,
    7.466663090475016e-05,
)


def time_cost(microseconds):
    return pl.CostEstimate(
        flops=int(microseconds * 1_000_000_000), transcendentals=0, bytes_accessed=1_000_000
    )


PAIR_COST = time_cost(16)

VMEM = pl.BlockSpec(memory_space=pltpu.VMEM)
SMEM = pl.BlockSpec(memory_space=pltpu.SMEM)
ANY = pl.BlockSpec(memory_space=pl.ANY)
Y_GROUPS = [[0, 1, 2, 3], [4, 5, 6, 7]]
F32 = jnp.float32
BF16 = jnp.bfloat16


def sublane():
    return lax.broadcasted_iota(jnp.int32, (8, BLK), 0)


def split3(value):
    high = value.astype(BF16).astype(F32)
    rest = value - high
    middle = rest.astype(BF16).astype(F32)
    return high, middle, rest - middle


def lane_gather(source, index):
    return jnp.take_along_axis(source, index, axis=1, mode="promise_in_bounds")


def here():
    return lax.axis_index("row"), lax.axis_index("col")


def prep_kernel(
    positions_hbm, type_hbm, krylov_hbm, order_hbm, packed, geometry, positions, atom_type, krylov, order, done
):
    loads = [
        pltpu.make_async_copy(source, target, done.at[k])
        for k, (source, target) in enumerate(
            (
                (krylov_hbm, krylov),
                (positions_hbm, positions),
                (type_hbm, atom_type),
                (order_hbm, order),
            )
        )
    ]
    for load in loads:
        load.start()
    place = here()
    for load in loads[1:]:
        load.wait()
    middle = BLOCKS // 2 * BLK
    geometry[0:3, :] = positions[:, 0:middle]
    geometry[3:4, :] = atom_type[:, 0:middle].astype(F32)
    geometry[4:7, :] = positions[:, middle:]
    geometry[7:8, :] = atom_type[:, middle:].astype(F32)
    level = sublane()
    corner_x = CELL[0] * place[0].astype(F32) + BOX[0] / 2
    corner_y = CELL[1] * place[1].astype(F32) + BOX[1] / 2

    def one_geometry(block, carry):
        wanted = jnp.broadcast_to(order[pl.ds(block, 1), :], (8, BLK))
        chunk = wanted >> 7
        lane = wanted & 127
        folded = chunk & (BLOCKS // 2 - 1)
        geo = jnp.zeros((8, BLK), F32)
        for s in range(BLOCKS // 2):
            geo = jnp.where(folded == s, lane_gather(geometry[:, s * BLK : (s + 1) * BLK], lane), geo)
        geo = jnp.where(chunk < BLOCKS // 2, geo, pltpu.roll(geo, 4, 0))
        corner_z = CELL[2] * block.astype(F32) + BOX[2] / 2
        corner = jnp.where(
            level == 0, corner_x, jnp.where(level == 1, corner_y, jnp.where(level == 2, corner_z, 0.0))
        )
        local = jnp.where(level < 4, geo - corner, 0.0)
        coarse = jnp.floor(local * 4.0 + 0.5) * 0.25
        fine = jnp.where(level < 3, local - coarse, local)
        coded = jnp.where(level < 3, coarse, pltpu.roll(fine, 3, 0))
        packed[block, VECS:ROWS, :] = coded.astype(BF16)
        return carry

    lax.fori_loop(0, BLOCKS, one_geometry, 0)
    loads[0].wait()

    def one_block(block, carry):
        wanted = jnp.broadcast_to(order[pl.ds(block, 1), :], (8, BLK))
        chunk = wanted >> 7
        lane = wanted & 127
        top = jnp.zeros((8, BLK), F32)
        low = jnp.zeros((8, BLK), F32)
        for s in range(BLOCKS):
            span = slice(s * BLK, (s + 1) * BLK)
            top = jnp.where(chunk == s, lane_gather(krylov[0:8, span], lane), top)
            low = jnp.where(chunk == s, lane_gather(krylov[8:16, span], lane), low)
        packed[block, 0:VECS, :] = jnp.concatenate([top, low], axis=0).astype(BF16)
        return carry

    lax.fori_loop(0, BLOCKS, one_block, 0)


def side_kernel(
    count_hbm, rows_hbm, cols_hbm, order_hbm, inverse, codes, counts, count, rows, cols, order, done
):
    loads = [
        pltpu.make_async_copy(source, target, done.at[k])
        for k, (source, target) in enumerate(
            ((count_hbm, count), (rows_hbm, rows), (cols_hbm, cols), (order_hbm, order))
        )
    ]
    for load in loads:
        load.start()
    place = here()
    for load in loads:
        load.wait()
    row = rows[...]
    col = cols[...] - place[0] * BLOCKS
    step_y = place[1] - (row >> 5) + 4
    step_z = (col & 31) - (row & 31) + 2
    step = ((col >> 5) * 9 + step_y) * 5 + step_z
    diagonal = jnp.logical_and(col < BLOCKS, row == place[1] * BLOCKS + col)
    code = (row & 127) | (col << 7) | (step << 14) | (diagonal.astype(jnp.int32) << 22)
    live = lax.broadcasted_iota(jnp.int32, (1, SLOTS), 1) < count[0, 0]
    same = (row >> 7) == (place[1] >> 2)
    near = jnp.logical_and(live, same).astype(F32)
    far = jnp.logical_and(live, jnp.logical_not(same)).astype(F32)
    level = lax.broadcasted_iota(jnp.int32, (8, SLOTS), 0)
    wide = lambda v: jnp.broadcast_to(v, (8, SLOTS))
    flags = jnp.where(level == 0, wide(near), jnp.where(level == 1, wide(far), 0.0)).astype(BF16)
    earlier = (
        (lax.broadcasted_iota(jnp.int32, (SLOTS, SLOTS), 0) < lax.broadcasted_iota(jnp.int32, (SLOTS, SLOTS), 1))
        .astype(F32)
        .astype(BF16)
    )
    ranks = jnp.dot(flags, earlier, preferred_element_type=F32)
    target = jnp.where(
        near > 0.5, ranks[0:1], jnp.where(far > 0.5, ranks[1:2] + float(SLOT_SPAN), -1.0)
    ).astype(jnp.int32)
    chosen = (
        (
            lax.broadcasted_iota(jnp.int32, (2 * SLOT_SPAN, SLOTS), 0)
            == jnp.broadcast_to(target, (2 * SLOT_SPAN, SLOTS))
        )
        .astype(F32)
        .astype(BF16)
    )
    low = wide((code & 255).astype(F32))
    middle = wide(((code >> 8) & 255).astype(F32))
    high = wide((code >> 16).astype(F32))
    parts = jnp.where(level == 0, low, jnp.where(level == 1, middle, jnp.where(level == 2, high, 0.0)))
    moved = lax.dot_general(
        parts.astype(BF16), chosen, (((1,), (1,)), ((), ())), preferred_element_type=F32
    )
    listed = (moved[0:1] + moved[1:2] * 256.0 + moved[2:3] * 65536.0).astype(jnp.int32)
    near_count = jnp.sum(near).astype(jnp.int32)
    far_count = jnp.sum(far).astype(jnp.int32)
    spot = lax.broadcasted_iota(jnp.int32, (1, 2 * SLOT_SPAN), 1)
    in_near = spot < SLOT_SPAN
    used = jnp.where(in_near, spot, spot - SLOT_SPAN) < jnp.where(in_near, near_count, far_count)
    codes[...] = jnp.where(used, listed, SPARE)
    counts[0] = near_count
    counts[1] = far_count

    level_h = lax.broadcasted_iota(jnp.int32, (BLOCKS, BLK), 0)
    level_l = lax.broadcasted_iota(jnp.int32, (BLK, BLK), 0)
    lanes = lax.broadcasted_iota(jnp.int32, (BLOCKS, BLK), 1).astype(F32)
    left = []
    right = []
    for block in range(BLOCKS):
        wanted = order[block : block + 1, :]
        in_high = (level_h == jnp.broadcast_to(wanted >> 7, (BLOCKS, BLK))).astype(F32)
        in_low = (level_l == jnp.broadcast_to(wanted & 127, (BLK, BLK))).astype(F32)
        left.append(jnp.concatenate([in_high * float(block), in_high * lanes], axis=0).astype(BF16))
        right.append(in_low.astype(BF16))
    total = lax.dot_general(
        jnp.concatenate(left, axis=1),
        jnp.concatenate(right, axis=1),
        (((1,), (1,)), ((), ())),
        preferred_element_type=F32,
    )
    inverse[...] = (total[0:BLOCKS] * float(BLK) + total[BLOCKS:]).astype(jnp.int32)


def feature_kernel(type_width, own, after, second, features, vectors):
    level = sublane()
    squares = jnp.zeros((8, BLK), F32)
    for t in range(NTYPES):
        squares = jnp.where(level == t, type_width[t] * type_width[t], squares)
    low3 = level < 3
    low6 = level < 6
    zero = jnp.zeros((8, BLK), F32)
    ones3 = jnp.where(low3, 1.0, 0.0)

    for part, source in enumerate((own, after, second)):

        def one_block(block, part=part, source=source):
            vectors[part * BLOCKS + block] = source[block, 0:VECS, :]
            coded = source[block, VECS:ROWS, :].astype(F32)
            near = coded + pltpu.roll(coded, 5, 0)
            square = near * near
            weight = square[0:1] + square[1:2] + square[2:3] + SOFTENING * SOFTENING
            weight_h, weight_m, weight_l = split3(weight)
            coarse = jnp.where(low3, coded, pltpu.roll(coded, 3, 0)) * -2.0
            fine = jnp.where(low3, pltpu.roll(coded, 5, 0), coded) * -2.0
            own_type = jnp.broadcast_to(coded[6:7], (8, BLK))
            own_square = jnp.zeros((8, BLK), F32)
            for t in range(NTYPES):
                own_square = jnp.where(own_type == float(t), type_width[t] * type_width[t], own_square)
            scale = 1.0 / (own_square + squares)
            scale_h, scale_m, scale_l = split3(jnp.where(low6, scale, 0.0))
            wide = lambda v: jnp.broadcast_to(v, (8, BLK))
            weights = jnp.where(
                level == 0,
                wide(weight_h),
                jnp.where(level == 1, wide(weight_m), jnp.where(level == 2, wide(weight_l), 0.0)),
            )
            stacked = jnp.concatenate(
                [
                    jnp.where(low6, coarse, 0.0),
                    jnp.where(low6, fine, 0.0),
                    jnp.where(low6, coded, 1.0),
                    weights,
                    ones3,
                    zero,
                    scale_h,
                    scale_m,
                    scale_l,
                ]
                + [zero] * 7,
                axis=0,
            )
            features[part * BLOCKS + block] = stacked.T.astype(BF16)

        def some_blocks(turn, carry, one_block=one_block):
            for extra in range(4):
                one_block(turn * 4 + extra)
            return carry

        lax.fori_loop(0, BLOCKS // 4, some_blocks, 0)


def row_operands(row_data, operands):
    level = sublane()
    zero = jnp.zeros((8, BLK), F32)

    def some_rows(turn, carry):
        for extra in range(8):
            row = turn * 8 + extra
            coded = row_data[row, VECS:ROWS, :].astype(F32)
            near = coded + pltpu.roll(coded, 5, 0)
            square = near * near
            weight_h, weight_m, weight_l = split3(square[0:1] + square[1:2] + square[2:3])
            wide = lambda v: jnp.broadcast_to(v, (8, BLK))
            weights = jnp.where(
                level == 0,
                wide(weight_h),
                jnp.where(level == 1, wide(weight_m), jnp.where(level == 2, wide(weight_l), 0.0)),
            )
            hot = (level.astype(F32) == wide(coded[6:7])).astype(F32)
            operands[row] = jnp.concatenate(
                [coded, coded, weights, zero, hot, hot, hot, zero], axis=0
            ).astype(BF16)
        return carry

    lax.fori_loop(0, HALF // 8, some_rows, 0)


def pair_products(code, operands, features, step_rows, step_lanes):
    step = (code >> 14) & 255
    right = operands[code & 127]
    empty = jnp.zeros((48, BLK), BF16)
    left = features[(code >> 7) & 127].reshape(8, 16, BLK) + step_lanes[step][None]
    both = jnp.concatenate(
        [
            jnp.concatenate([right[0:16], step_rows[step], right[16:32], empty[0:32]], axis=0),
            jnp.concatenate([empty, right[32:64]], axis=0),
        ],
        axis=1,
    )
    return jnp.dot(left.reshape(BLK, BLK)[:, 0:DEPTH], both, preferred_element_type=F32)


def tile_values(distance2, inverse_spread):
    square = distance2 * inverse_spread
    poly = ERF_COEFFS[-1]
    for coefficient in ERF_COEFFS[-2::-1]:
        poly = poly * square + coefficient
    poly = poly * square
    return (jnp.tanh(poly * lax.rsqrt(poly)) * lax.rsqrt(distance2)).astype(BF16)


def pair_loop(
    phase, counts, codes, row_data, operands, vectors, features, step_rows, step_lanes, row_acc, col_acc, waiting, tiles
):
    base = phase * SLOT_SPAN
    batches = (counts[phase] + UNROLL - 1) // UNROLL

    def one_turn(turn, carry):
        adding = base + jnp.maximum(turn - 2, 0) * UNROLL
        opening = base + jnp.maximum(jnp.minimum(turn, batches - 1), 0) * UNROLL
        sums = []
        for first in range(0, UNROLL, 2):
            done = [codes[0, adding + first + k] for k in range(2)]
            both = [tiles[first + k] for k in range(2)]
            forward = jnp.dot(
                jnp.concatenate([vectors[(code >> 7) & 127] for code in done], axis=0),
                jnp.concatenate(both, axis=1),
                preferred_element_type=F32,
            )
            backward = lax.dot_general(
                jnp.concatenate([row_data[code & 127, 0:VECS, :] for code in done], axis=0),
                jnp.concatenate(both, axis=0),
                (((1,), (1,)), ((), ())),
                preferred_element_type=F32,
            )
            for k, code in enumerate(done):
                to_row = jnp.where(jnp.logical_or(turn < 2, ((code >> 23) & 1) == 1), HALF, code & 127)
                to_col = jnp.where(
                    jnp.logical_or(turn < 2, ((code >> 22) & 1) == 1), COLS, (code >> 7) & 127
                )
                own = (slice(k * VECS, (k + 1) * VECS), slice(k * BLK, (k + 1) * BLK))
                sums.append((to_row, forward[own], to_col, backward[own]))
            for k in range(2):
                slot = first + k
                tiles[slot] = tile_values(waiting[slot, :, 0:BLK], waiting[slot, :, BLK:])
                code = codes[0, opening + slot]
                waiting[slot] = pair_products(code, operands, features, step_rows, step_lanes)
        for to_row, forward, to_col, backward in sums:
            row_acc[to_row] += forward
            col_acc[to_col] += backward
        return carry

    lax.fori_loop(0, batches + 2, one_turn, 0)


def near_far_kernel(phase, *refs):
    counts, codes = refs[0:2]
    pieces = refs[2:6]
    vectors, features, step_rows, step_lanes = refs[6:10]
    col_in = refs[10:11] if phase == 1 else ()
    outs = refs[10 + len(col_in) : -6]
    row_data, operands, row_acc, col_acc, waiting, tiles = refs[-6:]
    position = here()[1] & 3
    for k, piece in enumerate(pieces):
        start = pl.multiple_of(((position - k) & 3) * BLOCKS, BLOCKS)
        row_data[pl.ds(start, BLOCKS)] = piece[...]
    row_operands(row_data, operands)
    row_acc[...] = jnp.zeros_like(row_acc)
    if phase == 0:
        col_acc[...] = jnp.zeros_like(col_acc)
    else:
        col_acc[0:COLS] = col_in[0][...]
    pair_loop(
        phase,
        counts,
        codes,
        row_data,
        operands,
        vectors,
        features,
        step_rows,
        step_lanes,
        row_acc,
        col_acc,
        waiting,
        tiles,
    )
    for k in range(4):
        start = pl.multiple_of(((position + k) & 3) * BLOCKS, BLOCKS)
        outs[k][...] = row_acc[pl.ds(start, BLOCKS)].astype(outs[k].dtype)
    if phase == 0:
        outs[4][...] = col_acc[0:COLS]
    else:
        for step in range(3):
            outs[4 + step][...] = col_acc[step * BLOCKS : (step + 1) * BLOCKS].astype(outs[4 + step].dtype)


def sum_kernel(*refs):
    total = refs[0][...].astype(F32)
    for ref in refs[1:-1]:
        total = total + ref[...].astype(F32)
    refs[-1][...] = total.astype(refs[-1].dtype)


def final_kernel(type_hard, *refs):
    atom_type, krylov, inverse, out, blocked = refs[-5:]
    parts = refs[:-5]

    def add_up(block, carry):
        total = parts[0][block]
        for part in parts[1:]:
            total = total + part[block].astype(F32)
        blocked[block] = total
        return carry

    lax.fori_loop(0, BLOCKS, add_up, 0)
    for chunk in range(BLOCKS):
        wanted = jnp.broadcast_to(inverse[chunk : chunk + 1, :], (8, BLK))
        source = wanted >> 7
        lane = wanted & 127
        span = slice(chunk * BLK, (chunk + 1) * BLK)
        kind = jnp.broadcast_to(atom_type[:, span], (8, BLK))
        hard = jnp.zeros((8, BLK), F32)
        for t in range(NTYPES):
            hard = jnp.where(kind == t, type_hard[t], hard)

        def pick(block, carry, source=source, lane=lane):
            top, low = carry
            here = source == block
            top = jnp.where(here, lane_gather(blocked[block, 0:8, :], lane), top)
            low = jnp.where(here, lane_gather(blocked[block, 8:16, :], lane), low)
            return top, low

        start = (hard * 0.0, hard * 0.0)
        top, low = lax.fori_loop(0, BLOCKS, pick, start, unroll=True)
        out[0:8, span] = top + hard * krylov[0:8, span]
        out[8:16, span] = low + hard * krylov[8:16, span]


def shape(dims, dtype):
    return jax.ShapeDtypeStruct(dims, dtype)


def call(kernel, out_shape, in_specs, out_specs, name, scratch=(), vmem=20, cost=None):
    return pl.pallas_call(
        kernel,
        out_shape=out_shape,
        in_specs=in_specs,
        out_specs=out_specs,
        scratch_shapes=list(scratch),
        compiler_params=pltpu.CompilerParams(vmem_limit_bytes=vmem << 20),
        cost_estimate=cost,
        name=name,
    )


def step_tables():
    x, y, z = np.meshgrid(np.arange(3), np.arange(-4, 5), np.arange(-2, 3), indexing="ij")
    steps = np.stack([x, y, z], axis=-1).reshape(-1, 3) * np.array(CELL)
    squared = np.sum(steps * steps, axis=1).astype(np.float32)
    coarse = squared.astype(ml_dtypes.bfloat16).astype(np.float32)
    rows = np.zeros((len(steps), 16, BLK), np.float32)
    rows[:, 0:3] = rows[:, 3:6] = 2.0 * steps[:, :, None]
    rows[:, 6] = coarse[:, None]
    rows[:, 7] = (squared - coarse)[:, None]
    rows[:, 8:11] = 1.0
    lanes = np.zeros((len(steps), 16, BLK), np.float32)
    lanes[:, :, 0:3] = lanes[:, :, 3:6] = -2.0 * steps[:, None, :]
    return rows.astype(ml_dtypes.bfloat16), lanes.astype(ml_dtypes.bfloat16)


def passed_down(value, steps):
    count = lax.axis_size("row")
    return lax.ppermute(value, "row", [(s, s - steps) for s in range(steps, count)])


def passed_up(value, steps):
    count = lax.axis_size("row")
    return lax.ppermute(value, "row", [(s, s + steps) for s in range(count - steps)])


def across(value):
    return lax.ppermute(value, "col", [(c, c ^ 4) for c in range(8)])


def around(value, steps):
    return lax.ppermute(value, "col", [(c, (c & 4) + (c + steps) % 4) for c in range(8)])


def on_device(
    positions, atom_type, krylov, block_order, type_width, type_hard, pair_rows, pair_cols, pair_count
):
    order = block_order.reshape(BLOCKS, BLK)
    kinds = atom_type.reshape(1, -1)

    packed = call(
        prep_kernel,
        shape((BLOCKS, ROWS, BLK), BF16),
        [ANY, ANY, ANY, ANY],
        VMEM,
        "prep",
        scratch=[
            pltpu.VMEM((8, BLOCKS // 2 * BLK), F32),
            pltpu.VMEM((3, BLOCKS * BLK), F32),
            pltpu.VMEM((1, BLOCKS * BLK), jnp.int32),
            pltpu.VMEM((VECS, BLOCKS * BLK), F32),
            pltpu.VMEM((BLOCKS, BLK), jnp.int32),
            pltpu.SemaphoreType.DMA((4,)),
        ],
        vmem=62,
    )(positions, kinds, krylov, order)

    other = across(packed)
    after = passed_down(packed, 1)
    second = passed_down(packed, 2)
    rows_list, _ = lax.optimization_barrier((pair_rows.reshape(1, SLOTS), packed))

    inverse, codes, counts = call(
        side_kernel,
        (
            shape((BLOCKS, BLK), jnp.int32),
            shape((1, 2 * SLOT_SPAN), jnp.int32),
            shape((2,), jnp.int32),
        ),
        [ANY, ANY, ANY, ANY],
        (VMEM, VMEM, SMEM),
        "side",
        scratch=[
            pltpu.SMEM((1, 1), jnp.int32),
            pltpu.VMEM((1, SLOTS), jnp.int32),
            pltpu.VMEM((1, SLOTS), jnp.int32),
            pltpu.VMEM((BLOCKS, BLK), jnp.int32),
            pltpu.SemaphoreType.DMA((4,)),
        ],
        vmem=62,
        cost=time_cost(2),
    )(pair_count, rows_list, pair_cols.reshape(1, SLOTS), order)

    codes, packed = lax.optimization_barrier((codes, packed))
    near_rows = [packed] + [around(packed, k) for k in (1, 2, 3)]

    features, vectors = call(
        feature_kernel,
        (shape((COLS, BLK, BLK), BF16), shape((COLS, VECS, BLK), BF16)),
        [SMEM, VMEM, VMEM, VMEM],
        (VMEM, VMEM),
        "features",
        cost=time_cost(12),
    )(type_width, packed, after, second)

    far_rows = [other] + [around(other, k) for k in (1, 2, 3)]
    step_rows, step_lanes = step_tables()
    codes, _ = lax.optimization_barrier((codes, other))
    scratch = [
        pltpu.VMEM((HALF, ROWS, BLK), BF16),
        pltpu.VMEM((HALF, 64, BLK), BF16),
        pltpu.VMEM((HALF + 1, VECS, BLK), F32),
        pltpu.VMEM((COLS + 1, VECS, BLK), F32),
        pltpu.VMEM((UNROLL, BLK, 2 * BLK), F32),
        pltpu.VMEM((UNROLL, BLK, BLK), BF16),
    ]
    block_set = (BLOCKS, VECS, BLK)
    *near_sums, col_sums = call(
        functools.partial(near_far_kernel, 0),
        [shape(block_set, F32)] + [shape(block_set, BF16)] * 3 + [shape((COLS, VECS, BLK), F32)],
        [SMEM] * 2 + [VMEM] * 8,
        [VMEM] * 5,
        "pairs_near",
        scratch=scratch,
        cost=PAIR_COST,
    )(counts, codes, *near_rows, vectors, features, step_rows, step_lanes)

    *far_sums, own_sum, after_sum, last_sum = call(
        functools.partial(near_far_kernel, 1),
        [shape(block_set, BF16)] * 4 + [shape(block_set, F32)] + [shape(block_set, BF16)] * 2,
        [SMEM] * 2 + [VMEM] * 9,
        [VMEM] * 7,
        "pairs_far",
        scratch=scratch,
        cost=PAIR_COST,
    )(counts, codes, *far_rows, vectors, features, step_rows, step_lanes, col_sums)

    far_parts = [far_sums[0]] + [around(far_sums[k], k) for k in (1, 2, 3)]
    from_prior = passed_up(after_sum, 1)
    from_second = passed_up(last_sum, 2)
    far_sum = call(
        sum_kernel, shape((BLOCKS, VECS, BLK), BF16), [VMEM] * 4, VMEM, "far_sum"
    )(*far_parts)
    from_far = across(far_sum)
    near_sums, _ = lax.optimization_barrier((near_sums, (far_sum, from_prior, from_second)))
    near_parts = [near_sums[0]] + [around(near_sums[k], k) for k in (1, 2, 3)]

    parts = [own_sum, from_far, from_prior, from_second, *near_parts]
    return call(
        final_kernel,
        shape(krylov.shape, F32),
        [SMEM] + [VMEM] * (len(parts) + 3),
        VMEM,
        "final",
        scratch=[pltpu.VMEM((BLOCKS, VECS, BLK), F32)],
    )(type_hard, *parts, kinds, krylov, inverse)


def solution(mesh):
    placed = (
        P(None, ("row", "col")),
        P(("row", "col")),
        P(None, ("row", "col")),
        P(("row", "col")),
        P(),
        P(),
        P("row", "col", None),
        P("row", "col", None),
        P("row", "col"),
    )
    return jax.shard_map(
        on_device, mesh=mesh, in_specs=placed, out_specs=P(None, ("row", "col")), check_vma=False
    )
```

```python
import functools

import jax
import jax.numpy as jnp
import ml_dtypes
import numpy as np
from jax import lax
from jax.experimental import pallas as pl
from jax.experimental.pallas import tpu as pltpu
from jax.sharding import PartitionSpec as P

BLK = 128
VECS = 16
NTYPES = 6
BLOCKS = 32
HALF = 4 * BLOCKS
COLS = 3 * BLOCKS
ROWS = VECS + 8
DEPTH = 80
UNROLL = 8
SLOTS = 512
SLOT_SPAN = SLOTS + BLK
SPARE = 3 << 22
PREP_BLOCKS = 8
CELL = (11.0, 5.0, 11.0)
BOX = (44.0, 30.0, 44.0)
SOFTENING = 0.5

ERF_COEFFS = (
    1.2732353673862733,
    0.23198340332298037,
    0.01001461653081914,
    -0.0013852189685132543,
    7.466663090475016e-05,
)


def time_cost(microseconds):
    return pl.CostEstimate(
        flops=int(microseconds * 1_000_000_000), transcendentals=0, bytes_accessed=1_000_000
    )


PAIR_COST = time_cost(16)

VMEM = pl.BlockSpec(memory_space=pltpu.VMEM)
SMEM = pl.BlockSpec(memory_space=pltpu.SMEM)
ANY = pl.BlockSpec(memory_space=pl.ANY)
Y_GROUPS = [[0, 1, 2, 3], [4, 5, 6, 7]]
F32 = jnp.float32
BF16 = jnp.bfloat16


def sublane():
    return lax.broadcasted_iota(jnp.int32, (8, BLK), 0)


def split3(value):
    high = value.astype(BF16).astype(F32)
    rest = value - high
    middle = rest.astype(BF16).astype(F32)
    return high, middle, rest - middle


def lane_gather(source, index):
    return jnp.take_along_axis(source, index, axis=1, mode="promise_in_bounds")


def here():
    return lax.axis_index("row"), lax.axis_index("col")


def prep_kernel(
    positions_hbm, type_hbm, krylov_hbm, order_hbm, packed, geometry, positions, atom_type, krylov, order, done
):
    loads = [
        pltpu.make_async_copy(source, target, done.at[k])
        for k, (source, target) in enumerate(
            (
                (krylov_hbm, krylov),
                (positions_hbm, positions),
                (type_hbm, atom_type),
                (order_hbm, order),
            )
        )
    ]
    for load in loads:
        load.start()
    place = here()
    for load in loads[1:]:
        load.wait()
    middle = BLOCKS // 2 * BLK
    geometry[0:3, :] = positions[:, 0:middle]
    geometry[3:4, :] = atom_type[:, 0:middle].astype(F32)
    geometry[4:7, :] = positions[:, middle:]
    geometry[7:8, :] = atom_type[:, middle:].astype(F32)
    level = sublane()
    corner_x = CELL[0] * place[0].astype(F32) + BOX[0] / 2
    corner_y = CELL[1] * place[1].astype(F32) + BOX[1] / 2

    def one_block(block):
        wanted = jnp.broadcast_to(order[pl.ds(block, 1), :], (8, BLK))
        chunk = wanted >> 7
        lane = wanted & 127
        folded = chunk & (BLOCKS // 2 - 1)
        top = jnp.zeros((8, BLK), F32)
        low = jnp.zeros((8, BLK), F32)
        geo = jnp.zeros((8, BLK), F32)
        for s in range(BLOCKS):
            span = slice(s * BLK, (s + 1) * BLK)
            top = jnp.where(chunk == s, lane_gather(krylov[0:8, span], lane), top)
            low = jnp.where(chunk == s, lane_gather(krylov[8:16, span], lane), low)
            if s < BLOCKS // 2:
                geo = jnp.where(folded == s, lane_gather(geometry[:, span], lane), geo)
        geo = jnp.where(chunk < BLOCKS // 2, geo, pltpu.roll(geo, 4, 0))
        corner_z = CELL[2] * block.astype(F32) + BOX[2] / 2
        corner = jnp.where(
            level == 0, corner_x, jnp.where(level == 1, corner_y, jnp.where(level == 2, corner_z, 0.0))
        )
        local = jnp.where(level < 4, geo - corner, 0.0)
        coarse = jnp.floor(local * 4.0 + 0.5) * 0.25
        fine = jnp.where(level < 3, local - coarse, local)
        coded = jnp.where(level < 3, coarse, pltpu.roll(fine, 3, 0))
        packed[block, 0:VECS, :] = jnp.concatenate([top, low], axis=0).astype(BF16)
        packed[block, VECS:ROWS, :] = coded.astype(BF16)

    def some_blocks(turn, carry):
        for extra in range(PREP_BLOCKS):
            one_block(turn * PREP_BLOCKS + extra)
        return carry

    loads[0].wait()
    lax.fori_loop(0, BLOCKS // PREP_BLOCKS, some_blocks, 0)


def side_kernel(
    count_hbm, rows_hbm, cols_hbm, order_hbm, inverse, codes, counts, count, rows, cols, order, done
):
    loads = [
        pltpu.make_async_copy(source, target, done.at[k])
        for k, (source, target) in enumerate(
            ((count_hbm, count), (rows_hbm, rows), (cols_hbm, cols), (order_hbm, order))
        )
    ]
    for load in loads:
        load.start()
    place = here()
    for load in loads:
        load.wait()
    row = rows[...]
    col = cols[...] - place[0] * BLOCKS
    step_y = place[1] - (row >> 5) + 4
    step_z = (col & 31) - (row & 31) + 2
    step = ((col >> 5) * 9 + step_y) * 5 + step_z
    diagonal = jnp.logical_and(col < BLOCKS, row == place[1] * BLOCKS + col)
    code = (row & 127) | (col << 7) | (step << 14) | (diagonal.astype(jnp.int32) << 22)
    live = lax.broadcasted_iota(jnp.int32, (1, SLOTS), 1) < count[0, 0]
    same = (row >> 7) == (place[1] >> 2)
    near = jnp.logical_and(live, same).astype(F32)
    far = jnp.logical_and(live, jnp.logical_not(same)).astype(F32)
    level = lax.broadcasted_iota(jnp.int32, (8, SLOTS), 0)
    wide = lambda v: jnp.broadcast_to(v, (8, SLOTS))
    flags = jnp.where(level == 0, wide(near), jnp.where(level == 1, wide(far), 0.0)).astype(BF16)
    earlier = (
        (lax.broadcasted_iota(jnp.int32, (SLOTS, SLOTS), 0) < lax.broadcasted_iota(jnp.int32, (SLOTS, SLOTS), 1))
        .astype(F32)
        .astype(BF16)
    )
    ranks = jnp.dot(flags, earlier, preferred_element_type=F32)
    target = jnp.where(
        near > 0.5, ranks[0:1], jnp.where(far > 0.5, ranks[1:2] + float(SLOT_SPAN), -1.0)
    ).astype(jnp.int32)
    chosen = (
        (
            lax.broadcasted_iota(jnp.int32, (2 * SLOT_SPAN, SLOTS), 0)
            == jnp.broadcast_to(target, (2 * SLOT_SPAN, SLOTS))
        )
        .astype(F32)
        .astype(BF16)
    )
    low = wide((code & 255).astype(F32))
    middle = wide(((code >> 8) & 255).astype(F32))
    high = wide((code >> 16).astype(F32))
    parts = jnp.where(level == 0, low, jnp.where(level == 1, middle, jnp.where(level == 2, high, 0.0)))
    moved = lax.dot_general(
        parts.astype(BF16), chosen, (((1,), (1,)), ((), ())), preferred_element_type=F32
    )
    listed = (moved[0:1] + moved[1:2] * 256.0 + moved[2:3] * 65536.0).astype(jnp.int32)
    near_count = jnp.sum(near).astype(jnp.int32)
    far_count = jnp.sum(far).astype(jnp.int32)
    spot = lax.broadcasted_iota(jnp.int32, (1, 2 * SLOT_SPAN), 1)
    in_near = spot < SLOT_SPAN
    used = jnp.where(in_near, spot, spot - SLOT_SPAN) < jnp.where(in_near, near_count, far_count)
    codes[...] = jnp.where(used, listed, SPARE)
    counts[0] = near_count
    counts[1] = far_count

    level_h = lax.broadcasted_iota(jnp.int32, (BLOCKS, BLK), 0)
    level_l = lax.broadcasted_iota(jnp.int32, (BLK, BLK), 0)
    lanes = lax.broadcasted_iota(jnp.int32, (BLOCKS, BLK), 1).astype(F32)
    left = []
    right = []
    for block in range(BLOCKS):
        wanted = order[block : block + 1, :]
        in_high = (level_h == jnp.broadcast_to(wanted >> 7, (BLOCKS, BLK))).astype(F32)
        in_low = (level_l == jnp.broadcast_to(wanted & 127, (BLK, BLK))).astype(F32)
        left.append(jnp.concatenate([in_high * float(block), in_high * lanes], axis=0).astype(BF16))
        right.append(in_low.astype(BF16))
    total = lax.dot_general(
        jnp.concatenate(left, axis=1),
        jnp.concatenate(right, axis=1),
        (((1,), (1,)), ((), ())),
        preferred_element_type=F32,
    )
    inverse[...] = (total[0:BLOCKS] * float(BLK) + total[BLOCKS:]).astype(jnp.int32)


def feature_kernel(type_width, own, after, second, features, vectors):
    level = sublane()
    squares = jnp.zeros((8, BLK), F32)
    for t in range(NTYPES):
        squares = jnp.where(level == t, type_width[t] * type_width[t], squares)
    low3 = level < 3
    low6 = level < 6
    zero = jnp.zeros((8, BLK), F32)
    ones3 = jnp.where(low3, 1.0, 0.0)

    for part, source in enumerate((own, after, second)):

        def one_block(block, part=part, source=source):
            vectors[part * BLOCKS + block] = source[block, 0:VECS, :]
            coded = source[block, VECS:ROWS, :].astype(F32)
            near = coded + pltpu.roll(coded, 5, 0)
            square = near * near
            weight = square[0:1] + square[1:2] + square[2:3] + SOFTENING * SOFTENING
            weight_h, weight_m, weight_l = split3(weight)
            coarse = jnp.where(low3, coded, pltpu.roll(coded, 3, 0)) * -2.0
            fine = jnp.where(low3, pltpu.roll(coded, 5, 0), coded) * -2.0
            own_type = jnp.broadcast_to(coded[6:7], (8, BLK))
            own_square = jnp.zeros((8, BLK), F32)
            for t in range(NTYPES):
                own_square = jnp.where(own_type == float(t), type_width[t] * type_width[t], own_square)
            scale = 1.0 / (own_square + squares)
            scale_h, scale_m, scale_l = split3(jnp.where(low6, scale, 0.0))
            wide = lambda v: jnp.broadcast_to(v, (8, BLK))
            weights = jnp.where(
                level == 0,
                wide(weight_h),
                jnp.where(level == 1, wide(weight_m), jnp.where(level == 2, wide(weight_l), 0.0)),
            )
            stacked = jnp.concatenate(
                [
                    jnp.where(low6, coarse, 0.0),
                    jnp.where(low6, fine, 0.0),
                    jnp.where(low6, coded, 1.0),
                    weights,
                    ones3,
                    zero,
                    scale_h,
                    scale_m,
                    scale_l,
                ]
                + [zero] * 7,
                axis=0,
            )
            features[part * BLOCKS + block] = stacked.astype(BF16).T

        def some_blocks(turn, carry, one_block=one_block):
            for extra in range(16):
                one_block(turn * 16 + extra)
            return carry

        lax.fori_loop(0, BLOCKS // 16, some_blocks, 0)


def row_operands(row_data, operands):
    level = sublane()
    zero = jnp.zeros((8, BLK), F32)

    def some_rows(turn, carry):
        for extra in range(16):
            row = turn * 16 + extra
            coded = row_data[row, VECS:ROWS, :].astype(F32)
            near = coded + pltpu.roll(coded, 5, 0)
            square = near * near
            weight_h, weight_m, weight_l = split3(square[0:1] + square[1:2] + square[2:3])
            wide = lambda v: jnp.broadcast_to(v, (8, BLK))
            weights = jnp.where(
                level == 0,
                wide(weight_h),
                jnp.where(level == 1, wide(weight_m), jnp.where(level == 2, wide(weight_l), 0.0)),
            )
            hot = (level.astype(F32) == wide(coded[6:7])).astype(F32)
            operands[row] = jnp.concatenate(
                [coded, coded, weights, zero, hot, hot, hot, zero], axis=0
            ).astype(BF16)
        return carry

    lax.fori_loop(0, HALF // 16, some_rows, 0)


def pair_products(code, operands, features, step_rows, step_lanes):
    step = (code >> 14) & 255
    right = operands[code & 127]
    empty = jnp.zeros((48, BLK), BF16)
    left = features[(code >> 7) & 127].reshape(8, 16, BLK) + step_lanes[step][None]
    both = jnp.concatenate(
        [
            jnp.concatenate([right[0:16], step_rows[step], right[16:32], empty[0:32]], axis=0),
            jnp.concatenate([empty, right[32:64]], axis=0),
        ],
        axis=1,
    )
    return jnp.dot(left.reshape(BLK, BLK)[:, 0:DEPTH], both, preferred_element_type=F32)


def tile_values(distance2, inverse_spread):
    square = distance2 * inverse_spread
    poly = ERF_COEFFS[-1]
    for coefficient in ERF_COEFFS[-2::-1]:
        poly = poly * square + coefficient
    poly = poly * square
    return (jnp.tanh(poly * lax.rsqrt(poly)) * lax.rsqrt(distance2)).astype(BF16)


def pair_loop(
    phase, counts, codes, row_data, operands, vectors, features, step_rows, step_lanes, row_acc, col_acc, waiting, tiles
):
    base = phase * SLOT_SPAN
    batches = (counts[phase] + UNROLL - 1) // UNROLL

    def one_turn(turn, carry):
        adding = base + jnp.maximum(turn - 2, 0) * UNROLL
        opening = base + jnp.maximum(jnp.minimum(turn, batches - 1), 0) * UNROLL
        sums = []
        for first in range(0, UNROLL, 2):
            done = [codes[0, adding + first + k] for k in range(2)]
            both = [tiles[first + k] for k in range(2)]
            forward = jnp.dot(
                jnp.concatenate([vectors[(code >> 7) & 127] for code in done], axis=0),
                jnp.concatenate(both, axis=1),
                preferred_element_type=F32,
            )
            backward = lax.dot_general(
                jnp.concatenate([row_data[code & 127, 0:VECS, :] for code in done], axis=0),
                jnp.concatenate(both, axis=0),
                (((1,), (1,)), ((), ())),
                preferred_element_type=F32,
            )
            for k, code in enumerate(done):
                to_row = jnp.where(jnp.logical_or(turn < 2, ((code >> 23) & 1) == 1), HALF, code & 127)
                to_col = jnp.where(
                    jnp.logical_or(turn < 2, ((code >> 22) & 1) == 1), COLS, (code >> 7) & 127
                )
                own = (slice(k * VECS, (k + 1) * VECS), slice(k * BLK, (k + 1) * BLK))
                sums.append((to_row, forward[own], to_col, backward[own]))
            for k in range(2):
                slot = first + k
                tiles[slot] = tile_values(waiting[slot, :, 0:BLK], waiting[slot, :, BLK:])
                code = codes[0, opening + slot]
                waiting[slot] = pair_products(code, operands, features, step_rows, step_lanes)
        for to_row, forward, to_col, backward in sums:
            row_acc[to_row] += forward
            col_acc[to_col] += backward
        return carry

    lax.fori_loop(0, batches + 2, one_turn, 0)


def near_far_kernel(phase, *refs):
    counts, codes = refs[0:2]
    pieces = refs[2:6]
    vectors, features, step_rows, step_lanes = refs[6:10]
    col_in = refs[10:11] if phase == 1 else ()
    outs = refs[10 + len(col_in) : -6]
    row_data, operands, row_acc, col_acc, waiting, tiles = refs[-6:]
    position = here()[1] & 3
    for k, piece in enumerate(pieces):
        start = pl.multiple_of(((position - k) & 3) * BLOCKS, BLOCKS)
        row_data[pl.ds(start, BLOCKS)] = piece[...]
    row_operands(row_data, operands)
    row_acc[...] = jnp.zeros_like(row_acc)
    if phase == 0:
        col_acc[...] = jnp.zeros_like(col_acc)
    else:
        col_acc[0:COLS] = col_in[0][...]
    pair_loop(
        phase,
        counts,
        codes,
        row_data,
        operands,
        vectors,
        features,
        step_rows,
        step_lanes,
        row_acc,
        col_acc,
        waiting,
        tiles,
    )
    for k in range(4):
        start = pl.multiple_of(((position + k) & 3) * BLOCKS, BLOCKS)
        outs[k][...] = row_acc[pl.ds(start, BLOCKS)].astype(outs[k].dtype)
    if phase == 0:
        outs[4][...] = col_acc[0:COLS]
    else:
        for step in range(3):
            outs[4 + step][...] = col_acc[step * BLOCKS : (step + 1) * BLOCKS].astype(outs[4 + step].dtype)


def sum_kernel(*refs):
    total = refs[0][...].astype(F32)
    for ref in refs[1:-1]:
        total = total + ref[...].astype(F32)
    refs[-1][...] = total.astype(refs[-1].dtype)


def final_kernel(type_hard, *refs):
    atom_type, krylov, inverse, out, blocked = refs[-5:]
    parts = refs[:-5]

    def add_up(block, carry):
        total = parts[0][block]
        for part in parts[1:]:
            total = total + part[block].astype(F32)
        blocked[block] = total
        return carry

    lax.fori_loop(0, BLOCKS, add_up, 0)
    for chunk in range(BLOCKS):
        wanted = jnp.broadcast_to(inverse[chunk : chunk + 1, :], (8, BLK))
        source = wanted >> 7
        lane = wanted & 127
        span = slice(chunk * BLK, (chunk + 1) * BLK)
        kind = jnp.broadcast_to(atom_type[:, span], (8, BLK))
        hard = jnp.zeros((8, BLK), F32)
        for t in range(NTYPES):
            hard = jnp.where(kind == t, type_hard[t], hard)

        def pick(block, carry, source=source, lane=lane):
            top, low = carry
            here = source == block
            top = jnp.where(here, lane_gather(blocked[block, 0:8, :], lane), top)
            low = jnp.where(here, lane_gather(blocked[block, 8:16, :], lane), low)
            return top, low

        start = (hard * 0.0, hard * 0.0)
        top, low = lax.fori_loop(0, BLOCKS, pick, start, unroll=True)
        out[0:8, span] = top + hard * krylov[0:8, span]
        out[8:16, span] = low + hard * krylov[8:16, span]


def shape(dims, dtype):
    return jax.ShapeDtypeStruct(dims, dtype)


def call(kernel, out_shape, in_specs, out_specs, name, scratch=(), vmem=20, cost=None):
    return pl.pallas_call(
        kernel,
        out_shape=out_shape,
        in_specs=in_specs,
        out_specs=out_specs,
        scratch_shapes=list(scratch),
        compiler_params=pltpu.CompilerParams(vmem_limit_bytes=vmem << 20),
        cost_estimate=cost,
        name=name,
    )


def step_tables():
    x, y, z = np.meshgrid(np.arange(3), np.arange(-4, 5), np.arange(-2, 3), indexing="ij")
    steps = np.stack([x, y, z], axis=-1).reshape(-1, 3) * np.array(CELL)
    squared = np.sum(steps * steps, axis=1).astype(np.float32)
    coarse = squared.astype(ml_dtypes.bfloat16).astype(np.float32)
    rows = np.zeros((len(steps), 16, BLK), np.float32)
    rows[:, 0:3] = rows[:, 3:6] = 2.0 * steps[:, :, None]
    rows[:, 6] = coarse[:, None]
    rows[:, 7] = (squared - coarse)[:, None]
    rows[:, 8:11] = 1.0
    lanes = np.zeros((len(steps), 16, BLK), np.float32)
    lanes[:, :, 0:3] = lanes[:, :, 3:6] = -2.0 * steps[:, None, :]
    return rows.astype(ml_dtypes.bfloat16), lanes.astype(ml_dtypes.bfloat16)


def passed_down(value, steps):
    count = lax.axis_size("row")
    return lax.ppermute(value, "row", [(s, s - steps) for s in range(steps, count)])


def passed_up(value, steps):
    count = lax.axis_size("row")
    return lax.ppermute(value, "row", [(s, s + steps) for s in range(count - steps)])


def across(value):
    return lax.ppermute(value, "col", [(c, c ^ 4) for c in range(8)])


def around(value, steps):
    return lax.ppermute(value, "col", [(c, (c & 4) + (c + steps) % 4) for c in range(8)])


def on_device(
    positions, atom_type, krylov, block_order, type_width, type_hard, pair_rows, pair_cols, pair_count
):
    order = block_order.reshape(BLOCKS, BLK)
    kinds = atom_type.reshape(1, -1)

    packed = call(
        prep_kernel,
        shape((BLOCKS, ROWS, BLK), BF16),
        [ANY, ANY, ANY, ANY],
        VMEM,
        "prep",
        scratch=[
            pltpu.VMEM((8, BLOCKS // 2 * BLK), F32),
            pltpu.VMEM((3, BLOCKS * BLK), F32),
            pltpu.VMEM((1, BLOCKS * BLK), jnp.int32),
            pltpu.VMEM((VECS, BLOCKS * BLK), F32),
            pltpu.VMEM((BLOCKS, BLK), jnp.int32),
            pltpu.SemaphoreType.DMA((4,)),
        ],
        vmem=62,
    )(positions, kinds, krylov, order)

    other = across(packed)
    after = passed_down(packed, 1)
    second = passed_down(packed, 2)
    rows_list, _ = lax.optimization_barrier((pair_rows.reshape(1, SLOTS), packed))

    inverse, codes, counts = call(
        side_kernel,
        (
            shape((BLOCKS, BLK), jnp.int32),
            shape((1, 2 * SLOT_SPAN), jnp.int32),
            shape((2,), jnp.int32),
        ),
        [ANY, ANY, ANY, ANY],
        (VMEM, VMEM, SMEM),
        "side",
        scratch=[
            pltpu.SMEM((1, 1), jnp.int32),
            pltpu.VMEM((1, SLOTS), jnp.int32),
            pltpu.VMEM((1, SLOTS), jnp.int32),
            pltpu.VMEM((BLOCKS, BLK), jnp.int32),
            pltpu.SemaphoreType.DMA((4,)),
        ],
        vmem=62,
        cost=time_cost(2),
    )(pair_count, rows_list, pair_cols.reshape(1, SLOTS), order)

    codes, packed = lax.optimization_barrier((codes, packed))
    near_rows = [packed] + [around(packed, k) for k in (1, 2, 3)]

    features, vectors = call(
        feature_kernel,
        (shape((COLS, BLK, BLK), BF16), shape((COLS, VECS, BLK), BF16)),
        [SMEM, VMEM, VMEM, VMEM],
        (VMEM, VMEM),
        "features",
        cost=time_cost(12),
    )(type_width, packed, after, second)

    far_rows = [other] + [around(other, k) for k in (1, 2, 3)]
    step_rows, step_lanes = step_tables()
    codes, _ = lax.optimization_barrier((codes, other))
    scratch = [
        pltpu.VMEM((HALF, ROWS, BLK), BF16),
        pltpu.VMEM((HALF, 64, BLK), BF16),
        pltpu.VMEM((HALF + 1, VECS, BLK), F32),
        pltpu.VMEM((COLS + 1, VECS, BLK), F32),
        pltpu.VMEM((UNROLL, BLK, 2 * BLK), F32),
        pltpu.VMEM((UNROLL, BLK, BLK), BF16),
    ]
    block_set = (BLOCKS, VECS, BLK)
    *near_sums, col_sums = call(
        functools.partial(near_far_kernel, 0),
        [shape(block_set, F32)] + [shape(block_set, BF16)] * 3 + [shape((COLS, VECS, BLK), F32)],
        [SMEM] * 2 + [VMEM] * 8,
        [VMEM] * 5,
        "pairs_near",
        scratch=scratch,
        cost=PAIR_COST,
    )(counts, codes, *near_rows, vectors, features, step_rows, step_lanes)

    *far_sums, own_sum, after_sum, last_sum = call(
        functools.partial(near_far_kernel, 1),
        [shape(block_set, BF16)] * 4 + [shape(block_set, F32)] + [shape(block_set, BF16)] * 2,
        [SMEM] * 2 + [VMEM] * 9,
        [VMEM] * 7,
        "pairs_far",
        scratch=scratch,
        cost=PAIR_COST,
    )(counts, codes, *far_rows, vectors, features, step_rows, step_lanes, col_sums)

    far_parts = [far_sums[0]] + [around(far_sums[k], k) for k in (1, 2, 3)]
    from_prior = passed_up(after_sum, 1)
    from_second = passed_up(last_sum, 2)
    far_sum = call(
        sum_kernel, shape((BLOCKS, VECS, BLK), BF16), [VMEM] * 4, VMEM, "far_sum"
    )(*far_parts)
    from_far = across(far_sum)
    near_sums, _ = lax.optimization_barrier((near_sums, (far_sum, from_prior, from_second)))
    near_parts = [near_sums[0]] + [around(near_sums[k], k) for k in (1, 2, 3)]

    parts = [own_sum, from_far, from_prior, from_second, *near_parts]
    return call(
        final_kernel,
        shape(krylov.shape, F32),
        [SMEM] + [VMEM] * (len(parts) + 3),
        VMEM,
        "final",
        scratch=[pltpu.VMEM((BLOCKS, VECS, BLK), F32)],
    )(type_hard, *parts, kinds, krylov, inverse)


def solution(mesh):
    placed = (
        P(None, ("row", "col")),
        P(("row", "col")),
        P(None, ("row", "col")),
        P(("row", "col")),
        P(),
        P(),
        P("row", "col", None),
        P("row", "col", None),
        P("row", "col"),
    )
    return jax.shard_map(
        on_device, mesh=mesh, in_specs=placed, out_specs=P(None, ("row", "col")), check_vma=False
    )
```

```python
import functools

import jax
import jax.numpy as jnp
import ml_dtypes
import numpy as np
from jax import lax
from jax.experimental import pallas as pl
from jax.experimental.pallas import tpu as pltpu
from jax.sharding import PartitionSpec as P

BLK = 128
VECS = 16
NTYPES = 6
BLOCKS = 32
HALF = 4 * BLOCKS
COLS = 3 * BLOCKS
ROWS = VECS + 8
DEPTH = 80
UNROLL = 8
SLOTS = 512
SLOT_SPAN = SLOTS + BLK
SPARE = 3 << 22
PREP_BLOCKS = 8
CELL = (11.0, 5.0, 11.0)
BOX = (44.0, 30.0, 44.0)
SOFTENING = 0.5

ERF_COEFFS = (
    1.2732353673862733,
    0.23198340332298037,
    0.01001461653081914,
    -0.0013852189685132543,
    7.466663090475016e-05,
)


def time_cost(microseconds):
    return pl.CostEstimate(
        flops=int(microseconds * 1_000_000_000), transcendentals=0, bytes_accessed=1_000_000
    )


PAIR_COST = time_cost(16)

VMEM = pl.BlockSpec(memory_space=pltpu.VMEM)
SMEM = pl.BlockSpec(memory_space=pltpu.SMEM)
ANY = pl.BlockSpec(memory_space=pl.ANY)
Y_GROUPS = [[0, 1, 2, 3], [4, 5, 6, 7]]
F32 = jnp.float32
BF16 = jnp.bfloat16


def sublane():
    return lax.broadcasted_iota(jnp.int32, (8, BLK), 0)


def split3(value):
    high = value.astype(BF16).astype(F32)
    rest = value - high
    middle = rest.astype(BF16).astype(F32)
    return high, middle, rest - middle


def lane_gather(source, index):
    return jnp.take_along_axis(source, index, axis=1, mode="promise_in_bounds")


def here():
    return lax.axis_index("row"), lax.axis_index("col")


def prep_kernel(
    positions_hbm, type_hbm, krylov_hbm, order_hbm, packed, geometry, positions, atom_type, krylov, order, done
):
    loads = [
        pltpu.make_async_copy(source, target, done.at[k])
        for k, (source, target) in enumerate(
            (
                (krylov_hbm, krylov),
                (positions_hbm, positions),
                (type_hbm, atom_type),
                (order_hbm, order),
            )
        )
    ]
    for load in loads:
        load.start()
    place = here()
    for load in loads[1:]:
        load.wait()
    middle = BLOCKS // 2 * BLK
    geometry[0:3, :] = positions[:, 0:middle]
    geometry[3:4, :] = atom_type[:, 0:middle].astype(F32)
    geometry[4:7, :] = positions[:, middle:]
    geometry[7:8, :] = atom_type[:, middle:].astype(F32)
    level = sublane()
    corner_x = CELL[0] * place[0].astype(F32) + BOX[0] / 2
    corner_y = CELL[1] * place[1].astype(F32) + BOX[1] / 2

    def one_block(block):
        wanted = jnp.broadcast_to(order[pl.ds(block, 1), :], (8, BLK))
        chunk = wanted >> 7
        lane = wanted & 127
        folded = chunk & (BLOCKS // 2 - 1)
        top = jnp.zeros((8, BLK), F32)
        low = jnp.zeros((8, BLK), F32)
        geo = jnp.zeros((8, BLK), F32)
        for s in range(BLOCKS):
            span = slice(s * BLK, (s + 1) * BLK)
            top = jnp.where(chunk == s, lane_gather(krylov[0:8, span], lane), top)
            low = jnp.where(chunk == s, lane_gather(krylov[8:16, span], lane), low)
            if s < BLOCKS // 2:
                geo = jnp.where(folded == s, lane_gather(geometry[:, span], lane), geo)
        geo = jnp.where(chunk < BLOCKS // 2, geo, pltpu.roll(geo, 4, 0))
        corner_z = CELL[2] * block.astype(F32) + BOX[2] / 2
        corner = jnp.where(
            level == 0, corner_x, jnp.where(level == 1, corner_y, jnp.where(level == 2, corner_z, 0.0))
        )
        local = jnp.where(level < 4, geo - corner, 0.0)
        coarse = jnp.floor(local * 4.0 + 0.5) * 0.25
        fine = jnp.where(level < 3, local - coarse, local)
        coded = jnp.where(level < 3, coarse, pltpu.roll(fine, 3, 0))
        packed[block, 0:VECS, :] = jnp.concatenate([top, low], axis=0).astype(BF16)
        packed[block, VECS:ROWS, :] = coded.astype(BF16)

    def some_blocks(turn, carry):
        for extra in range(PREP_BLOCKS):
            one_block(turn * PREP_BLOCKS + extra)
        return carry

    loads[0].wait()
    lax.fori_loop(0, BLOCKS // PREP_BLOCKS, some_blocks, 0)


def side_kernel(
    count_hbm, rows_hbm, cols_hbm, order_hbm, inverse, codes, counts, count, rows, cols, order, done
):
    loads = [
        pltpu.make_async_copy(source, target, done.at[k])
        for k, (source, target) in enumerate(
            ((count_hbm, count), (rows_hbm, rows), (cols_hbm, cols), (order_hbm, order))
        )
    ]
    for load in loads:
        load.start()
    place = here()
    for load in loads:
        load.wait()
    row = rows[...]
    col = cols[...] - place[0] * BLOCKS
    step_y = place[1] - (row >> 5) + 4
    step_z = (col & 31) - (row & 31) + 2
    step = ((col >> 5) * 9 + step_y) * 5 + step_z
    diagonal = jnp.logical_and(col < BLOCKS, row == place[1] * BLOCKS + col)
    code = (row & 127) | (col << 7) | (step << 14) | (diagonal.astype(jnp.int32) << 22)
    live = lax.broadcasted_iota(jnp.int32, (1, SLOTS), 1) < count[0, 0]
    same = (row >> 7) == (place[1] >> 2)
    near = jnp.logical_and(live, same).astype(F32)
    far = jnp.logical_and(live, jnp.logical_not(same)).astype(F32)
    level = lax.broadcasted_iota(jnp.int32, (8, SLOTS), 0)
    wide = lambda v: jnp.broadcast_to(v, (8, SLOTS))
    flags = jnp.where(level == 0, wide(near), jnp.where(level == 1, wide(far), 0.0)).astype(BF16)
    earlier = (
        (lax.broadcasted_iota(jnp.int32, (SLOTS, SLOTS), 0) < lax.broadcasted_iota(jnp.int32, (SLOTS, SLOTS), 1))
        .astype(F32)
        .astype(BF16)
    )
    ranks = jnp.dot(flags, earlier, preferred_element_type=F32)
    target = jnp.where(
        near > 0.5, ranks[0:1], jnp.where(far > 0.5, ranks[1:2] + float(SLOT_SPAN), -1.0)
    ).astype(jnp.int32)
    chosen = (
        (
            lax.broadcasted_iota(jnp.int32, (2 * SLOT_SPAN, SLOTS), 0)
            == jnp.broadcast_to(target, (2 * SLOT_SPAN, SLOTS))
        )
        .astype(F32)
        .astype(BF16)
    )
    low = wide((code & 255).astype(F32))
    middle = wide(((code >> 8) & 255).astype(F32))
    high = wide((code >> 16).astype(F32))
    parts = jnp.where(level == 0, low, jnp.where(level == 1, middle, jnp.where(level == 2, high, 0.0)))
    moved = lax.dot_general(
        parts.astype(BF16), chosen, (((1,), (1,)), ((), ())), preferred_element_type=F32
    )
    listed = (moved[0:1] + moved[1:2] * 256.0 + moved[2:3] * 65536.0).astype(jnp.int32)
    near_count = jnp.sum(near).astype(jnp.int32)
    far_count = jnp.sum(far).astype(jnp.int32)
    spot = lax.broadcasted_iota(jnp.int32, (1, 2 * SLOT_SPAN), 1)
    in_near = spot < SLOT_SPAN
    used = jnp.where(in_near, spot, spot - SLOT_SPAN) < jnp.where(in_near, near_count, far_count)
    codes[...] = jnp.where(used, listed, SPARE)
    counts[0] = near_count
    counts[1] = far_count

    level_h = lax.broadcasted_iota(jnp.int32, (BLOCKS, BLK), 0)
    level_l = lax.broadcasted_iota(jnp.int32, (BLK, BLK), 0)
    lanes = lax.broadcasted_iota(jnp.int32, (BLOCKS, BLK), 1).astype(F32)
    left = []
    right = []
    for block in range(BLOCKS):
        wanted = order[block : block + 1, :]
        in_high = (level_h == jnp.broadcast_to(wanted >> 7, (BLOCKS, BLK))).astype(F32)
        in_low = (level_l == jnp.broadcast_to(wanted & 127, (BLK, BLK))).astype(F32)
        left.append(jnp.concatenate([in_high * float(block), in_high * lanes], axis=0).astype(BF16))
        right.append(in_low.astype(BF16))
    total = lax.dot_general(
        jnp.concatenate(left, axis=1),
        jnp.concatenate(right, axis=1),
        (((1,), (1,)), ((), ())),
        preferred_element_type=F32,
    )
    inverse[...] = (total[0:BLOCKS] * float(BLK) + total[BLOCKS:]).astype(jnp.int32)


def feature_kernel(type_width, own, after, second, features, vectors):
    level = sublane()
    squares = jnp.zeros((8, BLK), F32)
    for t in range(NTYPES):
        squares = jnp.where(level == t, type_width[t] * type_width[t], squares)
    low3 = level < 3
    low6 = level < 6
    zero = jnp.zeros((8, BLK), F32)
    ones3 = jnp.where(low3, 1.0, 0.0)

    for part, source in enumerate((own, after, second)):

        def one_block(block, part=part, source=source):
            vectors[part * BLOCKS + block] = source[block, 0:VECS, :]
            coded = source[block, VECS:ROWS, :].astype(F32)
            near = coded + pltpu.roll(coded, 5, 0)
            square = near * near
            weight = square[0:1] + square[1:2] + square[2:3] + SOFTENING * SOFTENING
            weight_h, weight_m, weight_l = split3(weight)
            coarse = jnp.where(low3, coded, pltpu.roll(coded, 3, 0)) * -2.0
            fine = jnp.where(low3, pltpu.roll(coded, 5, 0), coded) * -2.0
            own_type = jnp.broadcast_to(coded[6:7], (8, BLK))
            own_square = jnp.zeros((8, BLK), F32)
            for t in range(NTYPES):
                own_square = jnp.where(own_type == float(t), type_width[t] * type_width[t], own_square)
            scale = 1.0 / (own_square + squares)
            scale_h, scale_m, scale_l = split3(jnp.where(low6, scale, 0.0))
            wide = lambda v: jnp.broadcast_to(v, (8, BLK))
            weights = jnp.where(
                level == 0,
                wide(weight_h),
                jnp.where(level == 1, wide(weight_m), jnp.where(level == 2, wide(weight_l), 0.0)),
            )
            stacked = jnp.concatenate(
                [
                    jnp.where(low6, coarse, 0.0),
                    jnp.where(low6, fine, 0.0),
                    jnp.where(low6, coded, 1.0),
                    weights,
                    ones3,
                    zero,
                    scale_h,
                    scale_m,
                    scale_l,
                ]
                + [zero] * 7,
                axis=0,
            )
            features[part * BLOCKS + block] = stacked.astype(BF16).T

        def some_blocks(turn, carry, one_block=one_block):
            for extra in range(16):
                one_block(turn * 16 + extra)
            return carry

        lax.fori_loop(0, BLOCKS // 16, some_blocks, 0)


def row_operands(row_data, operands):
    level = sublane()
    zero = jnp.zeros((8, BLK), F32)

    def some_rows(turn, carry):
        for extra in range(16):
            row = turn * 16 + extra
            coded = row_data[row, VECS:ROWS, :].astype(F32)
            near = coded + pltpu.roll(coded, 5, 0)
            square = near * near
            weight_h, weight_m, weight_l = split3(square[0:1] + square[1:2] + square[2:3])
            wide = lambda v: jnp.broadcast_to(v, (8, BLK))
            weights = jnp.where(
                level == 0,
                wide(weight_h),
                jnp.where(level == 1, wide(weight_m), jnp.where(level == 2, wide(weight_l), 0.0)),
            )
            hot = (level.astype(F32) == wide(coded[6:7])).astype(F32)
            operands[row] = jnp.concatenate(
                [coded, coded, weights, zero, hot, hot, hot, zero], axis=0
            ).astype(BF16)
        return carry

    lax.fori_loop(0, HALF // 16, some_rows, 0)


def pair_products(code, operands, features, step_rows, step_lanes):
    step = (code >> 14) & 255
    right = operands[code & 127]
    empty = jnp.zeros((48, BLK), BF16)
    left = features[(code >> 7) & 127].reshape(8, 16, BLK) + step_lanes[step][None]
    both = jnp.concatenate(
        [
            jnp.concatenate([right[0:16], step_rows[step], right[16:32], empty[0:32]], axis=0),
            jnp.concatenate([empty, right[32:64]], axis=0),
        ],
        axis=1,
    )
    return jnp.dot(left.reshape(BLK, BLK)[:, 0:DEPTH], both, preferred_element_type=F32)


def tile_values(distance2, inverse_spread):
    square = distance2 * inverse_spread
    poly = ERF_COEFFS[-1]
    for coefficient in ERF_COEFFS[-2::-1]:
        poly = poly * square + coefficient
    poly = poly * square
    return (jnp.tanh(poly * lax.rsqrt(poly)) * lax.rsqrt(distance2)).astype(BF16)


def pair_loop(
    phase, counts, codes, row_data, operands, vectors, features, step_rows, step_lanes, row_acc, col_acc, waiting, tiles
):
    base = phase * SLOT_SPAN
    batches = (counts[phase] + UNROLL - 1) // UNROLL

    def one_turn(turn, carry):
        adding = base + jnp.maximum(turn - 2, 0) * UNROLL
        opening = base + jnp.maximum(jnp.minimum(turn, batches - 1), 0) * UNROLL
        sums = []
        for first in range(0, UNROLL, 2):
            done = [codes[0, adding + first + k] for k in range(2)]
            both = [tiles[first + k] for k in range(2)]
            forward = jnp.dot(
                jnp.concatenate([vectors[(code >> 7) & 127] for code in done], axis=0),
                jnp.concatenate(both, axis=1),
                preferred_element_type=F32,
            )
            backward = lax.dot_general(
                jnp.concatenate([row_data[code & 127, 0:VECS, :] for code in done], axis=0),
                jnp.concatenate(both, axis=0),
                (((1,), (1,)), ((), ())),
                preferred_element_type=F32,
            )
            for k, code in enumerate(done):
                to_row = jnp.where(jnp.logical_or(turn < 2, ((code >> 23) & 1) == 1), HALF, code & 127)
                to_col = jnp.where(
                    jnp.logical_or(turn < 2, ((code >> 22) & 1) == 1), COLS, (code >> 7) & 127
                )
                own = (slice(k * VECS, (k + 1) * VECS), slice(k * BLK, (k + 1) * BLK))
                sums.append((to_row, forward[own], to_col, backward[own]))
            for k in range(2):
                slot = first + k
                tiles[slot] = tile_values(waiting[slot, :, 0:BLK], waiting[slot, :, BLK:])
                code = codes[0, opening + slot]
                waiting[slot] = pair_products(code, operands, features, step_rows, step_lanes)
        for to_row, forward, to_col, backward in sums:
            row_acc[to_row] += forward
            col_acc[to_col] += backward
        return carry

    lax.fori_loop(0, batches + 2, one_turn, 0)


def near_far_kernel(phase, *refs):
    counts, codes = refs[0:2]
    pieces = refs[2:6]
    vectors, features, step_rows, step_lanes = refs[6:10]
    col_in = refs[10:11] if phase == 1 else ()
    outs = refs[10 + len(col_in) : -6]
    row_data, operands, row_acc, col_acc, waiting, tiles = refs[-6:]
    position = here()[1] & 3
    for k, piece in enumerate(pieces):
        start = pl.multiple_of(((position - k) & 3) * BLOCKS, BLOCKS)
        row_data[pl.ds(start, BLOCKS)] = piece[...]
    row_operands(row_data, operands)
    row_acc[...] = jnp.zeros_like(row_acc)
    if phase == 0:
        col_acc[...] = jnp.zeros_like(col_acc)
    else:
        col_acc[0:COLS] = col_in[0][...]
    pair_loop(
        phase,
        counts,
        codes,
        row_data,
        operands,
        vectors,
        features,
        step_rows,
        step_lanes,
        row_acc,
        col_acc,
        waiting,
        tiles,
    )
    for k in range(4):
        start = pl.multiple_of(((position + k) & 3) * BLOCKS, BLOCKS)
        outs[k][...] = row_acc[pl.ds(start, BLOCKS)].astype(outs[k].dtype)
    if phase == 0:
        outs[4][...] = col_acc[0:COLS]
    else:
        for step in range(3):
            outs[4 + step][...] = col_acc[step * BLOCKS : (step + 1) * BLOCKS].astype(outs[4 + step].dtype)


def sum_kernel(*refs):
    total = refs[0][...].astype(F32)
    for ref in refs[1:-1]:
        total = total + ref[...].astype(F32)
    refs[-1][...] = total.astype(refs[-1].dtype)


def final_kernel(type_hard, *refs):
    atom_type, krylov, inverse, out_hbm, blocked, out, done = refs[-7:]
    parts = refs[:-7]

    def add_up(turn, carry):
        for extra in range(8):
            block = turn * 8 + extra
            total = parts[0][block]
            for part in parts[1:]:
                total = total + part[block].astype(F32)
            blocked[block] = total
        return carry

    lax.fori_loop(0, BLOCKS // 8, add_up, 0)
    saves = []
    for chunk in range(BLOCKS):
        wanted = jnp.broadcast_to(inverse[chunk : chunk + 1, :], (8, BLK))
        source = wanted >> 7
        lane = wanted & 127
        span = slice(chunk * BLK, (chunk + 1) * BLK)
        kind = jnp.broadcast_to(atom_type[:, span], (8, BLK))
        hard = jnp.zeros((8, BLK), F32)
        for t in range(NTYPES):
            hard = jnp.where(kind == t, type_hard[t], hard)
        top = jnp.zeros((8, BLK), F32)
        low = jnp.zeros((8, BLK), F32)
        for block in range(BLOCKS):
            top = jnp.where(source == block, lane_gather(blocked[block, 0:8, :], lane), top)
            low = jnp.where(source == block, lane_gather(blocked[block, 8:16, :], lane), low)
        out[0:8, span] = top + hard * krylov[0:8, span]
        out[8:16, span] = low + hard * krylov[8:16, span]
        if chunk % 8 == 7:
            group = slice((chunk - 7) * BLK, (chunk + 1) * BLK)
            save = pltpu.make_async_copy(out.at[:, group], out_hbm.at[:, group], done.at[chunk // 8])
            save.start()
            saves.append(save)
    for save in saves:
        save.wait()


def shape(dims, dtype):
    return jax.ShapeDtypeStruct(dims, dtype)


def call(kernel, out_shape, in_specs, out_specs, name, scratch=(), vmem=20, cost=None):
    return pl.pallas_call(
        kernel,
        out_shape=out_shape,
        in_specs=in_specs,
        out_specs=out_specs,
        scratch_shapes=list(scratch),
        compiler_params=pltpu.CompilerParams(vmem_limit_bytes=vmem << 20),
        cost_estimate=cost,
        name=name,
    )


def step_tables():
    x, y, z = np.meshgrid(np.arange(3), np.arange(-4, 5), np.arange(-2, 3), indexing="ij")
    steps = np.stack([x, y, z], axis=-1).reshape(-1, 3) * np.array(CELL)
    squared = np.sum(steps * steps, axis=1).astype(np.float32)
    coarse = squared.astype(ml_dtypes.bfloat16).astype(np.float32)
    rows = np.zeros((len(steps), 16, BLK), np.float32)
    rows[:, 0:3] = rows[:, 3:6] = 2.0 * steps[:, :, None]
    rows[:, 6] = coarse[:, None]
    rows[:, 7] = (squared - coarse)[:, None]
    rows[:, 8:11] = 1.0
    lanes = np.zeros((len(steps), 16, BLK), np.float32)
    lanes[:, :, 0:3] = lanes[:, :, 3:6] = -2.0 * steps[:, None, :]
    return rows.astype(ml_dtypes.bfloat16), lanes.astype(ml_dtypes.bfloat16)


def passed_down(value, steps):
    count = lax.axis_size("row")
    return lax.ppermute(value, "row", [(s, s - steps) for s in range(steps, count)])


def passed_up(value, steps):
    count = lax.axis_size("row")
    return lax.ppermute(value, "row", [(s, s + steps) for s in range(count - steps)])


def across(value):
    return lax.ppermute(value, "col", [(c, c ^ 4) for c in range(8)])


def around(value, steps):
    return lax.ppermute(value, "col", [(c, (c & 4) + (c + steps) % 4) for c in range(8)])


def on_device(
    positions, atom_type, krylov, block_order, type_width, type_hard, pair_rows, pair_cols, pair_count
):
    order = block_order.reshape(BLOCKS, BLK)
    kinds = atom_type.reshape(1, -1)

    packed = call(
        prep_kernel,
        shape((BLOCKS, ROWS, BLK), BF16),
        [ANY, ANY, ANY, ANY],
        VMEM,
        "prep",
        scratch=[
            pltpu.VMEM((8, BLOCKS // 2 * BLK), F32),
            pltpu.VMEM((3, BLOCKS * BLK), F32),
            pltpu.VMEM((1, BLOCKS * BLK), jnp.int32),
            pltpu.VMEM((VECS, BLOCKS * BLK), F32),
            pltpu.VMEM((BLOCKS, BLK), jnp.int32),
            pltpu.SemaphoreType.DMA((4,)),
        ],
        vmem=62,
    )(positions, kinds, krylov, order)

    other = across(packed)
    after = passed_down(packed, 1)
    second = passed_down(packed, 2)
    rows_list, _ = lax.optimization_barrier((pair_rows.reshape(1, SLOTS), packed))

    inverse, codes, counts = call(
        side_kernel,
        (
            shape((BLOCKS, BLK), jnp.int32),
            shape((1, 2 * SLOT_SPAN), jnp.int32),
            shape((2,), jnp.int32),
        ),
        [ANY, ANY, ANY, ANY],
        (VMEM, VMEM, SMEM),
        "side",
        scratch=[
            pltpu.SMEM((1, 1), jnp.int32),
            pltpu.VMEM((1, SLOTS), jnp.int32),
            pltpu.VMEM((1, SLOTS), jnp.int32),
            pltpu.VMEM((BLOCKS, BLK), jnp.int32),
            pltpu.SemaphoreType.DMA((4,)),
        ],
        vmem=62,
        cost=time_cost(2),
    )(pair_count, rows_list, pair_cols.reshape(1, SLOTS), order)

    near_rows = [packed] + [around(packed, k) for k in (1, 2, 3)]

    features, vectors = call(
        feature_kernel,
        (shape((COLS, BLK, BLK), BF16), shape((COLS, VECS, BLK), BF16)),
        [SMEM, VMEM, VMEM, VMEM],
        (VMEM, VMEM),
        "features",
        cost=time_cost(12),
    )(type_width, packed, after, second)

    far_rows = [other] + [around(other, k) for k in (1, 2, 3)]
    step_rows, step_lanes = step_tables()
    codes, _ = lax.optimization_barrier((codes, other))
    scratch = [
        pltpu.VMEM((HALF, ROWS, BLK), BF16),
        pltpu.VMEM((HALF, 64, BLK), BF16),
        pltpu.VMEM((HALF + 1, VECS, BLK), F32),
        pltpu.VMEM((COLS + 1, VECS, BLK), F32),
        pltpu.VMEM((UNROLL, BLK, 2 * BLK), F32),
        pltpu.VMEM((UNROLL, BLK, BLK), BF16),
    ]
    block_set = (BLOCKS, VECS, BLK)
    *near_sums, col_sums = call(
        functools.partial(near_far_kernel, 0),
        [shape(block_set, F32)] + [shape(block_set, BF16)] * 3 + [shape((COLS, VECS, BLK), F32)],
        [SMEM] * 2 + [VMEM] * 8,
        [VMEM] * 5,
        "pairs_near",
        scratch=scratch,
        cost=PAIR_COST,
    )(counts, codes, *near_rows, vectors, features, step_rows, step_lanes)

    *far_sums, own_sum, after_sum, last_sum = call(
        functools.partial(near_far_kernel, 1),
        [shape(block_set, BF16)] * 4 + [shape(block_set, F32)] + [shape(block_set, BF16)] * 2,
        [SMEM] * 2 + [VMEM] * 9,
        [VMEM] * 7,
        "pairs_far",
        scratch=scratch,
        cost=PAIR_COST,
    )(counts, codes, *far_rows, vectors, features, step_rows, step_lanes, col_sums)

    far_parts = [far_sums[0]] + [around(far_sums[k], k) for k in (1, 2, 3)]
    from_prior = passed_up(after_sum, 1)
    from_second = passed_up(last_sum, 2)
    far_sum = call(
        sum_kernel, shape((BLOCKS, VECS, BLK), BF16), [VMEM] * 4, VMEM, "far_sum"
    )(*far_parts)
    from_far = across(far_sum)
    near_sums, _ = lax.optimization_barrier((near_sums, (far_sum, from_prior, from_second)))
    near_parts = [near_sums[0]] + [around(near_sums[k], k) for k in (1, 2, 3)]

    parts = [own_sum, from_far, from_prior, from_second, *near_parts]
    return call(
        final_kernel,
        shape(krylov.shape, F32),
        [SMEM] + [VMEM] * (len(parts) + 3),
        ANY,
        "final",
        scratch=[
            pltpu.VMEM((BLOCKS, VECS, BLK), F32),
            pltpu.VMEM((VECS, BLOCKS * BLK), F32),
            pltpu.SemaphoreType.DMA((4,)),
        ],
    )(type_hard, *parts, kinds, krylov, inverse)


def solution(mesh):
    placed = (
        P(None, ("row", "col")),
        P(("row", "col")),
        P(None, ("row", "col")),
        P(("row", "col")),
        P(),
        P(),
        P("row", "col", None),
        P("row", "col", None),
        P("row", "col"),
    )
    return jax.shard_map(
        on_device, mesh=mesh, in_specs=placed, out_specs=P(None, ("row", "col")), check_vma=False
    )
```

```python
import functools

import jax
import jax.numpy as jnp
import ml_dtypes
import numpy as np
from jax import lax
from jax.experimental import pallas as pl
from jax.experimental.pallas import tpu as pltpu
from jax.sharding import PartitionSpec as P

BLK = 128
VECS = 16
NTYPES = 6
BLOCKS = 32
HALF = 4 * BLOCKS
COLS = 3 * BLOCKS
ROWS = VECS + 8
DEPTH = 80
UNROLL = 8
SLOTS = 512
SLOT_SPAN = SLOTS + BLK
SPARE = 3 << 22
PREP_BLOCKS = 8
CELL = (11.0, 5.0, 11.0)
BOX = (44.0, 30.0, 44.0)
SOFTENING = 0.5

ERF_COEFFS = (
    1.2732353673862733,
    0.23198340332298037,
    0.01001461653081914,
    -0.0013852189685132543,
    7.466663090475016e-05,
)


def time_cost(microseconds):
    return pl.CostEstimate(
        flops=int(microseconds * 1_000_000_000), transcendentals=0, bytes_accessed=1_000_000
    )


PAIR_COST = time_cost(16)

VMEM = pl.BlockSpec(memory_space=pltpu.VMEM)
SMEM = pl.BlockSpec(memory_space=pltpu.SMEM)
ANY = pl.BlockSpec(memory_space=pl.ANY)
Y_GROUPS = [[0, 1, 2, 3], [4, 5, 6, 7]]
F32 = jnp.float32
BF16 = jnp.bfloat16


def sublane():
    return lax.broadcasted_iota(jnp.int32, (8, BLK), 0)


def split3(value):
    high = value.astype(BF16).astype(F32)
    rest = value - high
    middle = rest.astype(BF16).astype(F32)
    return high, middle, rest - middle


def lane_gather(source, index):
    return jnp.take_along_axis(source, index, axis=1, mode="promise_in_bounds")


def here():
    return lax.axis_index("row"), lax.axis_index("col")


def prep_kernel(
    positions_hbm, type_hbm, krylov_hbm, order_hbm, packed, geometry, positions, atom_type, krylov, order, done
):
    loads = [
        pltpu.make_async_copy(source, target, done.at[k])
        for k, (source, target) in enumerate(
            (
                (krylov_hbm, krylov),
                (positions_hbm, positions),
                (type_hbm, atom_type),
                (order_hbm, order),
            )
        )
    ]
    for load in loads:
        load.start()
    place = here()
    for load in loads[1:]:
        load.wait()
    middle = BLOCKS // 2 * BLK
    geometry[0:3, :] = positions[:, 0:middle]
    geometry[3:4, :] = atom_type[:, 0:middle].astype(F32)
    geometry[4:7, :] = positions[:, middle:]
    geometry[7:8, :] = atom_type[:, middle:].astype(F32)
    level = sublane()
    corner_x = CELL[0] * place[0].astype(F32) + BOX[0] / 2
    corner_y = CELL[1] * place[1].astype(F32) + BOX[1] / 2

    def one_block(block):
        wanted = jnp.broadcast_to(order[pl.ds(block, 1), :], (8, BLK))
        chunk = wanted >> 7
        lane = wanted & 127
        folded = chunk & (BLOCKS // 2 - 1)
        top = jnp.zeros((8, BLK), F32)
        low = jnp.zeros((8, BLK), F32)
        geo = jnp.zeros((8, BLK), F32)
        for s in range(BLOCKS):
            span = slice(s * BLK, (s + 1) * BLK)
            top = jnp.where(chunk == s, lane_gather(krylov[0:8, span], lane), top)
            low = jnp.where(chunk == s, lane_gather(krylov[8:16, span], lane), low)
            if s < BLOCKS // 2:
                geo = jnp.where(folded == s, lane_gather(geometry[:, span], lane), geo)
        geo = jnp.where(chunk < BLOCKS // 2, geo, pltpu.roll(geo, 4, 0))
        corner_z = CELL[2] * block.astype(F32) + BOX[2] / 2
        corner = jnp.where(
            level == 0, corner_x, jnp.where(level == 1, corner_y, jnp.where(level == 2, corner_z, 0.0))
        )
        local = jnp.where(level < 4, geo - corner, 0.0)
        coarse = jnp.floor(local * 4.0 + 0.5) * 0.25
        fine = jnp.where(level < 3, local - coarse, local)
        coded = jnp.where(level < 3, coarse, pltpu.roll(fine, 3, 0))
        packed[block, 0:VECS, :] = jnp.concatenate([top, low], axis=0).astype(BF16)
        packed[block, VECS:ROWS, :] = coded.astype(BF16)

    def some_blocks(turn, carry):
        for extra in range(PREP_BLOCKS):
            one_block(turn * PREP_BLOCKS + extra)
        return carry

    loads[0].wait()
    lax.fori_loop(0, BLOCKS // PREP_BLOCKS, some_blocks, 0)


def side_kernel(
    count_hbm, rows_hbm, cols_hbm, order_hbm, inverse, codes, counts, count, rows, cols, order, done
):
    loads = [
        pltpu.make_async_copy(source, target, done.at[k])
        for k, (source, target) in enumerate(
            ((count_hbm, count), (rows_hbm, rows), (cols_hbm, cols), (order_hbm, order))
        )
    ]
    for load in loads:
        load.start()
    place = here()
    for load in loads:
        load.wait()
    row = rows[...]
    col = cols[...] - place[0] * BLOCKS
    step_y = place[1] - (row >> 5) + 4
    step_z = (col & 31) - (row & 31) + 2
    step = ((col >> 5) * 9 + step_y) * 5 + step_z
    diagonal = jnp.logical_and(col < BLOCKS, row == place[1] * BLOCKS + col)
    code = (row & 127) | (col << 7) | (step << 14) | (diagonal.astype(jnp.int32) << 22)
    live = lax.broadcasted_iota(jnp.int32, (1, SLOTS), 1) < count[0, 0]
    same = (row >> 7) == (place[1] >> 2)
    near = jnp.logical_and(live, same).astype(F32)
    far = jnp.logical_and(live, jnp.logical_not(same)).astype(F32)
    level = lax.broadcasted_iota(jnp.int32, (8, SLOTS), 0)
    wide = lambda v: jnp.broadcast_to(v, (8, SLOTS))
    flags = jnp.where(level == 0, wide(near), jnp.where(level == 1, wide(far), 0.0)).astype(BF16)
    earlier = (
        (lax.broadcasted_iota(jnp.int32, (SLOTS, SLOTS), 0) < lax.broadcasted_iota(jnp.int32, (SLOTS, SLOTS), 1))
        .astype(F32)
        .astype(BF16)
    )
    ranks = jnp.dot(flags, earlier, preferred_element_type=F32)
    target = jnp.where(
        near > 0.5, ranks[0:1], jnp.where(far > 0.5, ranks[1:2] + float(SLOT_SPAN), -1.0)
    ).astype(jnp.int32)
    chosen = (
        (
            lax.broadcasted_iota(jnp.int32, (2 * SLOT_SPAN, SLOTS), 0)
            == jnp.broadcast_to(target, (2 * SLOT_SPAN, SLOTS))
        )
        .astype(F32)
        .astype(BF16)
    )
    low = wide((code & 255).astype(F32))
    middle = wide(((code >> 8) & 255).astype(F32))
    high = wide((code >> 16).astype(F32))
    parts = jnp.where(level == 0, low, jnp.where(level == 1, middle, jnp.where(level == 2, high, 0.0)))
    moved = lax.dot_general(
        parts.astype(BF16), chosen, (((1,), (1,)), ((), ())), preferred_element_type=F32
    )
    listed = (moved[0:1] + moved[1:2] * 256.0 + moved[2:3] * 65536.0).astype(jnp.int32)
    near_count = jnp.sum(near).astype(jnp.int32)
    far_count = jnp.sum(far).astype(jnp.int32)
    spot = lax.broadcasted_iota(jnp.int32, (1, 2 * SLOT_SPAN), 1)
    in_near = spot < SLOT_SPAN
    used = jnp.where(in_near, spot, spot - SLOT_SPAN) < jnp.where(in_near, near_count, far_count)
    codes[...] = jnp.where(used, listed, SPARE)
    counts[0] = near_count
    counts[1] = far_count

    level_h = lax.broadcasted_iota(jnp.int32, (BLOCKS, BLK), 0)
    level_l = lax.broadcasted_iota(jnp.int32, (BLK, BLK), 0)
    lanes = lax.broadcasted_iota(jnp.int32, (BLOCKS, BLK), 1).astype(F32)
    left = []
    right = []
    for block in range(BLOCKS):
        wanted = order[block : block + 1, :]
        in_high = (level_h == jnp.broadcast_to(wanted >> 7, (BLOCKS, BLK))).astype(F32)
        in_low = (level_l == jnp.broadcast_to(wanted & 127, (BLK, BLK))).astype(F32)
        left.append(jnp.concatenate([in_high * float(block), in_high * lanes], axis=0).astype(BF16))
        right.append(in_low.astype(BF16))
    total = lax.dot_general(
        jnp.concatenate(left, axis=1),
        jnp.concatenate(right, axis=1),
        (((1,), (1,)), ((), ())),
        preferred_element_type=F32,
    )
    inverse[...] = (total[0:BLOCKS] * float(BLK) + total[BLOCKS:]).astype(jnp.int32)


def feature_kernel(type_width, own, after, second, features, vectors):
    level = sublane()
    squares = jnp.zeros((8, BLK), F32)
    for t in range(NTYPES):
        squares = jnp.where(level == t, type_width[t] * type_width[t], squares)
    low3 = level < 3
    low6 = level < 6
    zero = jnp.zeros((8, BLK), F32)
    ones3 = jnp.where(low3, 1.0, 0.0)

    for part, source in enumerate((own, after, second)):

        def one_block(block, part=part, source=source):
            vectors[part * BLOCKS + block] = source[block, 0:VECS, :]
            coded = source[block, VECS:ROWS, :].astype(F32)
            near = coded + pltpu.roll(coded, 5, 0)
            square = near * near
            weight = square[0:1] + square[1:2] + square[2:3] + SOFTENING * SOFTENING
            weight_h, weight_m, weight_l = split3(weight)
            coarse = jnp.where(low3, coded, pltpu.roll(coded, 3, 0)) * -2.0
            fine = jnp.where(low3, pltpu.roll(coded, 5, 0), coded) * -2.0
            own_type = jnp.broadcast_to(coded[6:7], (8, BLK))
            own_square = jnp.zeros((8, BLK), F32)
            for t in range(NTYPES):
                own_square = jnp.where(own_type == float(t), type_width[t] * type_width[t], own_square)
            scale = 1.0 / (own_square + squares)
            scale_h, scale_m, scale_l = split3(jnp.where(low6, scale, 0.0))
            wide = lambda v: jnp.broadcast_to(v, (8, BLK))
            weights = jnp.where(
                level == 0,
                wide(weight_h),
                jnp.where(level == 1, wide(weight_m), jnp.where(level == 2, wide(weight_l), 0.0)),
            )
            stacked = jnp.concatenate(
                [
                    jnp.where(low6, coarse, 0.0),
                    jnp.where(low6, fine, 0.0),
                    jnp.where(low6, coded, 1.0),
                    weights,
                    ones3,
                    zero,
                    scale_h,
                    scale_m,
                    scale_l,
                ]
                + [zero] * 7,
                axis=0,
            )
            features[part * BLOCKS + block] = stacked.astype(BF16).T

        def some_blocks(turn, carry, one_block=one_block):
            for extra in range(16):
                one_block(turn * 16 + extra)
            return carry

        lax.fori_loop(0, BLOCKS // 16, some_blocks, 0)


def row_operands(row_data, operands):
    level = sublane()
    zero = jnp.zeros((8, BLK), F32)

    def some_rows(turn, carry):
        for extra in range(16):
            row = turn * 16 + extra
            coded = row_data[row, VECS:ROWS, :].astype(F32)
            near = coded + pltpu.roll(coded, 5, 0)
            square = near * near
            weight_h, weight_m, weight_l = split3(square[0:1] + square[1:2] + square[2:3])
            wide = lambda v: jnp.broadcast_to(v, (8, BLK))
            weights = jnp.where(
                level == 0,
                wide(weight_h),
                jnp.where(level == 1, wide(weight_m), jnp.where(level == 2, wide(weight_l), 0.0)),
            )
            hot = (level.astype(F32) == wide(coded[6:7])).astype(F32)
            operands[row] = jnp.concatenate(
                [coded, coded, weights, zero, hot, hot, hot, zero], axis=0
            ).astype(BF16)
        return carry

    lax.fori_loop(0, HALF // 16, some_rows, 0)


def pair_products(code, operands, features, step_rows, step_lanes):
    step = (code >> 14) & 255
    right = operands[code & 127]
    empty = jnp.zeros((48, BLK), BF16)
    left = features[(code >> 7) & 127].reshape(8, 16, BLK) + step_lanes[step][None]
    both = jnp.concatenate(
        [
            jnp.concatenate([right[0:16], step_rows[step], right[16:32], empty[0:32]], axis=0),
            jnp.concatenate([empty, right[32:64]], axis=0),
        ],
        axis=1,
    )
    return jnp.dot(left.reshape(BLK, BLK)[:, 0:DEPTH], both, preferred_element_type=F32)


def tile_values(distance2, inverse_spread):
    square = distance2 * inverse_spread
    poly = ERF_COEFFS[-1]
    for coefficient in ERF_COEFFS[-2::-1]:
        poly = poly * square + coefficient
    poly = poly * square
    return (jnp.tanh(poly * lax.rsqrt(poly)) * lax.rsqrt(distance2)).astype(BF16)


def pair_loop(
    phase, counts, codes, row_data, operands, vectors, features, step_rows, step_lanes, row_acc, col_acc, waiting, tiles
):
    base = phase * SLOT_SPAN
    batches = (counts[phase] + UNROLL - 1) // UNROLL

    def one_turn(turn, carry):
        adding = base + jnp.maximum(turn - 2, 0) * UNROLL
        opening = base + jnp.maximum(jnp.minimum(turn, batches - 1), 0) * UNROLL
        sums = []
        for first in range(0, UNROLL, 2):
            done = [codes[0, adding + first + k] for k in range(2)]
            both = [tiles[first + k] for k in range(2)]
            forward = jnp.dot(
                jnp.concatenate([vectors[(code >> 7) & 127] for code in done], axis=0),
                jnp.concatenate(both, axis=1),
                preferred_element_type=F32,
            )
            backward = lax.dot_general(
                jnp.concatenate([row_data[code & 127, 0:VECS, :] for code in done], axis=0),
                jnp.concatenate(both, axis=0),
                (((1,), (1,)), ((), ())),
                preferred_element_type=F32,
            )
            for k, code in enumerate(done):
                to_row = jnp.where(jnp.logical_or(turn < 2, ((code >> 23) & 1) == 1), HALF, code & 127)
                to_col = jnp.where(
                    jnp.logical_or(turn < 2, ((code >> 22) & 1) == 1), COLS, (code >> 7) & 127
                )
                own = (slice(k * VECS, (k + 1) * VECS), slice(k * BLK, (k + 1) * BLK))
                sums.append((to_row, forward[own], to_col, backward[own]))
            for k in range(2):
                slot = first + k
                tiles[slot] = tile_values(waiting[slot, :, 0:BLK], waiting[slot, :, BLK:])
                code = codes[0, opening + slot]
                waiting[slot] = pair_products(code, operands, features, step_rows, step_lanes)
        for to_row, forward, to_col, backward in sums:
            row_acc[to_row] += forward
            col_acc[to_col] += backward
        return carry

    lax.fori_loop(0, batches + 2, one_turn, 0)


def near_far_kernel(phase, *refs):
    counts, codes = refs[0:2]
    pieces = refs[2:6]
    vectors, features, step_rows, step_lanes = refs[6:10]
    col_in = refs[10:11] if phase == 1 else ()
    outs = refs[10 + len(col_in) : -6]
    row_data, operands, row_acc, col_acc, waiting, tiles = refs[-6:]
    position = here()[1] & 3
    for k, piece in enumerate(pieces):
        start = pl.multiple_of(((position - k) & 3) * BLOCKS, BLOCKS)
        row_data[pl.ds(start, BLOCKS)] = piece[...]
    row_operands(row_data, operands)
    row_acc[...] = jnp.zeros_like(row_acc)
    if phase == 0:
        col_acc[...] = jnp.zeros_like(col_acc)
    else:
        col_acc[0:COLS] = col_in[0][...]
    pair_loop(
        phase,
        counts,
        codes,
        row_data,
        operands,
        vectors,
        features,
        step_rows,
        step_lanes,
        row_acc,
        col_acc,
        waiting,
        tiles,
    )
    for k in range(4):
        start = pl.multiple_of(((position + k) & 3) * BLOCKS, BLOCKS)
        outs[k][...] = row_acc[pl.ds(start, BLOCKS)].astype(outs[k].dtype)
    if phase == 0:
        outs[4][...] = col_acc[0:COLS]
    else:
        for step in range(3):
            outs[4 + step][...] = col_acc[step * BLOCKS : (step + 1) * BLOCKS].astype(outs[4 + step].dtype)


def sum_kernel(*refs):
    total = refs[0][...].astype(F32)
    for ref in refs[1:-1]:
        total = total + ref[...].astype(F32)
    refs[-1][...] = total.astype(refs[-1].dtype)


def final_kernel(type_hard, *refs):
    atom_type, krylov, inverse, out_hbm, blocked, out, done = refs[-7:]
    parts = refs[:-7]

    def add_up(turn, carry):
        for extra in range(8):
            block = turn * 8 + extra
            total = parts[0][block]
            for part in parts[1:]:
                total = total + part[block].astype(F32)
            blocked[block] = total
        return carry

    lax.fori_loop(0, BLOCKS // 8, add_up, 0)
    saves = []
    for chunk in range(BLOCKS):
        wanted = jnp.broadcast_to(inverse[chunk : chunk + 1, :], (8, BLK))
        source = wanted >> 7
        lane = wanted & 127
        span = slice(chunk * BLK, (chunk + 1) * BLK)
        kind = jnp.broadcast_to(atom_type[:, span], (8, BLK))
        hard = jnp.zeros((8, BLK), F32)
        for t in range(NTYPES):
            hard = jnp.where(kind == t, type_hard[t], hard)
        top = jnp.zeros((8, BLK), F32)
        low = jnp.zeros((8, BLK), F32)
        for block in range(BLOCKS):
            top = jnp.where(source == block, lane_gather(blocked[block, 0:8, :], lane), top)
            low = jnp.where(source == block, lane_gather(blocked[block, 8:16, :], lane), low)
        out[0:8, span] = top + hard * krylov[0:8, span]
        out[8:16, span] = low + hard * krylov[8:16, span]
        if chunk % 8 == 7:
            group = slice((chunk - 7) * BLK, (chunk + 1) * BLK)
            save = pltpu.make_async_copy(out.at[:, group], out_hbm.at[:, group], done.at[chunk // 8])
            save.start()
            saves.append(save)
    for save in saves:
        save.wait()


def shape(dims, dtype):
    return jax.ShapeDtypeStruct(dims, dtype)


def call(kernel, out_shape, in_specs, out_specs, name, scratch=(), vmem=20, cost=None):
    return pl.pallas_call(
        kernel,
        out_shape=out_shape,
        in_specs=in_specs,
        out_specs=out_specs,
        scratch_shapes=list(scratch),
        compiler_params=pltpu.CompilerParams(vmem_limit_bytes=vmem << 20),
        cost_estimate=cost,
        name=name,
    )


def step_tables():
    x, y, z = np.meshgrid(np.arange(3), np.arange(-4, 5), np.arange(-2, 3), indexing="ij")
    steps = np.stack([x, y, z], axis=-1).reshape(-1, 3) * np.array(CELL)
    squared = np.sum(steps * steps, axis=1).astype(np.float32)
    coarse = squared.astype(ml_dtypes.bfloat16).astype(np.float32)
    rows = np.zeros((len(steps), 16, BLK), np.float32)
    rows[:, 0:3] = rows[:, 3:6] = 2.0 * steps[:, :, None]
    rows[:, 6] = coarse[:, None]
    rows[:, 7] = (squared - coarse)[:, None]
    rows[:, 8:11] = 1.0
    lanes = np.zeros((len(steps), 16, BLK), np.float32)
    lanes[:, :, 0:3] = lanes[:, :, 3:6] = -2.0 * steps[:, None, :]
    return rows.astype(ml_dtypes.bfloat16), lanes.astype(ml_dtypes.bfloat16)


def passed_down(value, steps):
    count = lax.axis_size("row")
    return lax.ppermute(value, "row", [(s, s - steps) for s in range(steps, count)])


def passed_up(value, steps):
    count = lax.axis_size("row")
    return lax.ppermute(value, "row", [(s, s + steps) for s in range(count - steps)])


def across(value):
    return lax.ppermute(value, "col", [(c, c ^ 4) for c in range(8)])


def around(value, steps):
    return lax.ppermute(value, "col", [(c, (c & 4) + (c + steps) % 4) for c in range(8)])


def on_device(
    positions, atom_type, krylov, block_order, type_width, type_hard, pair_rows, pair_cols, pair_count
):
    order = block_order.reshape(BLOCKS, BLK)
    kinds = atom_type.reshape(1, -1)

    packed = call(
        prep_kernel,
        shape((BLOCKS, ROWS, BLK), BF16),
        [ANY, ANY, ANY, ANY],
        VMEM,
        "prep",
        scratch=[
            pltpu.VMEM((8, BLOCKS // 2 * BLK), F32),
            pltpu.VMEM((3, BLOCKS * BLK), F32),
            pltpu.VMEM((1, BLOCKS * BLK), jnp.int32),
            pltpu.VMEM((VECS, BLOCKS * BLK), F32),
            pltpu.VMEM((BLOCKS, BLK), jnp.int32),
            pltpu.SemaphoreType.DMA((4,)),
        ],
        vmem=62,
    )(positions, kinds, krylov, order)

    other = across(packed)
    after = passed_down(packed, 1)
    rows_list, _ = lax.optimization_barrier((pair_rows.reshape(1, SLOTS), packed))

    inverse, codes, counts = call(
        side_kernel,
        (
            shape((BLOCKS, BLK), jnp.int32),
            shape((1, 2 * SLOT_SPAN), jnp.int32),
            shape((2,), jnp.int32),
        ),
        [ANY, ANY, ANY, ANY],
        (VMEM, VMEM, SMEM),
        "side",
        scratch=[
            pltpu.SMEM((1, 1), jnp.int32),
            pltpu.VMEM((1, SLOTS), jnp.int32),
            pltpu.VMEM((1, SLOTS), jnp.int32),
            pltpu.VMEM((BLOCKS, BLK), jnp.int32),
            pltpu.SemaphoreType.DMA((4,)),
        ],
        vmem=62,
        cost=time_cost(2),
    )(pair_count, rows_list, pair_cols.reshape(1, SLOTS), order)

    near_rows = [packed] + [around(packed, k) for k in (1, 2, 3)]

    codes, late = lax.optimization_barrier((codes, packed))
    second = passed_down(late, 2)
    features, vectors = call(
        feature_kernel,
        (shape((COLS, BLK, BLK), BF16), shape((COLS, VECS, BLK), BF16)),
        [SMEM, VMEM, VMEM, VMEM],
        (VMEM, VMEM),
        "features",
        cost=time_cost(12),
    )(type_width, packed, after, second)

    far_rows = [other] + [around(other, k) for k in (1, 2, 3)]
    step_rows, step_lanes = step_tables()
    codes, _ = lax.optimization_barrier((codes, other))
    scratch = [
        pltpu.VMEM((HALF, ROWS, BLK), BF16),
        pltpu.VMEM((HALF, 64, BLK), BF16),
        pltpu.VMEM((HALF + 1, VECS, BLK), F32),
        pltpu.VMEM((COLS + 1, VECS, BLK), F32),
        pltpu.VMEM((UNROLL, BLK, 2 * BLK), F32),
        pltpu.VMEM((UNROLL, BLK, BLK), BF16),
    ]
    block_set = (BLOCKS, VECS, BLK)
    *near_sums, col_sums = call(
        functools.partial(near_far_kernel, 0),
        [shape(block_set, F32)] + [shape(block_set, BF16)] * 3 + [shape((COLS, VECS, BLK), F32)],
        [SMEM] * 2 + [VMEM] * 8,
        [VMEM] * 5,
        "pairs_near",
        scratch=scratch,
        cost=PAIR_COST,
    )(counts, codes, *near_rows, vectors, features, step_rows, step_lanes)

    *far_sums, own_sum, after_sum, last_sum = call(
        functools.partial(near_far_kernel, 1),
        [shape(block_set, BF16)] * 4 + [shape(block_set, F32)] + [shape(block_set, BF16)] * 2,
        [SMEM] * 2 + [VMEM] * 9,
        [VMEM] * 7,
        "pairs_far",
        scratch=scratch,
        cost=PAIR_COST,
    )(counts, codes, *far_rows, vectors, features, step_rows, step_lanes, col_sums)

    far_parts = [far_sums[0]] + [around(far_sums[k], k) for k in (1, 2, 3)]
    from_prior = passed_up(after_sum, 1)
    from_second = passed_up(last_sum, 2)
    far_sum = call(
        sum_kernel, shape((BLOCKS, VECS, BLK), BF16), [VMEM] * 4, VMEM, "far_sum"
    )(*far_parts)
    from_far = across(far_sum)
    near_sums, _ = lax.optimization_barrier((near_sums, (far_sum, from_prior, from_second)))
    near_parts = [near_sums[0]] + [around(near_sums[k], k) for k in (1, 2, 3)]

    parts = [own_sum, from_far, from_prior, from_second, *near_parts]
    return call(
        final_kernel,
        shape(krylov.shape, F32),
        [SMEM] + [VMEM] * (len(parts) + 3),
        ANY,
        "final",
        scratch=[
            pltpu.VMEM((BLOCKS, VECS, BLK), F32),
            pltpu.VMEM((VECS, BLOCKS * BLK), F32),
            pltpu.SemaphoreType.DMA((4,)),
        ],
    )(type_hard, *parts, kinds, krylov, inverse)


def solution(mesh):
    placed = (
        P(None, ("row", "col")),
        P(("row", "col")),
        P(None, ("row", "col")),
        P(("row", "col")),
        P(),
        P(),
        P("row", "col", None),
        P("row", "col", None),
        P("row", "col"),
    )
    return jax.shard_map(
        on_device, mesh=mesh, in_specs=placed, out_specs=P(None, ("row", "col")), check_vma=False
    )
```
